32 devices in a mesh: dp: 16 (over z, y, x), tensor: 2 (over core).
Axes of the slice: x: 2, y: 2, z: 4, core: 2. Of those that a mesh axis runs over, the one named last changes fastest.
Arguments:
- inputs: bfloat16 [16, 1024, 768], P('dp', 'tensor'), may hold values from -6 to 6
- cotangent: bfloat16 [16, 1024, 768], P('dp', 'tensor'), may hold values from -6 to 6
- lengths: int32 [16], P('dp'), may hold values from 576 to 1024, as said below
- query_key: bfloat16 [768, 1536], P(('dp', 'tensor')), may hold values from -0.21875 to 0.21875
- value_proj: bfloat16 [768, 768], P(('dp', 'tensor')), may hold values from -0.375 to 0.375
- output_proj: bfloat16 [768, 768], P(('dp', 'tensor')), may hold values from -0.375 to 0.375
- hidden_in: bfloat16 [768, 3072], P('dp', 'tensor'), may hold values from -2 to 2
- hidden_out: bfloat16 [3072, 768], P('tensor', 'dp'), may hold values from -2 to 2
- first_gain: bfloat16 [768], P(('dp', 'tensor')), may hold values from 0.25 to 1.75
- second_gain: bfloat16 [768], P(('dp', 'tensor')), may hold values from 0.25 to 1.75
- third_gain: bfloat16 [768], P(('dp', 'tensor')), may hold values from 0.25 to 1.75
- fourth_gain: bfloat16 [3072], P('tensor'), may hold values from 0.25 to 1.75
Outputs:
- outputs: bfloat16 [16, 1024, 768], P('dp', 'tensor')
- inputs_grad: bfloat16 [16, 1024, 768], P('dp', 'tensor')
- query_key_grad: float32 [768, 1536], P(('dp', 'tensor'))
- value_proj_grad: float32 [768, 768], P(('dp', 'tensor'))
- output_proj_grad: float32 [768, 768], P(('dp', 'tensor'))
- hidden_in_grad: float32 [768, 3072], P('dp', 'tensor')
- hidden_out_grad: float32 [3072, 768], P('tensor', 'dp')
- first_gain_grad: float32 [768], P(('dp', 'tensor'))
- second_gain_grad: float32 [768], P(('dp', 'tensor'))
- third_gain_grad: float32 [768], P(('dp', 'tensor'))
- fourth_gain_grad: float32 [3072], P('tensor')
The draws below stay inside these ranges and needn't reach their ends.
Inputs may be any that keep to these rules, and one draw needn't show every extreme that they name: `lengths`: shorter sequences are more common; at least one sequence has exactly 1024 tokens.
All inputs are finite; a program needn't handle non-finite values.
Results may differ from the reference program's by a relative error of at most 0.019.
Values may be sent and summed in bfloat16 or wider, within the bound.
No kernel may reach another device: no remote copies, remote signals or barrier semaphores. Data moves between devices by JAX's collectives and lax.ppermute only.
A program may use at most 128 MiB of HBM per device.

```python
import jax
import jax.numpy as jnp
from jax import lax

D = 768
HEAD_DIM = 64
FF = 3072
SEQ_LEN = 1024
SEQS = 16


def draw_lengths(key, part):
    low_end = SEQ_LEN // 2 + SEQ_LEN // 16
    streams = jax.random.split(key, 4)
    first = jax.random.randint(streams[0], (SEQS,), low_end, SEQ_LEN + 1)
    second = jax.random.randint(streams[1], (SEQS,), low_end, SEQ_LEN + 1)
    third = jax.random.randint(streams[2], (SEQS,), low_end, SEQ_LEN + 1)
    shortest = jnp.minimum(jnp.minimum(first, second), third)
    picked = jax.random.randint(streams[3], (), 0, SEQS)
    return shortest.at[picked].set(SEQ_LEN).astype(jnp.int32)


def unit_scales(key, fan_value):
    ratio = 4.0
    place = jnp.arange(FF, dtype=jnp.float32) / (FF - 1)
    jitter = jax.random.uniform(key, (FF,), jnp.float32, 0.8, 1.25)
    return jnp.exp((place - 0.5) * jnp.log(ratio)) * jitter * jnp.sqrt(3.0 / fan_value)


def entries(key, shape):
    return jnp.clip(jax.random.normal(key, shape, jnp.float32), -6.0, 6.0)


def draw_hidden_in(key, part):
    streams = jax.random.split(jax.random.fold_in(key, 11), 2)
    return (entries(streams[0], (D, FF)) * unit_scales(streams[1], D)[None, :]).astype(jnp.bfloat16)


def draw_hidden_out(key, part):
    streams = jax.random.split(jax.random.fold_in(key, 23), 2)
    return (entries(streams[0], (FF, D)) * unit_scales(streams[1], FF)[:, None]).astype(jnp.bfloat16)


def raised(drawn, key, source, target, parts, factor):
    owner, partner = [(jnp.arange(drawn.shape[position]) // (drawn.shape[position] // parts)).reshape([-1 if axis == position else 1 for axis in range(drawn.ndim)]) for position in (source, target)]
    chosen = jax.random.permutation(key, parts)[partner]
    strong = (owner == chosen) | (owner == (partner + parts // 2) % parts)
    return jnp.where(strong, factor * drawn, drawn)


def block_scale(stream_key, extent, pieces, smallest, high):
    def one(axis_at, parts):
        heights = jax.random.uniform(jax.random.fold_in(jax.random.fold_in(stream_key, 6), axis_at), (parts,), jnp.float32, smallest / len(pieces), high / len(pieces))
        return jnp.repeat(jnp.exp(heights), extent[axis_at] // parts).reshape((-1,) + (1,) * (len(extent) - axis_at - 1))

    level = one(*pieces[0])
    for cut in pieces[1:]:
        level = level * one(*cut)
    return level


def centred(rng, extent, width, bound, pieces=(), kind=jnp.bfloat16):
    gain = block_scale(rng, extent, pieces, -0.22, 0.18) if pieces else 1.0
    values = jax.random.normal(rng, extent, jnp.float32) * width * gain
    return jnp.minimum(jnp.maximum(values, -bound), bound).astype(kind)


def gaussian_with(own_key, dims, width, reach, shards, heavy, kind=jnp.bfloat16):
    array = width * jax.random.normal(own_key, dims, jnp.float32)
    if shards:
        array = array * block_scale(own_key, dims, shards, -0.22, 0.18)
    return jnp.clip(raised(array, jax.random.fold_in(own_key, 3), *heavy), -reach, reach).astype(kind)


def setup_inputs(seed: int = 0) -> dict:
    streams_of = jax.random.split(jax.random.key(seed), 13)
    return {
        "inputs": gaussian_with(streams_of[0], (SEQS, SEQ_LEN, D), 1.0, 6.0, ((0, 16), (1, 2)), (0, 2, 16, 2.0)),
        "cotangent": gaussian_with(streams_of[1], (SEQS, SEQ_LEN, D), 1.0, 6.0, ((0, 16), (1, 2)), (0, 2, 16, 2.0)),
        "lengths": draw_lengths(jax.random.fold_in(streams_of[12], 71), 0),
        "query_key": centred(streams_of[3], (D, 2 * D), D ** -0.5, 0.21875, ((0, 32),)),
        "value_proj": centred(streams_of[4], (D, D), (D // 3) ** -0.5, 0.375, ((0, 32),)),
        "output_proj": centred(streams_of[5], (D, D), (D // 3) ** -0.5, 0.375, ((0, 32),)),
        "hidden_in": draw_hidden_in(jax.random.fold_in(streams_of[12], 71), 0),
        "hidden_out": draw_hidden_out(jax.random.fold_in(streams_of[12], 71), 0),
        "first_gain": jnp.clip(1.0 + 0.15 * jax.random.normal(streams_of[8], (D,), jnp.float32), 0.25, 1.75).astype(jnp.bfloat16),
        "second_gain": jnp.clip(1.0 + 0.15 * jax.random.normal(streams_of[9], (D,), jnp.float32), 0.25, 1.75).astype(jnp.bfloat16),
        "third_gain": jnp.clip(1.0 + 0.15 * jax.random.normal(streams_of[10], (D,), jnp.float32), 0.25, 1.75).astype(jnp.bfloat16),
        "fourth_gain": jnp.clip(1.0 + 0.15 * jax.random.normal(streams_of[11], (FF,), jnp.float32), 0.25, 1.75).astype(jnp.bfloat16),
    }


EPSILON = 1e-05
MASKED = -1000000000.0

@jax.custom_vjp
def low(v):
    return lax.optimization_barrier(v.astype(jnp.bfloat16)).astype(jnp.float32)

@jax.custom_vjp
def low_back(v):
    return v

def low_keep(v):
    return (low(v), None)

def low_pass(kept, grad):
    return (grad,)

def back_keep(v):
    return (v, None)

def back_low(kept, grad):
    return (low(grad),)
low.defvjp(low_keep, low_pass)
low_back.defvjp(back_keep, back_low)

def matmul(former, latter):
    return jnp.dot(former, latter, precision=lax.Precision.HIGHEST, preferred_element_type=jnp.float32)

def normalize(series, scales):
    center = lax.optimization_barrier(jnp.mean(series, -1, keepdims=True))
    spread = lax.optimization_barrier(jnp.mean(series * series, -1, keepdims=True)) - center * center
    return (series - center) * lax.rsqrt(spread + EPSILON) * scales

def attend(queries, key_rows, value_rows, allowed):
    row_total = queries.shape[0]
    pair_count = queries.shape[1] // (2 * HEAD_DIM)

    def split_heads(matrix):
        return matrix.reshape(row_total, pair_count, 2, HEAD_DIM).transpose(1, 0, 2, 3)

    def one_pair(element):
        query_heads, key_heads, value_heads = element
        raw_scores = jnp.einsum('qhd,khd->hqk', query_heads, key_heads, precision=lax.Precision.HIGHEST) * 0.125
        scores = jnp.where(allowed[None], low_back(raw_scores), MASKED)
        highest = lax.optimization_barrier(jnp.max(scores, -1, keepdims=True))
        expo = jnp.exp(scores - highest)
        probs = expo / lax.optimization_barrier(jnp.sum(expo, -1, keepdims=True))
        probs_low = low(probs)
        return jnp.einsum('hqk,khd->qhd', probs_low, value_heads, precision=lax.Precision.HIGHEST)
    stacked = lax.map(jax.checkpoint(one_pair), (split_heads(queries), split_heads(key_rows), split_heads(value_rows)))
    return stacked.transpose(1, 0, 2, 3).reshape(row_total, pair_count * 2 * HEAD_DIM)

def layer(series, weights, kept_rows, allowed):
    query_key, value_proj, output_proj, hidden_in, hidden_out, first_gain, second_gain, third_gain, fourth_gain = weights
    model_width = series.shape[1]
    normed_in = low(normalize(series, first_gain))
    projected = low(low_back(matmul(normed_in, query_key)))
    value_rows = low(low_back(matmul(normed_in, value_proj)))
    attended = low_back(attend(projected[:, :model_width], projected[:, model_width:], value_rows, allowed))
    sub_normed = low(normalize(attended, second_gain))
    middle = series + low_back(matmul(sub_normed, output_proj))
    ffn_normed = low(normalize(middle, third_gain))
    pre_act = low_back(matmul(ffn_normed, hidden_in))
    hidden_normed = low(normalize(jax.nn.gelu(pre_act, approximate=False), fourth_gain))
    branch = low_back(matmul(hidden_normed, hidden_out))
    return kept_rows * (middle + branch)

def reference(inputs, cotangent, lengths, query_key, value_proj, output_proj, hidden_in, hidden_out, first_gain, second_gain, third_gain, fourth_gain):
    params = tuple((array_in.astype(jnp.float32) for array_in in (query_key, value_proj, output_proj, hidden_in, hidden_out, first_gain, second_gain, third_gain, fourth_gain)))
    places = jnp.arange(SEQ_LEN, dtype=jnp.int32)

    def one_sequence(totals, element):
        series, grad_in, seq_length = element
        kept_rows = (places < seq_length).astype(jnp.float32)[:, None]
        allowed = (places[None, :] <= places[:, None]) & (places[None, :] < seq_length)

        def forward(values_in, *weights):
            return layer(values_in, weights, kept_rows, allowed)
        result, backward = jax.vjp(forward, series.astype(jnp.float32), *params)
        gradients = backward(grad_in.astype(jnp.float32))
        totals = tuple((running + fresh for running, fresh in zip(totals, gradients[1:])))
        return (totals, (result.astype(jnp.bfloat16), gradients[0].astype(jnp.bfloat16)))
    zeros_init = tuple((jnp.zeros(array_in.shape, jnp.float32) for array_in in params))
    totals, (outputs, inputs_grad) = lax.scan(one_sequence, zeros_init, (inputs, cotangent, lengths))
    return (outputs, inputs_grad, totals[0], totals[1], totals[2], totals[3], totals[4], totals[5], totals[6], totals[7], totals[8])
```

```python
import jax
import jax.numpy as jnp
from jax import lax
from jax.experimental import pallas as pl
from jax.experimental.pallas import tpu as pltpu
from jax.sharding import Mesh
from jax.sharding import PartitionSpec as P

HEAD_DIM = 64
PAIR = 2 * HEAD_DIM
EPSILON = 1e-05
MASKED = -1000000000.0
F32 = jnp.float32
BF16 = jnp.bfloat16
VMEM_LIMIT = 60 * 1024 * 1024
TILE = 256


def mm(former, latter):
    return jnp.dot(former, latter, preferred_element_type=F32)


def mm_tail(former, latter):
    return lax.dot_general(former, latter, (((1,), (1,)), ((), ())), preferred_element_type=F32)


def mm_lead(former, latter):
    return lax.dot_general(former, latter, (((0,), (0,)), ((), ())), preferred_element_type=F32)


def call(body, name, out_shape, grid, in_specs, out_specs, scratch=(), flops=0, nbytes=0, aliases=None):
    return pl.pallas_call(
        body,
        name=name,
        out_shape=out_shape,
        grid_spec=pltpu.PrefetchScalarGridSpec(
            num_scalar_prefetch=1,
            grid=grid,
            in_specs=in_specs,
            out_specs=out_specs,
            scratch_shapes=list(scratch),
        ),
        input_output_aliases=aliases or {},
        compiler_params=pltpu.CompilerParams(vmem_limit_bytes=VMEM_LIMIT),
        cost_estimate=pl.CostEstimate(flops=flops, bytes_accessed=nbytes, transcendentals=0),
    )


def shaped(shape, kind):
    return jax.ShapeDtypeStruct(shape, kind)


def whole(shape):
    return pl.BlockSpec(shape, lambda i, s: (0,) * len(shape))


def rows_of(shape):
    return pl.BlockSpec(shape, lambda i, s: (i, 0))


def norm_stats(series):
    center = jnp.mean(series, -1, keepdims=True)
    spread = jnp.mean(series * series, -1, keepdims=True) - center * center
    inverse = lax.rsqrt(spread + EPSILON)
    return (series - center) * inverse, inverse


def norm_back(grad, gain, hat, inverse):
    scaled = grad * gain
    first = jnp.mean(scaled, -1, keepdims=True)
    second = jnp.mean(scaled * hat, -1, keepdims=True)
    return inverse * (scaled - first - hat * second)


def project(inputs, weights, gains, scalars):
    rows, width = inputs.shape
    tile = min(TILE, rows)

    def body(s_ref, x_ref, w_ref, g_ref, q_ref, k_ref, v_ref, n_ref):
        hat, _ = norm_stats(x_ref[...].astype(F32))
        low = (hat * g_ref[0:1, :]).astype(BF16)
        n_ref[...] = low
        for at, out in enumerate((q_ref, k_ref, v_ref)):
            out[...] = mm(low, w_ref[:, at * width : (at + 1) * width]).astype(BF16)

    spec = rows_of((tile, width))
    return call(
        body,
        "project",
        tuple(shaped((rows, width), BF16) for _ in range(4)),
        (rows // tile,),
        [spec, whole((width, 3 * width)), whole((8, width))],
        (spec,) * 4,
        flops=2 * rows * width * 3 * width,
        nbytes=rows * width * 10 + width * width * 6,
    )(scalars, inputs, weights, gains)


def lane_of(head):
    lanes = lax.broadcasted_iota(jnp.int32, (1, PAIR), 1)
    return (lanes >= head * HEAD_DIM) & (lanes < (head + 1) * HEAD_DIM)


def attend(queries, keys, values, far_keys, far_values, scalars):
    rows, width = queries.shape
    tile = min(TILE, rows)
    pairs = width // PAIR

    def body(s_ref, q_ref, k_ref, v_ref, fk_ref, fv_ref, o_ref, l_ref):
        offset = s_ref[1] * rows
        length = s_ref[2]

        def run(far):
            query = q_ref[...] * jnp.asarray(0.125, BF16)
            for t in range(rows // tile):
                near = (t + 1) * tile
                place = lax.broadcasted_iota(jnp.int32, (tile, near), 0) + t * tile
                key_at = lax.broadcasted_iota(jnp.int32, (tile, near), 1)
                allowed = (key_at <= place) & (key_at + offset < length)
                sums = []
                logs = []
                for head in range(2):
                    mine = jnp.where(
                        lane_of(head), query[t * tile : near], jnp.zeros((), BF16)
                    )
                    scores = jnp.where(allowed, mm_tail(mine, k_ref[0:near]), MASKED)
                    highest = jnp.max(scores, -1, keepdims=True)
                    if far:
                        beyond = mm_tail(mine, fk_ref[...])
                        highest = jnp.maximum(highest, jnp.max(beyond, -1, keepdims=True))
                        beyond = jnp.exp(beyond - highest)
                    scores = jnp.exp(scores - highest)
                    total = jnp.sum(scores, -1, keepdims=True)
                    mixed = mm(scores.astype(BF16), v_ref[0:near])
                    if far:
                        total = total + jnp.sum(beyond, -1, keepdims=True)
                        mixed = mixed + mm(beyond.astype(BF16), fv_ref[...])
                    sums.append(mixed / total)
                    logs.append(jnp.broadcast_to(highest + jnp.log(total), (tile, PAIR)))
                o_ref[t * tile : near] = jnp.where(lane_of(0), sums[0], sums[1])
                l_ref[t * tile : near] = jnp.where(lane_of(0), logs[0], logs[1])

        @pl.when(s_ref[1] == 0)
        def _():
            run(False)

        @pl.when(s_ref[1] != 0)
        def _():
            run(True)

    spec = pl.BlockSpec((rows, PAIR), lambda i, s: (0, i))
    return call(
        body,
        "attend",
        (shaped((rows, width), F32), shaped((rows, width), F32)),
        (pairs,),
        [spec] * 5,
        (spec, spec),
        flops=8 * rows * rows * width,
        nbytes=rows * width * 18,
    )(scalars, queries, keys, values, far_keys, far_values)


def attend_back(queries, keys, values, far_keys, far_values, grads, attended, logs, scalars):
    rows, width = queries.shape
    tile = min(TILE, rows)
    pairs = width // PAIR

    def body(
        s_ref, q_ref, k_ref, v_ref, fk_ref, fv_ref, d_ref, o_ref, l_ref,
        dq_ref, dk_ref, dv_ref, fdk_ref, fdv_ref,
    ):
        offset = s_ref[1] * rows
        length = s_ref[2]

        def run(far):
            query = q_ref[...] * jnp.asarray(0.125, BF16)
            grad = d_ref[...]
            log_rows = jnp.transpose(l_ref[...])
            picker = jnp.where(
                lax.broadcasted_iota(jnp.int32, (8, PAIR), 1) // HEAD_DIM
                == lax.broadcasted_iota(jnp.int32, (8, PAIR), 0),
                1.0,
                0.0,
            ).astype(F32)
            dots = lax.dot_general(
                picker,
                grad.astype(F32) * o_ref[...],
                (((1,), (1,)), ((), ())),
                precision=lax.Precision.HIGHEST,
                preferred_element_type=F32,
            )
            blocks = [
                (k_ref, v_ref, dk_ref, dv_ref, t * tile, t * tile, True)
                for t in range(rows // tile)
            ]
            if far:
                blocks += [
                    (fk_ref, fv_ref, fdk_ref, fdv_ref, t * tile, 0, False)
                    for t in range(rows // tile)
                ]
            turned = [[jnp.zeros((HEAD_DIM, tile), F32) for _ in range(rows // tile)] for _ in range(2)]
            for key_ref, value_ref, dkey_ref, dvalue_ref, at, low, masked in blocks:
                key = key_ref[at : at + tile]
                value = value_ref[at : at + tile]
                key_turned = jnp.transpose(key)
                count = rows - low
                kgrads, vgrads = [], []
                if masked:
                    key_at = lax.broadcasted_iota(jnp.int32, (tile, count), 0) + at
                    place = lax.broadcasted_iota(jnp.int32, (tile, count), 1) + low
                    allowed = (key_at <= place) & (key_at + offset < length)
                for head in range(2):
                    lanes = lane_of(head)
                    mine = jnp.where(lanes, query[low:rows], jnp.zeros((), BF16))
                    mine_grad = jnp.where(lanes, grad[low:rows], jnp.zeros((), BF16))
                    scores = mm_tail(key, mine)
                    if masked:
                        scores = jnp.where(allowed, scores, MASKED)
                    base = head * HEAD_DIM
                    probs = jnp.exp(scores - log_rows[base : base + 1, low:rows])
                    prob_grad = mm_tail(value, mine_grad)
                    score_grad = (probs * (prob_grad - dots[head : head + 1, low:rows])).astype(BF16)
                    vgrads.append(mm(probs.astype(BF16), grad[low:rows]))
                    kgrads.append(mm(score_grad, query[low:rows]))
                    part = mm(key_turned[base : base + HEAD_DIM], score_grad)
                    for t in range(low // tile, rows // tile):
                        turned[head][t] = turned[head][t] + part[:, t * tile - low : (t + 1) * tile - low]
                dkey_ref[at : at + tile] = jnp.where(lane_of(0), kgrads[0], kgrads[1]).astype(dkey_ref.dtype)
                dvalue_ref[at : at + tile] = jnp.where(lane_of(0), vgrads[0], vgrads[1]).astype(dvalue_ref.dtype)
            for t in range(rows // tile):
                both = jnp.concatenate([turned[0][t], turned[1][t]], 0)
                dq_ref[t * tile : (t + 1) * tile] = (jnp.transpose(both) * 0.125).astype(BF16)

        @pl.when(s_ref[1] == 0)
        def _():
            run(False)
            fdk_ref[...] = jnp.zeros_like(fdk_ref)
            fdv_ref[...] = jnp.zeros_like(fdv_ref)

        @pl.when(s_ref[1] != 0)
        def _():
            run(True)

    spec = pl.BlockSpec((rows, PAIR), lambda i, s: (0, i))
    return call(
        body,
        "attend_back",
        tuple(shaped((rows, width), kind) for kind in (BF16, F32, F32, BF16, BF16)),
        (pairs,),
        [spec] * 8,
        (spec,) * 5,
        flops=20 * rows * rows * width,
        nbytes=rows * width * 34,
    )(scalars, queries, keys, values, far_keys, far_values, grads, attended, logs)


def join(attended, inputs, weights, gains, scalars):
    rows, width = attended.shape
    tile = min(TILE, rows)

    def body(s_ref, a_ref, x_ref, w_ref, g_ref, sub_ref, mid_ref, ffn_ref):
        hat, _ = norm_stats(a_ref[...])
        low = (hat * g_ref[1:2, :]).astype(BF16)
        sub_ref[...] = low
        middle = x_ref[...].astype(F32) + mm(low, w_ref[...])
        mid_ref[...] = middle
        hat, _ = norm_stats(middle)
        ffn_ref[...] = (hat * g_ref[2:3, :]).astype(BF16)

    spec = rows_of((tile, width))
    return call(
        body,
        "join",
        (shaped((rows, width), BF16), shaped((rows, width), F32), shaped((rows, width), BF16)),
        (rows // tile,),
        [spec, spec, whole((width, width)), whole((8, width))],
        (spec,) * 3,
        flops=2 * rows * width * width,
        nbytes=rows * width * 14 + width * width * 2,
    )(scalars, attended, inputs, weights, gains)


def join_back(branch, far_branch, fgrad, far_fgrad, middle, cotangent, sub_low, attended, weights, gains, scalars):
    rows, width = middle.shape
    tile = min(TILE, rows)
    steps = rows // tile
    half = width // 2

    def body(
        s_ref, b_ref, fb_ref, f_ref, ff_ref, m_ref, c_ref, s_low_ref, a_ref, w_ref, g_ref,
        out_ref, mg_ref, ag_ref, keep_ref, send_ref, terms_ref, total,
    ):
        step = pl.program_id(0)
        places = lax.broadcasted_iota(jnp.int32, (tile, 1), 0) + (step * tile + s_ref[1] * rows)
        kept = (places < s_ref[2]).astype(F32)
        middle = m_ref[...]
        branch = b_ref[...].astype(F32) + fb_ref[...].astype(F32)
        out_ref[...] = (kept * (middle + branch)).astype(BF16)
        hat, inverse = norm_stats(middle)
        grad = f_ref[...].astype(F32) + ff_ref[...].astype(F32)
        third = jnp.sum(grad * hat, 0, keepdims=True)
        middle_grad = c_ref[...].astype(F32) * kept + norm_back(grad, g_ref[2:3, :], hat, inverse)
        mg_ref[...] = middle_grad
        low = middle_grad.astype(BF16)
        part = mm_lead(s_low_ref[...], low)
        sub_grad = mm_tail(low, w_ref[...])
        hat, inverse = norm_stats(a_ref[...])
        second = jnp.sum(sub_grad * hat, 0, keepdims=True)
        ag_ref[...] = norm_back(sub_grad, g_ref[1:2, :], hat, inverse).astype(BF16)

        @pl.when(step == 0)
        def _():
            total[...] = part
            terms_ref[...] = jnp.zeros_like(terms_ref)

        @pl.when(step > 0)
        def _():
            total[...] += part

        terms_ref[1:2, :] += second
        terms_ref[2:3, :] += third

        @pl.when(step == steps - 1)
        def _():
            core = s_ref[1]
            keep_ref[...] = total[:, pl.ds(pl.multiple_of(core * half, 128), half)].astype(BF16)
            send_ref[...] = total[:, pl.ds(pl.multiple_of((1 - core) * half, 128), half)].astype(BF16)

    spec = rows_of((tile, width))
    return call(
        body,
        "join_back",
        (
            shaped((rows, width), BF16),
            shaped((rows, width), F32),
            shaped((rows, width), BF16),
            shaped((width, half), BF16),
            shaped((width, half), BF16),
            shaped((8, width), F32),
        ),
        (steps,),
        [spec] * 8 + [whole((width, width)), whole((8, width))],
        (spec, spec, spec, whole((width, half)), whole((width, half)), whole((8, width))),
        scratch=[pltpu.VMEM((width, width), F32)],
        flops=4 * rows * width * width,
        nbytes=rows * width * 30 + width * width * 4,
    )(scalars, branch, far_branch, fgrad, far_fgrad, middle, cotangent, sub_low, attended, weights, gains)


def two_sided(tile, width, steps):
    near = pl.BlockSpec((tile, width), lambda i, s: (jnp.minimum(i, steps - 1), 0))
    far = pl.BlockSpec((tile, width), lambda i, s: (jnp.maximum(i - steps, 0), 0))
    return near, far


def lane_stats(first, second):
    lanes = lax.broadcasted_iota(jnp.int32, (first.shape[0], 128), 1)
    return jnp.where(lanes == 0, first, jnp.where(lanes == 1, second, 0.0))


def ffn_in(near, far, weights, scalars):
    rows, width = near.shape
    units = weights.shape[1] // 2
    tile = min(TILE, rows)
    steps = rows // tile
    chunk = 512 if units % 512 == 0 else units

    def body(s_ref, n_ref, f_ref, w_ref, act_ref, slope_ref, stat_ref):
        def run(low):
            sums = jnp.zeros((tile, 1), F32)
            squares = jnp.zeros((tile, 1), F32)
            for at in range(0, units, chunk):
                pre = mm(low, w_ref[:, at : at + chunk])
                cdf = 0.5 * (1.0 + lax.erf(pre * 0.7071067811865476))
                pdf = 0.3989422804014327 * jnp.exp(-0.5 * pre * pre)
                act = pre * cdf
                act_ref[:, at : at + chunk] = act
                slope_ref[:, at : at + chunk] = (cdf + pre * pdf).astype(slope_ref.dtype)
                sums = sums + jnp.sum(act, -1, keepdims=True)
                squares = squares + jnp.sum(act * act, -1, keepdims=True)
            stat_ref[...] = lane_stats(sums, squares)

        @pl.when(pl.program_id(0) < steps)
        def _():
            run(n_ref[...])

        @pl.when(pl.program_id(0) >= steps)
        def _():
            run(f_ref[...])

    near_spec, far_spec = two_sided(tile, width, steps)
    return call(
        body,
        "ffn_in",
        (
            shaped((2 * rows, units), F32),
            shaped((2 * rows, units), BF16),
            shaped((2 * rows, 128), F32),
        ),
        (2 * steps,),
        [near_spec, far_spec, pl.BlockSpec((width, units), lambda i, s: (0, 0))],
        (rows_of((tile, units)), rows_of((tile, units)), rows_of((tile, 128))),
        flops=4 * rows * width * units,
        nbytes=rows * units * 12 + width * units * 2,
    )(scalars, near, far, weights)


def swapped(tile, steps):
    return pl.BlockSpec((tile, 128), lambda i, s: (lax.rem(i + steps, 2 * steps), 0))


def unit_norm(stat, other, total):
    both = stat + other
    center = both[:, 0:1] / total
    inverse = lax.rsqrt(both[:, 1:2] / total - center * center + EPSILON)
    return center, inverse


def ffn_out(act, stats, far_stats, gain, near_grad, far_grad, weights, scalars, order):
    rows, width = near_grad.shape
    units = act.shape[1]
    tile = min(TILE, rows)
    steps = rows // tile
    total_units = 2 * units
    depth = width // len(order)

    def body(
        s_ref, a_ref, st_ref, fs_ref, g_ref, n_ref, f_ref, w_ref,
        b_ref, sg_ref, stat_ref, four_ref, out_ref, total,
    ):
        step = pl.program_id(0)
        center, inverse = unit_norm(st_ref[...], fs_ref[...], total_units)
        gain = g_ref[...]

        def run(grad):
            hat = (a_ref[...] - center) * inverse
            low = (hat * gain).astype(BF16)
            b_ref[...] = mm_tail(low, w_ref[...]).astype(BF16)
            normed = mm(grad, w_ref[...])
            part = mm_lead(grad, low)
            scaled = normed * gain
            sg_ref[...] = scaled
            stat_ref[...] = lane_stats(
                jnp.sum(scaled, -1, keepdims=True), jnp.sum(scaled * hat, -1, keepdims=True)
            )
            fourth = jnp.sum(normed * hat, 0, keepdims=True)

            @pl.when(step == 0)
            def _():
                total[...] = part
                four_ref[...] = jnp.broadcast_to(fourth, four_ref.shape)

            @pl.when(step > 0)
            def _():
                total[...] += part
                four_ref[...] += jnp.broadcast_to(fourth, four_ref.shape)

        @pl.when(step < steps)
        def _():
            run(n_ref[...])

        @pl.when(step >= steps)
        def _():
            run(f_ref[...])

        @pl.when(step == 2 * steps - 1)
        def _():
            for at, block in enumerate(order):
                out_ref[at * depth : (at + 1) * depth] = total[
                    block * depth : (block + 1) * depth
                ].astype(BF16)

    near_spec, far_spec = two_sided(tile, width, steps)
    wide = rows_of((tile, units))
    return call(
        body,
        "ffn_out",
        (
            shaped((2 * rows, width), BF16),
            shaped((2 * rows, units), F32),
            shaped((2 * rows, 128), F32),
            shaped((8, units), F32),
            shaped((width, units), BF16),
        ),
        (2 * steps,),
        [
            wide,
            rows_of((tile, 128)),
            swapped(tile, steps),
            whole((1, units)),
            near_spec,
            far_spec,
            pl.BlockSpec((width, units), lambda i, s: (0, 1)),
        ],
        (rows_of((tile, width)), wide, rows_of((tile, 128)), whole((8, units)), whole((width, units))),
        scratch=[pltpu.VMEM((width, units), F32)],
        flops=12 * rows * width * units,
        nbytes=rows * units * 16 + width * units * 4,
    )(scalars, act, stats, far_stats, gain, near_grad, far_grad, weights)


def ffn_back(act, slope, scaled, stats, far_stats, grads, far_grads, near, far, weights, scalars, order):
    rows, width = near.shape
    units = act.shape[1]
    tile = min(TILE, rows)
    steps = rows // tile
    total_units = 2 * units
    depth = width // len(order)

    def body(
        s_ref, a_ref, sl_ref, sg_ref, st_ref, fs_ref, gt_ref, fg_ref, n_ref, f_ref, w_ref,
        b_ref, out_ref, total,
    ):
        step = pl.program_id(0)
        center, inverse = unit_norm(st_ref[...], fs_ref[...], total_units)
        both = gt_ref[...] + fg_ref[...]
        first = both[:, 0:1] / total_units
        second = both[:, 1:2] / total_units

        def run(low):
            hat = (a_ref[...] - center) * inverse
            act_grad = inverse * (sg_ref[...] - first - hat * second)
            pre = (act_grad * sl_ref[...].astype(F32)).astype(BF16)
            b_ref[...] = mm_tail(pre, w_ref[...]).astype(BF16)
            part = mm_lead(low, pre)

            @pl.when(step == 0)
            def _():
                total[...] = part

            @pl.when(step > 0)
            def _():
                total[...] += part

        @pl.when(step < steps)
        def _():
            run(n_ref[...])

        @pl.when(step >= steps)
        def _():
            run(f_ref[...])

        @pl.when(step == 2 * steps - 1)
        def _():
            for at, block in enumerate(order):
                out_ref[at * depth : (at + 1) * depth] = total[
                    block * depth : (block + 1) * depth
                ].astype(BF16)

    near_spec, far_spec = two_sided(tile, width, steps)
    wide = rows_of((tile, units))
    thin = rows_of((tile, 128))
    return call(
        body,
        "ffn_back",
        (shaped((2 * rows, width), BF16), shaped((width, units), BF16)),
        (2 * steps,),
        [
            wide, wide, wide, thin, swapped(tile, steps), thin, swapped(tile, steps),
            near_spec, far_spec, pl.BlockSpec((width, units), lambda i, s: (0, 0)),
        ],
        (rows_of((tile, width)), whole((width, units))),
        scratch=[pltpu.VMEM((width, units), F32)],
        flops=8 * rows * width * units,
        nbytes=rows * units * 20 + width * units * 4,
    )(scalars, act, slope, scaled, stats, far_stats, grads, far_grads, near, far, weights)


def project_grads(normed, dq, dk, far_dk, dv, far_dv, scalars, blocks):
    rows, width = normed.shape
    depth = width // blocks
    half = 3 * width // 2

    def body(s_ref, n_ref, q_ref, k_ref, fk_ref, v_ref, fv_ref, kl_ref, vl_ref, keep_ref, send_ref, low_ref):
        me, core = s_ref[0], s_ref[1]
        near = core == 0
        key = k_ref[...] + jnp.where(near, fk_ref[...].astype(F32), 0.0)
        value = v_ref[...] + jnp.where(near, fv_ref[...].astype(F32), 0.0)
        kl_ref[...] = key.astype(BF16)
        vl_ref[...] = value.astype(BF16)
        low_ref[:, 0:width] = q_ref[...]
        low_ref[:, width : 2 * width] = key.astype(BF16)
        low_ref[:, 2 * width : 3 * width] = value.astype(BF16)
        turned = jnp.transpose(n_ref[...])
        for side, out in ((0, keep_ref), (1, send_ref)):
            owner = core if side == 0 else 1 - core
            column = pl.multiple_of(owner * half, 128)
            part = mm(turned, low_ref[:, pl.ds(column, half)]).astype(BF16)
            for block in range(blocks):
                out[block ^ me] = part[block * depth : (block + 1) * depth]

    return call(
        body,
        "project_grads",
        (
            shaped((rows, width), BF16),
            shaped((rows, width), BF16),
            shaped((blocks, depth, half), BF16),
            shaped((blocks, depth, half), BF16),
        ),
        (1,),
        [whole((rows, width))] * 6,
        (whole((rows, width)), whole((rows, width)), whole((blocks, depth, half)), whole((blocks, depth, half))),
        scratch=[pltpu.VMEM((rows, 3 * width), BF16)],
        flops=6 * rows * width * width,
        nbytes=rows * width * 20 + width * width * 6,
    )(scalars, normed, dq, dk, far_dk, dv, far_dv)


def project_back(dq, dk, dv, inputs, middle_grad, weights, gains, scalars):
    rows, width = inputs.shape
    tile = min(TILE, rows)

    def body(s_ref, q_ref, k_ref, v_ref, x_ref, m_ref, w_ref, g_ref, out_ref, term_ref):
        hat, inverse = norm_stats(x_ref[...].astype(F32))
        grad = mm_tail(q_ref[...], w_ref[:, 0:width])
        grad = grad + mm_tail(k_ref[...], w_ref[:, width : 2 * width])
        grad = grad + mm_tail(v_ref[...], w_ref[:, 2 * width : 3 * width])
        first = jnp.sum(grad * hat, 0, keepdims=True)
        out_ref[...] = (m_ref[...] + norm_back(grad, g_ref[0:1, :], hat, inverse)).astype(BF16)

        @pl.when(pl.program_id(0) == 0)
        def _():
            term_ref[...] = jnp.zeros_like(term_ref)

        term_ref[0:1, :] += first

    spec = rows_of((tile, width))
    return call(
        body,
        "project_back",
        (shaped((rows, width), BF16), shaped((8, width), F32)),
        (rows // tile,),
        [spec] * 5 + [whole((width, 3 * width)), whole((8, width))],
        (spec, whole((8, width))),
        flops=6 * rows * width * width,
        nbytes=rows * width * 14 + width * width * 6,
    )(scalars, dq, dk, dv, inputs, middle_grad, weights, gains)


CHIPS = ("outer", "inner")
CORES = "tensor"


def other_core(array):
    return lax.ppermute(array, CORES, [(0, 1), (1, 0)])


def exchange(array, bit, chips):
    return lax.ppermute(array, CHIPS, [(i, i ^ (1 << bit)) for i in range(chips)])


def bit_count(chips):
    return chips.bit_length() - 1


def by_core(mine, other, axis):
    core = lax.axis_index(CORES)
    return jnp.where(
        core == 0,
        jnp.concatenate([mine, other], axis),
        jnp.concatenate([other, mine], axis),
    )


def gather_pairwise(shard, chips):
    bits = bit_count(chips)
    held = shard[None]
    for bit in range(2, bits):
        held = jnp.concatenate([held, exchange(held, bit, chips)], 0)
    columns = shard.shape[1]
    cut = -(-columns // 256) * 128
    first, second = held[:, :, :cut], held[:, :, cut:]
    far_first, far_second = exchange(first, 1, chips), exchange(second, 0, chips)
    first = jnp.concatenate([first, far_first], 0)
    second = jnp.concatenate([second, far_second], 0)
    far_first, far_second = exchange(first, 0, chips), exchange(second, 1, chips)
    first = jnp.concatenate([first, far_first], 0)
    second = jnp.concatenate([second, far_second], 0)
    return first, second


def reorder(first_bits, chips):
    places = []
    for position in range(chips):
        value = 0
        for at, bit in enumerate(first_bits):
            value |= ((position >> at) & 1) << bit
        places.append(value)
    return places


def on_device(
    inputs,
    cotangent,
    lengths,
    query_key,
    value_proj,
    output_proj,
    hidden_in,
    hidden_out,
    first_gain,
    second_gain,
    third_gain,
    fourth_gain,
):
    rows, width = inputs.shape[1:]
    chips = lax.axis_size(CHIPS)
    inner = lax.axis_size("inner")
    chip = lax.axis_index(CHIPS)
    core = lax.axis_index(CORES)
    depth = width // chips
    pairwise = chips & (chips - 1) == 0 and chips >= 4 and depth % 16 == 0
    series = inputs[0]
    scalars = jnp.stack([chip, core, lengths[0]]).astype(jnp.int32)
    scalars = jnp.concatenate([scalars, jnp.zeros((5,), jnp.int32)])

    gain_columns = jnp.stack([first_gain, second_gain, third_gain], 1)
    gain_columns = jnp.pad(gain_columns, ((0, 0), (0, 256 - 3)))
    shard = jnp.concatenate([query_key, value_proj, output_proj, gain_columns], 1)
    half = shard.shape[1] // 2
    ffn_shard = jnp.concatenate([hidden_in, hidden_out.T], 1)
    if pairwise:
        kept_part = lax.dynamic_slice_in_dim(shard, core * half, half, 1)
        sent_part = lax.dynamic_slice_in_dim(shard, (1 - core) * half, half, 1)
        chip_rows = by_core(kept_part, other_core(sent_part), 0)
        first, second = gather_pairwise(chip_rows, chips)
        bits = list(range(2, bit_count(chips)))
        stacks = []
        for stack, order in ((first, bits + [1, 0]), (second, bits + [0, 1])):
            stacks.append((stack, order))
        parts = [s for s, _ in stacks]
        parts = parts + [other_core(p) for p in parts]
        orders = [reorder(o, chips) for _, o in stacks]
        weights, out_weights, gains = assemble_ordered(parts, scalars, orders, chips, depth)
    else:
        gathered = lax.all_gather(shard, CHIPS + (CORES,), axis=0, tiled=True)
        weights, out_weights = gathered[:, : 3 * width], gathered[:, 3 * width : 4 * width]
        gains = gathered[:, 4 * width : 4 * width + 8].astype(F32).T
    ffn_weights = lax.all_gather(ffn_shard, CHIPS, axis=0, tiled=True)

    kept = (core * rows + jnp.arange(rows) < lengths[0])[:, None]
    near_grad = jnp.where(kept, cotangent[0], jnp.zeros((), BF16))
    far_grad = other_core(near_grad)

    queries, keys, values, normed = project(series, weights, gains, scalars)
    far_keys, far_values = (
        lax.ppermute(keys, CORES, [(0, 1)]),
        lax.ppermute(values, CORES, [(0, 1)]),
    )
    attended, logs = attend(queries, keys, values, far_keys, far_values, scalars)
    sub_low, middle, near = join(attended, series, out_weights, gains, scalars)
    far = other_core(near)

    act, slope, stats = ffn_in(near, far, ffn_weights, scalars)
    far_stats = other_core(stats)
    if pairwise and chips % inner == 0:
        outer = chips // inner
        order = [o * inner + i for i in range(inner) for o in range(outer)]
    else:
        order = list(range(chips))
    gain_four = fourth_gain.astype(F32)[None, :]
    branch, scaled, grad_stats, fourth_term, out_payload = ffn_out(
        act, stats, far_stats, gain_four, near_grad, far_grad, ffn_weights, scalars, order
    )
    far_grad_stats = other_core(grad_stats)
    far_branch = other_core(branch[rows:])
    ffn_grad, in_payload = ffn_back(
        act, slope, scaled, stats, far_stats, grad_stats, far_grad_stats, near, far, ffn_weights, scalars, order
    )
    far_ffn_grad = other_core(ffn_grad[rows:])

    outputs, middle_grad, attended_low, o_keep, o_send, terms = join_back(
        branch, far_branch, ffn_grad, far_ffn_grad, middle, near_grad, sub_low, attended, out_weights, gains, scalars
    )
    o_payload = (o_keep.astype(F32) + other_core(o_send).astype(F32)).astype(BF16)

    def scatter_chips(payload):
        if pairwise:
            payload = lax.psum_scatter(payload, "inner", scatter_dimension=0, tiled=True)
            return lax.psum_scatter(payload, "outer", scatter_dimension=0, tiled=True)
        return lax.psum_scatter(payload, CHIPS, scatter_dimension=0, tiled=True)

    if pairwise:
        o_payload = jnp.concatenate([o_payload[b * depth : (b + 1) * depth] for b in order], 0)
    hidden_out_sum = scatter_chips(out_payload).astype(F32).T
    joined = scatter_chips(jnp.concatenate([in_payload, o_payload], 1)).astype(F32)
    units = hidden_in.shape[1]
    hidden_in_sum, o_half = joined[:, :units], joined[:, units:]

    dq, dk, dv, far_dk, far_dv = attend_back(
        queries, keys, values, far_keys, far_values, attended_low, attended, logs, scalars
    )
    far_dk = lax.ppermute(far_dk, CORES, [(1, 0)])
    far_dv = lax.ppermute(far_dv, CORES, [(1, 0)])
    block_count = chips if pairwise else 1
    dk_low, dv_low, keep, send = project_grads(normed, dq, dk, far_dk, dv, far_dv, scalars, block_count)
    inputs_grad, first_term = project_back(dq, dk_low, dv_low, series, middle_grad, weights, gains, scalars)

    shared = jnp.concatenate([first_term[0:1], terms[1:3]], 0)
    fourth = fourth_term[0:1]
    mine = (keep.astype(F32) + other_core(send).astype(F32)).astype(BF16)
    shared = shared + other_core(shared)
    gain_vector = jnp.concatenate([shared.reshape(1, -1), fourth], 1)
    if pairwise:
        attention_part = scatter_pairwise(mine, chips).astype(F32)
        for bit in range(bit_count(chips)):
            gain_vector = gain_vector + exchange(gain_vector, bit, chips)
    else:
        attention_part = lax.psum_scatter(mine[0], CHIPS, scatter_dimension=0, tiled=True).astype(F32)
        gain_vector = lax.psum(gain_vector, CHIPS)
    attention_half = jnp.concatenate([attention_part, o_half], 1)

    own = depth // 2
    kept_part = lax.dynamic_slice_in_dim(attention_half, core * own, own, 0)
    sent_part = lax.dynamic_slice_in_dim(attention_half, (1 - core) * own, own, 0)
    got = other_core(sent_part)
    cut = attention_part.shape[1]
    attention_rows = by_core(kept_part[:, :cut], got[:, :cut], 1)
    output_sum = by_core(kept_part[:, cut:], got[:, cut:], 1)
    qk_sum, value_sum = attention_rows[:, : 2 * width], attention_rows[:, 2 * width :]

    start = chip * depth + core * own
    pieces = [
        lax.dynamic_slice_in_dim(gain_vector[0], at * width + start, own, 0) for at in range(3)
    ]
    fourth_sum = gain_vector[0, 3 * width :]
    return (
        outputs[None],
        inputs_grad[None],
        qk_sum,
        value_sum,
        output_sum,
        hidden_in_sum,
        hidden_out_sum,
        *pieces,
        fourth_sum,
    )


def assemble_ordered(parts, scalars, orders, blocks, depth):
    widths = [p.shape[2] for p in parts[:2]]
    half = sum(widths)
    rows = blocks * depth

    def body(s_ref, *refs):
        ins, (w_ref, o_ref, g_ref, full) = refs[: len(parts)], refs[len(parts) :]
        me, core = s_ref[0], s_ref[1]
        for side in range(2):
            base = (core if side == 0 else 1 - core) * half
            for k, width in enumerate(widths):
                src = ins[side * 2 + k]
                column = pl.multiple_of(base + sum(widths[:k]), 128)
                for at, place in enumerate(orders[k]):
                    row = pl.multiple_of((me ^ place) * depth, 16)
                    full[pl.ds(row, depth), pl.ds(column, width)] = src[at]
        w_ref[...] = full[:, 0 : 3 * rows]
        o_ref[...] = full[:, 3 * rows : 4 * rows]
        gains = full[:, 4 * rows : 4 * rows + 128].astype(F32)
        g_ref[...] = jnp.transpose(gains)[0:8]

    return call(
        body,
        "assemble",
        (shaped((rows, 3 * rows), BF16), shaped((rows, rows), BF16), shaped((8, rows), F32)),
        (1,),
        [whole(p.shape) for p in parts],
        (whole((rows, 3 * rows)), whole((rows, rows)), whole((8, rows))),
        scratch=[pltpu.VMEM((rows, 2 * half), BF16)],
        nbytes=rows * half * 8,
    )(scalars, *parts)


def scatter_pairwise(stack, chips):
    bits = bit_count(chips)
    columns = stack.shape[2]
    cut = -(-columns // 256) * 128

    def halves(held, axis):
        kept = lax.index_in_dim(held, 0, axis, keepdims=False)
        sent = lax.index_in_dim(held, 1, axis, keepdims=False)
        return kept, sent

    def add(kept, got):
        return (kept.astype(F32) + got.astype(F32)).astype(BF16)

    cube = stack.reshape((chips // 4, 2, 2) + stack.shape[1:])
    first, second = cube[..., :cut], cube[..., cut:]
    kept_first, sent_first = halves(first, 2)
    kept_second, sent_second = halves(second, 1)
    first = add(kept_first, exchange(sent_first, 0, chips))
    second = add(kept_second, exchange(sent_second, 1, chips))
    kept_first, sent_first = halves(first, 1)
    kept_second, sent_second = halves(second, 1)
    first = add(kept_first, exchange(sent_first, 1, chips))
    second = add(kept_second, exchange(sent_second, 0, chips))
    held = jnp.concatenate([first, second], -1)
    for bit in range(2, bits):
        held = held.reshape((held.shape[0] // 2, 2) + held.shape[1:])
        kept, sent = halves(held, 1)
        held = add(kept, exchange(sent, bit, chips))
    return held.reshape(stack.shape[1:])


def solution(mesh):
    chips, cores = mesh.devices.shape
    inner = 4 if chips % 4 == 0 else 1
    split = Mesh(mesh.devices.reshape(chips // inner, inner, cores), CHIPS + (CORES,))
    every = CHIPS + (CORES,)
    return jax.shard_map(
        on_device,
        mesh=split,
        in_specs=(
            P(CHIPS, CORES, None),
            P(CHIPS, CORES, None),
            P(CHIPS),
            P(every, None),
            P(every, None),
            P(every, None),
            P(CHIPS, CORES),
            P(CORES, CHIPS),
            P(every),
            P(every),
            P(every),
            P(CORES),
        ),
        out_specs=(
            P(CHIPS, CORES, None),
            P(CHIPS, CORES, None),
            P(every, None),
            P(every, None),
            P(every, None),
            P(CHIPS, CORES),
            P(CORES, CHIPS),
            P(every),
            P(every),
            P(every),
            P(CORES),
        ),
        check_vma=False,
    )
```

```python
import jax
import jax.numpy as jnp
from jax import lax
from jax.experimental import pallas as pl
from jax.experimental.pallas import tpu as pltpu
from jax.sharding import Mesh
from jax.sharding import PartitionSpec as P

HEAD_DIM = 64
PAIR = 2 * HEAD_DIM
EPSILON = 1e-05
MASKED = -1000000000.0
F32 = jnp.float32
BF16 = jnp.bfloat16
VMEM_LIMIT = 60 * 1024 * 1024
TILE = 256
EXTRA = 16
COST_SCALE = 0.5
COSTS = {
    "project": 8,
    "attend": 15,
    "join": 5,
    "ffn_in": 10,
    "ffn_out": 17,
    "ffn_back": 15,
    "join_back": 7,
    "attend_back": 12,
    "project_grads": 6,
    "project_back": 7,
}


def mm(former, latter):
    return jnp.dot(former, latter, preferred_element_type=F32)


def mm_tail(former, latter):
    return lax.dot_general(former, latter, (((1,), (1,)), ((), ())), preferred_element_type=F32)


def mm_lead(former, latter):
    return lax.dot_general(former, latter, (((0,), (0,)), ((), ())), preferred_element_type=F32)


def call(body, name, out_shape, grid, in_specs, out_specs, scratch=(), aliases=None):
    return pl.pallas_call(
        body,
        name=name,
        out_shape=out_shape,
        grid_spec=pltpu.PrefetchScalarGridSpec(
            num_scalar_prefetch=1,
            grid=grid,
            in_specs=in_specs,
            out_specs=out_specs,
            scratch_shapes=list(scratch),
        ),
        input_output_aliases=aliases or {},
        compiler_params=pltpu.CompilerParams(vmem_limit_bytes=VMEM_LIMIT),
        cost_estimate=pl.CostEstimate(
            flops=1, bytes_accessed=int(COST_SCALE * COSTS[name] * 3690000), transcendentals=0
        ),
    )


def shaped(shape, kind):
    return jax.ShapeDtypeStruct(shape, kind)


def whole(shape):
    return pl.BlockSpec(shape, lambda i, s: (0,) * len(shape))


def rows_of(shape):
    return pl.BlockSpec(shape, lambda i, s: (i, 0))


def norm_stats(series):
    center = jnp.mean(series, -1, keepdims=True)
    spread = jnp.mean(series * series, -1, keepdims=True) - center * center
    inverse = lax.rsqrt(spread + EPSILON)
    return (series - center) * inverse, inverse


def norm_back(grad, gain, hat, inverse):
    scaled = grad * gain
    first = jnp.mean(scaled, -1, keepdims=True)
    second = jnp.mean(scaled * hat, -1, keepdims=True)
    return inverse * (scaled - first - hat * second)


def put_blocks(s_ref, pieces, places, target, column, width):
    at = 0
    for piece in pieces:
        depth = piece.shape[1]
        for block in range(piece.shape[0]):
            row = (s_ref[0] ^ places[at]) * depth
            if depth % 16 == 0:
                row = pl.multiple_of(row, 16)
            target[pl.ds(row, depth), pl.ds(column, width)] = piece[block]
            at += 1


def project(inputs, parts, places, scalars):
    rows, width = inputs.shape
    tile = min(TILE, rows)
    flat = [piece for half in parts for part in half for piece in part]
    cuts = [part[0].shape[2] for part in parts[0]]
    half_columns = sum(cuts)

    def body(s_ref, x_ref, *refs):
        pieces, (q_ref, kv_ref, n_ref, w_ref, o_ref, g_ref, full) = refs[: len(flat)], refs[len(flat) :]
        core = s_ref[1]

        @pl.when(pl.program_id(0) == 0)
        def _():
            at = 0
            for side in range(len(parts)):
                base = (core if side == 0 else 1 - core) * half_columns if len(parts) == 2 else 0
                for k, part in enumerate(parts[side]):
                    column = base + sum(cuts[:k])
                    if len(parts) == 2:
                        column = pl.multiple_of(column, 128)
                    put_blocks(s_ref, pieces[at : at + len(part)], places[k], full, column, cuts[k])
                    at += len(part)
            w_ref[...] = full[:, 0 : 3 * width]
            o_ref[...] = full[:, 3 * width : 4 * width]
            g_ref[...] = jnp.transpose(full[:, 4 * width : 4 * width + 128].astype(F32))[0:8]

        hat, _ = norm_stats(x_ref[...].astype(F32))
        low = (hat * g_ref[0:1, :]).astype(BF16)
        n_ref[...] = low
        q_ref[...] = mm(low, full[:, 0:width]).astype(BF16)
        for which in range(2):
            part = mm(low, full[:, (1 + which) * width : (2 + which) * width]).astype(BF16)
            for pair in range(width // PAIR):
                at = (2 * pair + which) * PAIR
                kv_ref[:, at : at + PAIR] = part[:, pair * PAIR : (pair + 1) * PAIR]

    spec = rows_of((tile, width))
    return call(
        body,
        "project",
        (
            shaped((rows, width), BF16),
            shaped((rows, 2 * width), BF16),
            shaped((rows, width), BF16),
            shaped((width, 3 * width), BF16),
            shaped((width, width), BF16),
            shaped((8, width), F32),
        ),
        (rows // tile,),
        [spec] + [whole(p.shape) for p in flat],
        (spec, rows_of((tile, 2 * width)), spec, whole((width, 3 * width)), whole((width, width)), whole((8, width))),
        scratch=[pltpu.VMEM((width, half_columns * len(parts)), BF16)],
    )(scalars, inputs, *flat)


def lane_of(head):
    lanes = lax.broadcasted_iota(jnp.int32, (1, PAIR), 1)
    return (lanes >= head * HEAD_DIM) & (lanes < (head + 1) * HEAD_DIM)


def attend(queries, near, far_side, scalars):
    rows, width = queries.shape
    tile = min(TILE, rows)
    pairs = width // PAIR

    def body(s_ref, q_ref, kv_ref, fkv_ref, o_ref, l_ref):
        offset = s_ref[1] * rows
        length = s_ref[2]

        def run(far):
            query = q_ref[...] * jnp.asarray(0.125, BF16)
            for t in range(rows // tile):
                end = (t + 1) * tile
                place = lax.broadcasted_iota(jnp.int32, (tile, end), 0) + t * tile
                key_at = lax.broadcasted_iota(jnp.int32, (tile, end), 1)
                allowed = (key_at <= place) & (key_at + offset < length)
                sums = []
                logs = []
                for head in range(2):
                    mine = jnp.where(
                        lane_of(head), query[t * tile : end], jnp.zeros((), BF16)
                    )
                    scores = jnp.where(allowed, mm_tail(mine, kv_ref[0:end, 0:PAIR]), MASKED)
                    highest = jnp.max(scores, -1, keepdims=True)
                    if far:
                        beyond = mm_tail(mine, fkv_ref[:, 0:PAIR])
                        highest = jnp.maximum(highest, jnp.max(beyond, -1, keepdims=True))
                        beyond = jnp.exp(beyond - highest)
                    scores = jnp.exp(scores - highest)
                    total = jnp.sum(scores, -1, keepdims=True)
                    mixed = mm(scores.astype(BF16), kv_ref[0:end, PAIR : 2 * PAIR])
                    if far:
                        total = total + jnp.sum(beyond, -1, keepdims=True)
                        mixed = mixed + mm(beyond.astype(BF16), fkv_ref[:, PAIR : 2 * PAIR])
                    sums.append(mixed / total)
                    logs.append(jnp.broadcast_to(highest + jnp.log(total), (tile, PAIR)))
                o_ref[t * tile : end] = jnp.where(lane_of(0), sums[0], sums[1])
                l_ref[t * tile : end] = jnp.where(lane_of(0), logs[0], logs[1])

        @pl.when(s_ref[1] == 0)
        def _():
            run(False)

        @pl.when(s_ref[1] != 0)
        def _():
            run(True)

    spec = pl.BlockSpec((rows, PAIR), lambda i, s: (0, i))
    both = pl.BlockSpec((rows, 2 * PAIR), lambda i, s: (0, i))
    return call(
        body,
        "attend",
        (shaped((rows, width), F32), shaped((rows, width), F32)),
        (pairs,),
        [spec, both, both],
        (spec, spec),
    )(scalars, queries, near, far_side)


def attend_back(queries, near, far_side, grads, attended, logs, scalars, first, pairs):
    rows = queries.shape[0]
    tile = min(TILE, rows)
    width = pairs * PAIR

    def body(
        s_ref, q_ref, kv_ref, fkv_ref, d_ref, o_ref, l_ref,
        dq_ref, dkv_ref, fdkv_ref,
    ):
        offset = s_ref[1] * rows
        length = s_ref[2]

        def run(far):
            query = q_ref[...] * jnp.asarray(0.125, BF16)
            grad = d_ref[...]
            log_rows = jnp.transpose(l_ref[...])
            picker = jnp.where(
                lax.broadcasted_iota(jnp.int32, (8, PAIR), 1) // HEAD_DIM
                == lax.broadcasted_iota(jnp.int32, (8, PAIR), 0),
                1.0,
                0.0,
            ).astype(F32)
            dots = lax.dot_general(
                picker,
                grad.astype(F32) * o_ref[...],
                (((1,), (1,)), ((), ())),
                precision=lax.Precision.HIGHEST,
                preferred_element_type=F32,
            )
            blocks = [
                (kv_ref, dkv_ref, t * tile, t * tile, True)
                for t in range(rows // tile)
            ]
            if far:
                blocks += [
                    (fkv_ref, fdkv_ref, t * tile, 0, False)
                    for t in range(rows // tile)
                ]
            turned = [[jnp.zeros((HEAD_DIM, tile), F32) for _ in range(rows // tile)] for _ in range(2)]
            for pair_ref, dpair_ref, at, low, masked in blocks:
                key = pair_ref[at : at + tile, 0:PAIR]
                value = pair_ref[at : at + tile, PAIR : 2 * PAIR]
                key_turned = jnp.transpose(key)
                count = rows - low
                kgrads, vgrads = [], []
                if masked:
                    key_at = lax.broadcasted_iota(jnp.int32, (tile, count), 0) + at
                    place = lax.broadcasted_iota(jnp.int32, (tile, count), 1) + low
                    allowed = (key_at <= place) & (key_at + offset < length)
                for head in range(2):
                    lanes = lane_of(head)
                    mine = jnp.where(lanes, query[low:rows], jnp.zeros((), BF16))
                    mine_grad = jnp.where(lanes, grad[low:rows], jnp.zeros((), BF16))
                    scores = mm_tail(key, mine)
                    if masked:
                        scores = jnp.where(allowed, scores, MASKED)
                    base = head * HEAD_DIM
                    probs = jnp.exp(scores - log_rows[base : base + 1, low:rows])
                    prob_grad = mm_tail(value, mine_grad)
                    score_grad = (probs * (prob_grad - dots[head : head + 1, low:rows])).astype(BF16)
                    vgrads.append(mm(probs.astype(BF16), grad[low:rows]))
                    kgrads.append(mm(score_grad, query[low:rows]))
                    part = mm(key_turned[base : base + HEAD_DIM], score_grad)
                    for t in range(low // tile, rows // tile):
                        turned[head][t] = turned[head][t] + part[:, t * tile - low : (t + 1) * tile - low]
                dpair_ref[at : at + tile, 0:PAIR] = jnp.where(lane_of(0), kgrads[0], kgrads[1]).astype(dpair_ref.dtype)
                dpair_ref[at : at + tile, PAIR : 2 * PAIR] = jnp.where(lane_of(0), vgrads[0], vgrads[1]).astype(dpair_ref.dtype)
            for t in range(rows // tile):
                both = jnp.concatenate([turned[0][t], turned[1][t]], 0)
                dq_ref[t * tile : (t + 1) * tile] = (jnp.transpose(both) * 0.125).astype(BF16)

        @pl.when(s_ref[1] == 0)
        def _():
            run(False)
            fdkv_ref[...] = jnp.zeros_like(fdkv_ref)

        @pl.when(s_ref[1] != 0)
        def _():
            run(True)

    spec = pl.BlockSpec((rows, PAIR), lambda i, s: (0, i + first))
    both = pl.BlockSpec((rows, 2 * PAIR), lambda i, s: (0, i + first))
    own = pl.BlockSpec((rows, PAIR), lambda i, s: (0, i))
    own_both = pl.BlockSpec((rows, 2 * PAIR), lambda i, s: (0, i))
    return call(
        body,
        "attend_back",
        (shaped((rows, width), BF16), shaped((rows, 2 * width), F32), shaped((rows, 2 * width), BF16)),
        (pairs,),
        [spec, both, both, spec, spec, spec],
        (own, own_both, own_both),
    )(scalars, queries, near, far_side, grads, attended, logs)


def join(attended, inputs, weights, gains, scalars):
    rows, width = attended.shape
    tile = min(TILE, rows)

    def body(s_ref, a_ref, x_ref, w_ref, g_ref, sub_ref, mid_ref, ffn_ref):
        hat, _ = norm_stats(a_ref[...])
        low = (hat * g_ref[1:2, :]).astype(BF16)
        sub_ref[...] = low
        middle = x_ref[...].astype(F32) + mm(low, w_ref[...])
        mid_ref[...] = middle
        hat, _ = norm_stats(middle)
        ffn_ref[...] = (hat * g_ref[2:3, :]).astype(BF16)

    spec = rows_of((tile, width))
    return call(
        body,
        "join",
        (shaped((rows, width), BF16), shaped((rows, width), F32), shaped((rows, width), BF16)),
        (rows // tile,),
        [spec, spec, whole((width, width)), whole((8, width))],
        (spec,) * 3,
    )(scalars, attended, inputs, weights, gains)


def join_back(branch, far_branch, fgrad, far_fgrad, middle, cotangent, attended, weights, gains, scalars):
    rows, width = middle.shape
    tile = min(TILE, rows)
    steps = rows // tile

    def body(
        s_ref, b_ref, fb_ref, f_ref, ff_ref, m_ref, c_ref, a_ref, w_ref, g_ref,
        out_ref, mg_ref, ml_ref, ag_ref,
    ):
        step = pl.program_id(0)
        places = lax.broadcasted_iota(jnp.int32, (tile, 1), 0) + (step * tile + s_ref[1] * rows)
        kept = (places < s_ref[2]).astype(F32)
        middle = m_ref[...]
        branch = b_ref[...].astype(F32) + fb_ref[...].astype(F32)
        out_ref[...] = (kept * (middle + branch)).astype(BF16)
        hat, inverse = norm_stats(middle)
        grad = f_ref[...].astype(F32) + ff_ref[...].astype(F32)
        middle_grad = c_ref[...].astype(F32) * kept + norm_back(grad, g_ref[2:3, :], hat, inverse)
        mg_ref[...] = middle_grad
        low = middle_grad.astype(BF16)
        ml_ref[...] = low
        sub_grad = mm_tail(low, w_ref[...])
        hat, inverse = norm_stats(a_ref[...])
        ag_ref[...] = norm_back(sub_grad, g_ref[1:2, :], hat, inverse).astype(BF16)

    spec = rows_of((tile, width))
    return call(
        body,
        "join_back",
        (
            shaped((rows, width), BF16),
            shaped((rows, width), F32),
            shaped((rows, width), BF16),
            shaped((rows, width), BF16),
        ),
        (steps,),
        [spec] * 7 + [whole((width, width)), whole((8, width))],
        (spec,) * 4,
    )(scalars, branch, far_branch, fgrad, far_fgrad, middle, cotangent, attended, weights, gains)


def two_sided(tile, width, steps):
    near = pl.BlockSpec((tile, width), lambda i, s: (jnp.minimum(i, steps - 1), 0))
    far = pl.BlockSpec((tile, width), lambda i, s: (jnp.maximum(i - steps, 0), 0))
    return near, far


def lane_stats(first, second):
    lanes = lax.broadcasted_iota(jnp.int32, (first.shape[0], 128), 1)
    return jnp.where(lanes == 0, first, jnp.where(lanes == 1, second, 0.0))


def ffn_in(near, far, parts, places, scalars):
    rows, width = near.shape
    pieces = [piece for part in parts for piece in part]
    cuts = [part[0].shape[2] for part in parts]
    units = sum(cuts)
    tile = min(TILE, rows)
    steps = rows // tile
    chunk = 512 if units % 512 == 0 else units

    def body(s_ref, n_ref, f_ref, *refs):
        blocks, (act_ref, slope_ref, stat_ref, w_ref) = refs[: len(pieces)], refs[len(pieces) :]

        @pl.when(pl.program_id(0) == 0)
        def _():
            at = 0
            for k, part in enumerate(parts):
                put_blocks(s_ref, blocks[at : at + len(part)], places[k], w_ref, sum(cuts[:k]), cuts[k])
                at += len(part)

        def run(low):
            sums = jnp.zeros((tile, 1), F32)
            squares = jnp.zeros((tile, 1), F32)
            for at in range(0, units, chunk):
                pre = mm(low, w_ref[:, at : at + chunk])
                cdf = 0.5 * (1.0 + lax.erf(pre * 0.7071067811865476))
                pdf = 0.3989422804014327 * jnp.exp(-0.5 * pre * pre)
                act = pre * cdf
                act_ref[:, at : at + chunk] = act
                slope_ref[:, at : at + chunk] = (cdf + pre * pdf).astype(slope_ref.dtype)
                sums = sums + jnp.sum(act, -1, keepdims=True)
                squares = squares + jnp.sum(act * act, -1, keepdims=True)
            stat_ref[...] = lane_stats(sums, squares)

        @pl.when(pl.program_id(0) < steps)
        def _():
            run(n_ref[...])

        @pl.when(pl.program_id(0) >= steps)
        def _():
            run(f_ref[...])

    near_spec, far_spec = two_sided(tile, width, steps)
    return call(
        body,
        "ffn_in",
        (
            shaped((2 * rows, units), F32),
            shaped((2 * rows, units), BF16),
            shaped((2 * rows, 128), F32),
            shaped((width, units), BF16),
        ),
        (2 * steps,),
        [near_spec, far_spec] + [whole(p.shape) for p in pieces],
        (rows_of((tile, units)), rows_of((tile, units)), rows_of((tile, 128)), whole((width, units))),
    )(scalars, near, far, *pieces)


def swapped(tile, steps):
    return pl.BlockSpec((tile, 128), lambda i, s: (lax.rem(i + steps, 2 * steps), 0))


def unit_norm(stat, other, total):
    both = stat + other
    center = both[:, 0:1] / total
    inverse = lax.rsqrt(both[:, 1:2] / total - center * center + EPSILON)
    return center, inverse


def ffn_out(act, stats, far_stats, gain, near_grad, far_grad, pieces, places, scalars, order):
    rows, width = near_grad.shape
    units = act.shape[1]
    tile = min(TILE, rows)
    steps = rows // tile
    total_units = 2 * units
    depth = width // len(order)

    def body(
        s_ref, a_ref, st_ref, fs_ref, g_ref, n_ref, f_ref, *refs
    ):
        blocks = refs[: len(pieces)]
        b_ref, sg_ref, stat_ref, four_ref, out_ref, total = refs[1:]
        w_ref = blocks[0].at[0]
        step = pl.program_id(0)

        center, inverse = unit_norm(st_ref[...], fs_ref[...], total_units)
        gain = g_ref[...]

        def run(grad):
            hat = (a_ref[...] - center) * inverse
            low = (hat * gain).astype(BF16)
            b_ref[...] = mm_tail(low, w_ref[...]).astype(BF16)
            normed = mm(grad, w_ref[...])
            part = mm_lead(grad, low)
            scaled = normed * gain
            sg_ref[...] = scaled
            stat_ref[...] = lane_stats(
                jnp.sum(scaled, -1, keepdims=True), jnp.sum(scaled * hat, -1, keepdims=True)
            )
            fourth = jnp.sum(normed * hat, 0, keepdims=True)

            @pl.when(step == 0)
            def _():
                total[...] = part
                four_ref[...] = jnp.broadcast_to(fourth, four_ref.shape)

            @pl.when(step > 0)
            def _():
                total[...] += part
                four_ref[...] += jnp.broadcast_to(fourth, four_ref.shape)

        @pl.when(step < steps)
        def _():
            run(n_ref[...])

        @pl.when(step >= steps)
        def _():
            run(f_ref[...])

        @pl.when(step == 2 * steps - 1)
        def _():
            for at, block in enumerate(order):
                out_ref[at * depth : (at + 1) * depth] = total[
                    block * depth : (block + 1) * depth
                ].astype(BF16)

    near_spec, far_spec = two_sided(tile, width, steps)
    wide = rows_of((tile, units))
    return call(
        body,
        "ffn_out",
        (
            shaped((2 * rows, width), BF16),
            shaped((2 * rows, units), F32),
            shaped((2 * rows, 128), F32),
            shaped((8, units), F32),
            shaped((width, units), BF16),
        ),
        (2 * steps,),
        [
            wide,
            rows_of((tile, 128)),
            swapped(tile, steps),
            whole((1, units)),
            near_spec,
            far_spec,
        ]
        + [whole(p.shape) for p in pieces],
        (rows_of((tile, width)), wide, rows_of((tile, 128)), whole((8, units)), whole((width, units))),
        scratch=[pltpu.VMEM((width, units), F32)],
    )(scalars, act, stats, far_stats, gain, near_grad, far_grad, *pieces)


def ffn_back(act, slope, scaled, stats, far_stats, grads, far_grads, near, far, weights, fourth, scalars, blocks):
    rows, width = near.shape
    units = act.shape[1]
    tile = min(TILE, rows)
    steps = rows // tile
    total_units = 2 * units
    depth = width // blocks

    def body(
        s_ref, a_ref, sl_ref, sg_ref, st_ref, fs_ref, gt_ref, fg_ref, n_ref, f_ref, w_ref, four_ref,
        b_ref, *rest,
    ):
        outs, total = rest[:-1], rest[-1]
        step = pl.program_id(0)
        center, inverse = unit_norm(st_ref[...], fs_ref[...], total_units)
        both = gt_ref[...] + fg_ref[...]
        first = both[:, 0:1] / total_units
        second = both[:, 1:2] / total_units

        def run(low):
            hat = (a_ref[...] - center) * inverse
            act_grad = inverse * (sg_ref[...] - first - hat * second)
            pre = (act_grad * sl_ref[...].astype(F32)).astype(BF16)
            b_ref[...] = mm_tail(pre, w_ref[...]).astype(BF16)
            part = mm_lead(low, pre)

            @pl.when(step == 0)
            def _():
                total[...] = part

            @pl.when(step > 0)
            def _():
                total[...] += part

        @pl.when(step < steps)
        def _():
            run(n_ref[...])

        @pl.when(step >= steps)
        def _():
            run(f_ref[...])

        @pl.when(step == 2 * steps - 1)
        def _():
            if blocks == 1:
                outs[0][...] = total[...].astype(BF16)
            else:
                for position in range(blocks):
                    at = pl.multiple_of((s_ref[0] ^ position) * depth, 8)
                    to = (position >> 1) * depth
                    outs[position & 1][to : to + depth] = total[pl.ds(at, depth)].astype(BF16)
                value = four_ref[0:1, :]
                high = value.astype(BF16)
                rest_of = (value - high.astype(F32)).astype(BF16)
                at_row = lax.broadcasted_iota(jnp.int32, (EXTRA, units), 0)
                extra = jnp.where(at_row == 0, high.astype(F32), jnp.where(at_row == 1, rest_of.astype(F32), 0.0))
                outs[1][width // 2 : width // 2 + EXTRA] = extra.astype(BF16)

    near_spec, far_spec = two_sided(tile, width, steps)
    wide = rows_of((tile, units))
    thin = rows_of((tile, 128))
    shapes = ((width, units),) if blocks == 1 else ((width // 2, units), (width // 2 + EXTRA, units))
    return call(
        body,
        "ffn_back",
        (shaped((2 * rows, width), BF16),) + tuple(shaped(shape, BF16) for shape in shapes),
        (2 * steps,),
        [
            wide, wide, wide, thin, swapped(tile, steps), thin, swapped(tile, steps),
            near_spec, far_spec, whole((width, units)), whole((8, units)),
        ],
        (rows_of((tile, width)),) + tuple(whole(shape) for shape in shapes),
        scratch=[pltpu.VMEM((width, units), F32)],
    )(scalars, act, slope, scaled, stats, far_stats, grads, far_grads, near, far, weights, fourth)


def project_grads(normed, dq, dkv, far_dkv, extra, scalars, blocks):
    rows, width = normed.shape
    cols = dq.shape[1]
    depth = width // blocks
    total = 3 * cols + (width if extra else 0)
    half = total // 2
    pairs = cols // PAIR

    def body(s_ref, n_ref, q_ref, kv_ref, fkv_ref, *refs):
        if extra:
            left_ref, right_ref = refs[:2]
            refs = refs[2:]
        low_ref, keep_ref, send_ref, grad_ref = refs
        me, core = s_ref[0], s_ref[1]
        near = core == 0
        both = kv_ref[...] + jnp.where(near, fkv_ref[...].astype(F32), 0.0)
        low_ref[:, 0:cols] = q_ref[...]
        for pair in range(pairs):
            for which in range(2):
                to = (1 + which) * cols + pair * PAIR
                at = (2 * pair + which) * PAIR
                low_ref[:, to : to + PAIR] = both[:, at : at + PAIR].astype(BF16)
        turned = jnp.transpose(n_ref[...])
        grad_ref[:, 0 : 3 * cols] = mm(turned, low_ref[...]).astype(BF16)
        if extra:
            grad_ref[:, 3 * cols : total] = mm_lead(left_ref[...], right_ref[...]).astype(BF16)
        for side, out in ((0, keep_ref), (1, send_ref)):
            owner = core if side == 0 else 1 - core
            column = pl.multiple_of(owner * half, 128)
            for block in range(blocks):
                out[block ^ me] = grad_ref[block * depth : (block + 1) * depth, pl.ds(column, half)]

    more = list(extra) if extra else []
    return call(
        body,
        "project_grads",
        (
            shaped((rows, 3 * cols), BF16),
            shaped((blocks, depth, half), BF16),
            shaped((blocks, depth, half), BF16),
        ),
        (1,),
        [whole((rows, width)), whole((rows, cols)), whole((rows, 2 * cols)), whole((rows, 2 * cols))]
        + [whole((rows, width))] * len(more),
        (whole((rows, 3 * cols)), whole((blocks, depth, half)), whole((blocks, depth, half))),
        scratch=[pltpu.VMEM((width, total), BF16)],
    )(scalars, normed, dq, dkv, far_dkv, *more)


def project_back(lows, inputs, middle_grad, weights, gains, scalars):
    rows, width = inputs.shape
    tile = min(TILE, rows)
    sizes = [low.shape[1] // 3 for low in lows]

    def body(s_ref, *refs):
        low_refs, (x_ref, m_ref, w_ref, g_ref, out_ref) = refs[: len(lows)], refs[len(lows) :]
        hat, inverse = norm_stats(x_ref[...].astype(F32))
        grad = jnp.zeros((tile, width), F32)
        at = 0
        for low_ref, size in zip(low_refs, sizes):
            for which in range(3):
                base = which * width + at
                grad = grad + mm_tail(
                    low_ref[:, which * size : (which + 1) * size], w_ref[:, base : base + size]
                )
            at += size
        out_ref[...] = (m_ref[...] + norm_back(grad, g_ref[0:1, :], hat, inverse)).astype(BF16)

    spec = rows_of((tile, width))
    return call(
        body,
        "project_back",
        shaped((rows, width), BF16),
        (rows // tile,),
        [rows_of((tile, 3 * size)) for size in sizes]
        + [spec, spec, whole((width, 3 * width)), whole((8, width))],
        spec,
    )(scalars, *lows, inputs, middle_grad, weights, gains)


CHIPS = ("outer", "inner")
CORES = "tensor"


def other_core(array):
    return lax.ppermute(array, CORES, [(0, 1), (1, 0)])


def exchange(array, bit, chips):
    return lax.ppermute(array, CHIPS, [(i, i ^ (1 << bit)) for i in range(chips)])


def bit_count(chips):
    return chips.bit_length() - 1


def by_core(mine, other, axis):
    core = lax.axis_index(CORES)
    return jnp.where(
        core == 0,
        jnp.concatenate([mine, other], axis),
        jnp.concatenate([other, mine], axis),
    )


def after(value, *others):
    return lax.optimization_barrier((value,) + others)[0]


def gather_outer(shard, chips):
    held = shard[None]
    places = [0]
    for bit in reversed(range(2, bit_count(chips))):
        held = jnp.concatenate([held, exchange(held, bit, chips)], 0)
        places = places + [p | (1 << bit) for p in places]
    return held, places


def widen(pieces, places, bit, chips):
    held = pieces[0] if len(pieces) == 1 else jnp.concatenate(pieces, 0)
    return pieces + [exchange(held, bit, chips)], places + [p | (1 << bit) for p in places]


def on_device(
    inputs,
    cotangent,
    lengths,
    query_key,
    value_proj,
    output_proj,
    hidden_in,
    hidden_out,
    first_gain,
    second_gain,
    third_gain,
    fourth_gain,
):
    rows, width = inputs.shape[1:]
    chips = lax.axis_size(CHIPS)
    inner = lax.axis_size("inner")
    chip = lax.axis_index(CHIPS)
    core = lax.axis_index(CORES)
    depth = width // chips
    pairwise = chips & (chips - 1) == 0 and chips >= 4 and depth % 16 == 0
    series = inputs[0]
    scalars = jnp.stack([chip if pairwise else jnp.zeros_like(chip), core, lengths[0]]).astype(jnp.int32)
    scalars = jnp.concatenate([scalars, jnp.zeros((5,), jnp.int32)])

    gain_columns = jnp.stack([first_gain, second_gain, third_gain], 1)
    gain_columns = jnp.pad(gain_columns, ((0, 0), (0, 256 - 3)))
    shard = jnp.concatenate([query_key, value_proj, output_proj, gain_columns], 1)
    half = shard.shape[1] // 2
    units = hidden_in.shape[1]
    if pairwise:
        kept_part = lax.dynamic_slice_in_dim(shard, core * half, half, 1)
        sent_part = lax.dynamic_slice_in_dim(shard, (1 - core) * half, half, 1)
        chip_rows = by_core(kept_part, other_core(sent_part), 0)
        stack, places = gather_outer(chip_rows, chips)
        cut = -(-half // 256) * 128
        first, first_places = widen([stack[:, :, :cut]], places, 1, chips)
        second, second_places = widen([stack[:, :, cut:]], places, 0, chips)
        in_stack, in_places = after(hidden_in, stack)[None], [0]
        outer_bits = list(reversed(range(2, bit_count(chips))))
        for step, bit in enumerate(outer_bits):
            in_stack = jnp.concatenate([in_stack, exchange(in_stack, bit, chips)], 0)
            in_places = in_places + [p | (1 << bit) for p in in_places]
            if step == 0:
                first[-1], second[-1], in_stack = lax.optimization_barrier((first[-1], second[-1], in_stack))
                first, first_places = widen(first, first_places, 0, chips)
                second, second_places = widen(second, second_places, 1, chips)
        first[-1], second[-1], in_stack = lax.optimization_barrier((first[-1], second[-1], in_stack))
        middle_unit = units // 2
        in_first, in_first_places = widen([in_stack[:, :, :middle_unit]], in_places, 0, chips)
        in_second, in_second_places = widen([in_stack[:, :, middle_unit:]], in_places, 1, chips)
        out_pieces, out_places = [lax.all_gather(hidden_out.T, CHIPS, axis=0, tiled=True)[None]], [0]
        mine = [jnp.concatenate(first, 0), jnp.concatenate(second, 0)]
        parts = [[[p] for p in mine], [[other_core(p)] for p in mine]]
        part_places = [first_places, second_places]
    else:
        gathered = lax.all_gather(shard, CHIPS + (CORES,), axis=0, tiled=True)
        parts, part_places = [[[gathered[None]]]], [[0]]
        in_parts = [[lax.all_gather(hidden_in, CHIPS, axis=0, tiled=True)[None]]]
        in_part_places = [[0]]
        out_pieces, out_places = [lax.all_gather(hidden_out.T, CHIPS, axis=0, tiled=True)[None]], [0]

    kept = (core * rows + jnp.arange(rows) < lengths[0])[:, None]
    near_grad = jnp.where(kept, cotangent[0], jnp.zeros((), BF16))
    far_grad = other_core(near_grad)

    queries, near_kv, normed, weights, out_weights, gains = project(series, parts, part_places, scalars)
    far_kv = lax.ppermute(near_kv, CORES, [(0, 1)])
    if pairwise:
        far_kv, in_first[-1], in_second[-1] = lax.optimization_barrier((far_kv, in_first[-1], in_second[-1]))
        in_first, in_first_places = widen(in_first, in_first_places, 1, chips)
        in_second, in_second_places = widen(in_second, in_second_places, 0, chips)
        in_parts = [in_first, in_second]
        in_part_places = [in_first_places, in_second_places]
    attended, logs = attend(queries, near_kv, far_kv, scalars)
    if pairwise:
        attended, in_first[-1], in_second[-1] = lax.optimization_barrier((attended, in_first[-1], in_second[-1]))
    sub_low, middle, near = join(attended, series, out_weights, gains, scalars)
    far = other_core(near)

    act, slope, stats, in_weights = ffn_in(near, far, in_parts, in_part_places, scalars)
    far_stats = other_core(stats)
    outer = chips // inner
    order = list(range(chips))
    if pairwise:
        order = [o * inner + i for i in range(inner) for o in range(outer)]
    gain_four = fourth_gain.astype(F32)[None, :]
    branch, scaled, grad_stats, fourth_term, out_payload = ffn_out(
        act, stats, far_stats, gain_four, near_grad, far_grad, out_pieces, out_places, scalars, order
    )
    if pairwise:
        out_payload = lax.psum_scatter(out_payload, "inner", scatter_dimension=0, tiled=True)
    else:
        out_payload = lax.psum_scatter(out_payload, CHIPS, scatter_dimension=0, tiled=True)
    far_grad_stats = other_core(grad_stats)
    far_branch = other_core(branch[rows:])
    blocks = chips if pairwise else 1
    ffn_grad, *in_payload = ffn_back(
        act, slope, scaled, stats, far_stats, grad_stats, far_grad_stats, near, far, in_weights, fourth_term, scalars, blocks
    )
    far_ffn_grad = other_core(ffn_grad[rows:])
    if pairwise:
        got = exchange(in_payload[1], 0, chips)
    outputs, middle_grad, middle_low, attended_low = join_back(
        branch, far_branch, ffn_grad, far_ffn_grad, middle, near_grad, attended, out_weights, gains, scalars
    )

    pairs = width // PAIR
    counts = (pairs - pairs // 3, pairs // 3)
    extra = (sub_low, middle_low)
    barrier = lax.optimization_barrier
    if pairwise:
        dq, dkv, far_dkv = attend_back(
            queries, near_kv, far_kv, attended_low, attended, logs, scalars, 0, counts[0]
        )
        got, dkv, out_payload, far_dkv = barrier((got, dkv, out_payload, far_dkv))
        out_payload = lax.psum_scatter(out_payload, "outer", scatter_dimension=0, tiled=True)
        far_dkv = lax.ppermute(far_dkv, CORES, [(1, 0)])
        in_held = add_low(in_payload[0], got[: width // 2]).reshape(chips // 2, depth, units)
        fourth = add_rows(fourth_term[0:1], got[width // 2 :])
        kept, sent = halve_send(in_held, fourth)
        far_dkv, kept, sent = barrier((far_dkv, kept, sent))
        got = exchange(sent, 1, chips)
        low_one, keep, send = project_grads(normed, dq, dkv, far_dkv, extra, scalars, chips)
        queries, keep, send = barrier((queries, keep, send))
        other = other_core(send)
        dq, dkv, far_dkv = attend_back(
            queries, near_kv, far_kv, attended_low, attended, logs, scalars, counts[0], counts[1]
        )
        got, other, dkv, far_dkv = barrier((got, other, dkv, far_dkv))
        far_dkv = lax.ppermute(far_dkv, CORES, [(1, 0)])
        in_held, fourth = halve_add(kept, fourth, got)
        kept, sent = halve_send(in_held, fourth)
        large = scatter_split(add_low(keep, other), chips)
        large_kept, large_sent = split_first(large)
        far_dkv, sent, large_sent = barrier((far_dkv, sent, large_sent))
        got = exchange(sent, 2, chips)
        large_got = exchange_first(large_sent, chips)
        low_two, keep, send = project_grads(normed, dq, dkv, far_dkv, None, scalars, chips)
        other = other_core(send)
        small = scatter_split(add_low(keep, other), chips)
        small_kept, small_sent = split_first(small)
        middle_grad, small_sent, small_kept = barrier((middle_grad, small_sent, small_kept))
        small_got = exchange_first(small_sent, chips)
        inputs_grad = project_back([low_one, low_two], series, middle_grad, weights, gains, scalars)
        inputs_grad, got, large_got, small_got = barrier((inputs_grad, got, large_got, small_got))
        in_held, fourth = halve_add(kept, fourth, got)
        both = [
            jnp.concatenate([add_low(lk, lg), add_low(sk, sg)], -1)
            for lk, lg, sk, sg in zip(large_kept, large_got, small_kept, small_got)
        ]
        kept_first, sent_first = split_pair(both[0], 1)
        kept_second, sent_second = split_pair(both[1], 1)
        got_first, got_second = exchange(sent_first, 1, chips), exchange(sent_second, 0, chips)
        for bit in range(3, bit_count(chips)):
            kept, sent = halve_send(in_held, fourth)
            in_held, fourth = halve_add(kept, fourth, exchange(sent, bit, chips))
        in_payload = in_held.reshape(depth, units)
        both = jnp.concatenate([add_low(kept_first, got_first), add_low(kept_second, got_second)], -1)
        for bit in range(2, bit_count(chips)):
            both = halve(both, bit, chips)
        both = both.reshape(depth, both.shape[-1])
        sizes = [large_kept[0].shape[-1], small_kept[0].shape[-1], large_kept[1].shape[-1], small_kept[1].shape[-1]]
        edges = [sum(sizes[:k]) for k in range(5)]
        held = [
            jnp.concatenate([both[:, edges[k] : edges[k + 1]], both[:, edges[k + 2] : edges[k + 3]]], 1)
            for k in range(2)
        ]
    else:
        lows, held = [], []
        for index, count in enumerate(counts):
            dq, dkv, far_dkv = attend_back(
                queries, near_kv, far_kv, attended_low, attended, logs, scalars, index * counts[0], count
            )
            far_dkv = lax.ppermute(far_dkv, CORES, [(1, 0)])
            low, keep, send = project_grads(
                normed, dq, dkv, far_dkv, extra if index == 0 else None, scalars, 1
            )
            lows.append(low)
            mine = add_low(keep, other_core(send))
            held.append(lax.psum_scatter(mine[0], CHIPS, scatter_dimension=0, tiled=True))
        inputs_grad = project_back(lows, series, middle_grad, weights, gains, scalars)
        in_payload = lax.psum_scatter(in_payload[0], CHIPS, scatter_dimension=0, tiled=True)
        fourth = lax.psum(fourth_term[0:1], CHIPS)
    hidden_out_sum = out_payload.astype(F32).T
    hidden_in_sum = in_payload.astype(F32)

    own = depth // 2
    together = jnp.concatenate(held, 1).astype(F32)
    third_part = jnp.sum(hidden_in.astype(F32) * hidden_in_sum, 1, keepdims=True)
    together = jnp.concatenate([together, jnp.broadcast_to(third_part, (depth, 128))], 1)
    kept_part = lax.dynamic_slice_in_dim(together, core * own, own, 0)
    sent_part = lax.dynamic_slice_in_dim(together, (1 - core) * own, own, 0)
    got = other_core(sent_part)
    cut = held[0].shape[1]
    end = cut + held[1].shape[1]
    large = by_core(kept_part[:, :cut], got[:, :cut], 1)
    small = by_core(kept_part[:, cut:end], got[:, cut:end], 1)
    third_sum = (kept_part[:, end] + got[:, end]) / third_gain.astype(F32)
    wide, thin = counts[0] * PAIR, counts[1] * PAIR
    qk_sum = jnp.concatenate(
        [large[:, :wide], small[:, :thin], large[:, wide : 2 * wide], small[:, thin : 2 * thin]], 1
    )
    value_sum = jnp.concatenate([large[:, 2 * wide : 3 * wide], small[:, 2 * thin :]], 1)
    output_sum = large[:, 3 * wide :]
    first_sum = (
        jnp.sum(query_key.astype(F32) * qk_sum, 1) + jnp.sum(value_proj.astype(F32) * value_sum, 1)
    ) / first_gain.astype(F32)
    second_sum = jnp.sum(output_proj.astype(F32) * output_sum, 1) / second_gain.astype(F32)
    return (
        outputs[None],
        inputs_grad[None],
        qk_sum,
        value_sum,
        output_sum,
        hidden_in_sum,
        hidden_out_sum,
        first_sum,
        second_sum,
        third_sum,
        fourth[0],
    )


def add_low(kept, got):
    return (kept.astype(F32) + got.astype(F32)).astype(BF16)


def add_rows(value, rows):
    return value + (rows[0:1].astype(F32) + rows[1:2].astype(F32))


def split_pair(held, axis):
    kept = lax.index_in_dim(held, 0, axis, keepdims=False)
    sent = lax.index_in_dim(held, 1, axis, keepdims=False)
    return kept, sent


def halve(held, bit, chips):
    kept, sent = split_pair(held.reshape((held.shape[0] // 2, 2) + held.shape[1:]), 1)
    return add_low(kept, exchange(sent, bit, chips))


def halve_send(held, vector):
    kept, sent = split_pair(held.reshape((held.shape[0] // 2, 2) + held.shape[1:]), 1)
    columns = held.shape[-1]
    high = lax.reduce_precision(vector, 8, 7)
    rest = lax.reduce_precision(vector - high, 8, 7)
    rows = jnp.concatenate([high, rest, jnp.zeros((EXTRA - 2, columns), F32)], 0).astype(BF16)
    return kept, jnp.concatenate([sent.reshape(-1, columns), rows], 0)


def halve_add(kept, vector, got):
    count = kept.shape[0] * kept.shape[1]
    return add_low(kept, got[:count].reshape(kept.shape)), add_rows(vector, got[count:])


def scatter_split(stack, chips):
    columns = stack.shape[2]
    cut = -(-columns // 256) * 128
    cube = stack.reshape((chips // 4, 2, 2) + stack.shape[1:])
    return cube[..., :cut], cube[..., cut:]


def split_first(part):
    kept_first, sent_first = split_pair(part[0], 2)
    kept_second, sent_second = split_pair(part[1], 1)
    return [kept_first, kept_second], [sent_first, sent_second]


def exchange_first(sent, chips):
    return [exchange(sent[0], 0, chips), exchange(sent[1], 1, chips)]


def solution(mesh):
    chips, cores = mesh.devices.shape
    inner = 4 if chips % 4 == 0 else 1
    split = Mesh(mesh.devices.reshape(chips // inner, inner, cores), CHIPS + (CORES,))
    every = CHIPS + (CORES,)
    return jax.shard_map(
        on_device,
        mesh=split,
        in_specs=(
            P(CHIPS, CORES, None),
            P(CHIPS, CORES, None),
            P(CHIPS),
            P(every, None),
            P(every, None),
            P(every, None),
            P(CHIPS, CORES),
            P(CORES, CHIPS),
            P(every),
            P(every),
            P(every),
            P(CORES),
        ),
        out_specs=(
            P(CHIPS, CORES, None),
            P(CHIPS, CORES, None),
            P(every, None),
            P(every, None),
            P(every, None),
            P(CHIPS, CORES),
            P(CORES, CHIPS),
            P(every),
            P(every),
            P(every),
            P(CORES),
        ),
        check_vma=False,
    )
```

```python
import jax
import jax.numpy as jnp
from jax import lax
from jax.experimental import pallas as pl
from jax.experimental.pallas import tpu as pltpu
from jax.sharding import Mesh
from jax.sharding import PartitionSpec as P

HEAD_DIM = 64
PAIR = 2 * HEAD_DIM
EPSILON = 1e-05
MASKED = -1000000000.0
F32 = jnp.float32
BF16 = jnp.bfloat16
VMEM_LIMIT = 60 * 1024 * 1024
TILE = 256
EXTRA = 16
COST_SCALE = 0.05
COSTS = {
    "project": 8,
    "attend": 15,
    "join": 5,
    "ffn_in": 10,
    "ffn_out": 10,
    "ffn_back": 14,
    "join_back": 7,
    "attend_back": 20,
    "project_grads": 11,
    "project_back": 7,
}


def mm(former, latter):
    return jnp.dot(former, latter, preferred_element_type=F32)


def mm_tail(former, latter):
    return lax.dot_general(former, latter, (((1,), (1,)), ((), ())), preferred_element_type=F32)


def mm_lead(former, latter):
    return lax.dot_general(former, latter, (((0,), (0,)), ((), ())), preferred_element_type=F32)


def call(body, name, out_shape, grid, in_specs, out_specs, scratch=(), aliases=None):
    return pl.pallas_call(
        body,
        name=name,
        out_shape=out_shape,
        grid_spec=pltpu.PrefetchScalarGridSpec(
            num_scalar_prefetch=1,
            grid=grid,
            in_specs=in_specs,
            out_specs=out_specs,
            scratch_shapes=list(scratch),
        ),
        input_output_aliases=aliases or {},
        compiler_params=pltpu.CompilerParams(vmem_limit_bytes=VMEM_LIMIT),
        cost_estimate=pl.CostEstimate(
            flops=1, bytes_accessed=int(COST_SCALE * COSTS[name] * 3690000), transcendentals=0
        ),
    )


def shaped(shape, kind):
    return jax.ShapeDtypeStruct(shape, kind)


def whole(shape):
    return pl.BlockSpec(shape, lambda i, s: (0,) * len(shape), pipeline_mode=pl.Buffered(1))


def rows_of(shape):
    return pl.BlockSpec(shape, lambda i, s: (i, 0))


def norm_stats(series):
    center = jnp.mean(series, -1, keepdims=True)
    spread = jnp.mean(series * series, -1, keepdims=True) - center * center
    inverse = lax.rsqrt(spread + EPSILON)
    return (series - center) * inverse, inverse


def norm_back(grad, gain, hat, inverse):
    scaled = grad * gain
    first = jnp.mean(scaled, -1, keepdims=True)
    second = jnp.mean(scaled * hat, -1, keepdims=True)
    return inverse * (scaled - first - hat * second)


def put_blocks(s_ref, pieces, places, target, column, width):
    at = 0
    for piece in pieces:
        depth = piece.shape[1]
        for block in range(piece.shape[0]):
            row = (s_ref[0] ^ places[at]) * depth
            if depth % 16 == 0:
                row = pl.multiple_of(row, 16)
            target[pl.ds(row, depth), pl.ds(column, width)] = piece[block, :, 0:width]
            at += 1


def put_rows(s_ref, mine, other, places, target, column, folds):
    near = s_ref[1] == 0
    own = mine.shape[1] // folds
    width = mine.shape[2]
    for block in range(mine.shape[0]):
        row = pl.multiple_of((s_ref[0] ^ places[block]) * (2 * own), 16)
        one, two = mine[block].astype(F32), other[block].astype(F32)
        upper, lower = jnp.where(near, one, two), jnp.where(near, two, one)
        for at in range(folds):
            rows = slice(at * own, (at + 1) * own)
            target[pl.ds(row, 2 * own), column + at * width : column + (at + 1) * width] = jnp.concatenate(
                [upper[rows], lower[rows]], 0
            ).astype(BF16)


def project(inputs, parts, places, scalars):
    rows, width = inputs.shape
    tile = min(TILE, rows)
    flat = [piece for part in parts for piece in part]
    cuts = [part[0].shape[2] for part in parts]
    columns = sum(cuts)

    def body(s_ref, x_ref, *refs):
        pieces, (q_ref, kv_ref, n_ref, w_ref, g_ref, full) = refs[: len(flat)], refs[len(flat) :]

        @pl.when(pl.program_id(0) == 0)
        def _():
            at = 0
            for k, part in enumerate(parts):
                column = sum(cuts[:k])
                if len(part) == 2:
                    put_rows(s_ref, pieces[at], pieces[at + 1], places[k], full, column, 1)
                else:
                    put_blocks(s_ref, pieces[at : at + 1], places[k], full, column, cuts[k])
                at += len(part)
            w_ref[...] = full[:, 0 : 3 * width]
            g_ref[...] = jnp.transpose(full[:, 3 * width : 3 * width + 128].astype(F32))[0:8]

        hat, _ = norm_stats(x_ref[...].astype(F32))
        low = (hat * g_ref[0:1, :]).astype(BF16)
        n_ref[...] = low
        q_ref[...] = mm(low, full[:, 0:width]).astype(BF16)
        for which in range(2):
            part = mm(low, full[:, (1 + which) * width : (2 + which) * width]).astype(BF16)
            for pair in range(width // PAIR):
                at = (2 * pair + which) * PAIR
                kv_ref[:, at : at + PAIR] = part[:, pair * PAIR : (pair + 1) * PAIR]

    spec = rows_of((tile, width))
    return call(
        body,
        "project",
        (
            shaped((rows, width), BF16),
            shaped((rows, 2 * width), BF16),
            shaped((rows, width), BF16),
            shaped((width, 3 * width), BF16),
            shaped((8, width), F32),
        ),
        (rows // tile,),
        [spec] + [whole(p.shape) for p in flat],
        (spec, rows_of((tile, 2 * width)), spec, whole((width, 3 * width)), whole((8, width))),
        scratch=[pltpu.VMEM((width, columns), BF16)],
    )(scalars, inputs, *flat)


def lane_of(head):
    lanes = lax.broadcasted_iota(jnp.int32, (1, PAIR), 1)
    return (lanes >= head * HEAD_DIM) & (lanes < (head + 1) * HEAD_DIM)


def attend(queries, near, far_side, scalars):
    rows, width = queries.shape
    tile = min(TILE, rows)
    pairs = width // PAIR

    def body(s_ref, q_ref, kv_ref, fkv_ref, o_ref, l_ref):
        offset = s_ref[1] * rows
        length = s_ref[2]

        def run(far):
            query = q_ref[...] * jnp.asarray(0.125, BF16)
            for t in range(rows // tile):
                end = (t + 1) * tile
                place = lax.broadcasted_iota(jnp.int32, (tile, end), 0) + t * tile
                key_at = lax.broadcasted_iota(jnp.int32, (tile, end), 1)
                allowed = (key_at <= place) & (key_at + offset < length)
                sums = []
                logs = []
                for head in range(2):
                    mine = jnp.where(
                        lane_of(head), query[t * tile : end], jnp.zeros((), BF16)
                    )
                    scores = jnp.where(allowed, mm_tail(mine, kv_ref[0:end, 0:PAIR]), MASKED)
                    highest = jnp.max(scores, -1, keepdims=True)
                    if far:
                        beyond = mm_tail(mine, fkv_ref[:, 0:PAIR])
                        highest = jnp.maximum(highest, jnp.max(beyond, -1, keepdims=True))
                        beyond = jnp.exp(beyond - highest)
                    scores = jnp.exp(scores - highest)
                    total = jnp.sum(scores, -1, keepdims=True)
                    mixed = mm(scores.astype(BF16), kv_ref[0:end, PAIR : 2 * PAIR])
                    if far:
                        total = total + jnp.sum(beyond, -1, keepdims=True)
                        mixed = mixed + mm(beyond.astype(BF16), fkv_ref[:, PAIR : 2 * PAIR])
                    sums.append(mixed / total)
                    logs.append(jnp.broadcast_to(highest + jnp.log(total), (tile, PAIR)))
                o_ref[t * tile : end] = jnp.where(lane_of(0), sums[0], sums[1])
                l_ref[t * tile : end] = jnp.where(lane_of(0), logs[0], logs[1])

        @pl.when(s_ref[1] == 0)
        def _():
            run(False)

        @pl.when(s_ref[1] != 0)
        def _():
            run(True)

    spec = pl.BlockSpec((rows, PAIR), lambda i, s: (0, i))
    both = pl.BlockSpec((rows, 2 * PAIR), lambda i, s: (0, i))
    return call(
        body,
        "attend",
        (shaped((rows, width), F32), shaped((rows, width), F32)),
        (pairs,),
        [spec, both, both],
        (spec, spec),
    )(scalars, queries, near, far_side)


def attend_back(queries, near, far_side, grads, attended, logs, scalars, first, pairs):
    rows = queries.shape[0]
    tile = min(TILE, rows)
    width = pairs * PAIR

    def body(
        s_ref, q_ref, kv_ref, fkv_ref, d_ref, o_ref, l_ref,
        dq_ref, dkv_ref, fdkv_ref,
    ):
        offset = s_ref[1] * rows
        length = s_ref[2]

        def run(far):
            query = q_ref[...] * jnp.asarray(0.125, BF16)
            grad = d_ref[...]
            log_rows = jnp.transpose(l_ref[...])
            picker = jnp.where(
                lax.broadcasted_iota(jnp.int32, (8, PAIR), 1) // HEAD_DIM
                == lax.broadcasted_iota(jnp.int32, (8, PAIR), 0),
                1.0,
                0.0,
            ).astype(F32)
            dots = lax.dot_general(
                picker,
                grad.astype(F32) * o_ref[...],
                (((1,), (1,)), ((), ())),
                precision=lax.Precision.HIGHEST,
                preferred_element_type=F32,
            )
            blocks = [
                (kv_ref, dkv_ref, t * tile, t * tile, True)
                for t in range(rows // tile)
            ]
            if far:
                blocks += [
                    (fkv_ref, fdkv_ref, t * tile, 0, False)
                    for t in range(rows // tile)
                ]
            turned = [[jnp.zeros((HEAD_DIM, tile), F32) for _ in range(rows // tile)] for _ in range(2)]
            for pair_ref, dpair_ref, at, low, masked in blocks:
                key = pair_ref[at : at + tile, 0:PAIR]
                value = pair_ref[at : at + tile, PAIR : 2 * PAIR]
                key_turned = jnp.transpose(key)
                count = rows - low
                kgrads, vgrads = [], []
                if masked:
                    key_at = lax.broadcasted_iota(jnp.int32, (tile, count), 0) + at
                    place = lax.broadcasted_iota(jnp.int32, (tile, count), 1) + low
                    allowed = (key_at <= place) & (key_at + offset < length)
                for head in range(2):
                    lanes = lane_of(head)
                    mine = jnp.where(lanes, query[low:rows], jnp.zeros((), BF16))
                    mine_grad = jnp.where(lanes, grad[low:rows], jnp.zeros((), BF16))
                    scores = mm_tail(key, mine)
                    if masked:
                        scores = jnp.where(allowed, scores, MASKED)
                    base = head * HEAD_DIM
                    probs = jnp.exp(scores - log_rows[base : base + 1, low:rows])
                    prob_grad = mm_tail(value, mine_grad)
                    score_grad = (probs * (prob_grad - dots[head : head + 1, low:rows])).astype(BF16)
                    vgrads.append(mm(probs.astype(BF16), grad[low:rows]))
                    kgrads.append(mm(score_grad, query[low:rows]))
                    part = mm(key_turned[base : base + HEAD_DIM], score_grad)
                    for t in range(low // tile, rows // tile):
                        turned[head][t] = turned[head][t] + part[:, t * tile - low : (t + 1) * tile - low]
                dpair_ref[at : at + tile, 0:PAIR] = jnp.where(lane_of(0), kgrads[0], kgrads[1]).astype(dpair_ref.dtype)
                dpair_ref[at : at + tile, PAIR : 2 * PAIR] = jnp.where(lane_of(0), vgrads[0], vgrads[1]).astype(dpair_ref.dtype)
            for t in range(rows // tile):
                both = jnp.concatenate([turned[0][t], turned[1][t]], 0)
                dq_ref[t * tile : (t + 1) * tile] = (jnp.transpose(both) * 0.125).astype(BF16)

        @pl.when(s_ref[1] == 0)
        def _():
            run(False)
            fdkv_ref[...] = jnp.zeros_like(fdkv_ref)

        @pl.when(s_ref[1] != 0)
        def _():
            run(True)

    spec = pl.BlockSpec((rows, PAIR), lambda i, s: (0, i + first))
    both = pl.BlockSpec((rows, 2 * PAIR), lambda i, s: (0, i + first))
    own = pl.BlockSpec((rows, PAIR), lambda i, s: (0, i))
    own_both = pl.BlockSpec((rows, 2 * PAIR), lambda i, s: (0, i))
    return call(
        body,
        "attend_back",
        (shaped((rows, width), BF16), shaped((rows, 2 * width), F32), shaped((rows, 2 * width), BF16)),
        (pairs,),
        [spec, both, both, spec, spec, spec],
        (own, own_both, own_both),
    )(scalars, queries, near, far_side, grads, attended, logs)


def join(attended, inputs, parts, places, gains, scalars):
    rows, width = attended.shape
    tile = min(TILE, rows)
    flat = parts

    def body(s_ref, a_ref, x_ref, g_ref, *refs):
        pieces, (sub_ref, mid_ref, ffn_ref, w_ref) = refs[: len(flat)], refs[len(flat) :]

        @pl.when(pl.program_id(0) == 0)
        def _():
            if len(parts) == 2:
                put_rows(s_ref, pieces[0], pieces[1], places, w_ref, 0, width // pieces[0].shape[2])
            else:
                put_blocks(s_ref, pieces, places, w_ref, 0, width)

        hat, _ = norm_stats(a_ref[...])
        low = (hat * g_ref[1:2, :]).astype(BF16)
        sub_ref[...] = low
        middle = x_ref[...].astype(F32) + mm(low, w_ref[...])
        mid_ref[...] = middle
        hat, _ = norm_stats(middle)
        ffn_ref[...] = (hat * g_ref[2:3, :]).astype(BF16)

    spec = rows_of((tile, width))
    return call(
        body,
        "join",
        (
            shaped((rows, width), BF16),
            shaped((rows, width), F32),
            shaped((rows, width), BF16),
            shaped((width, width), BF16),
        ),
        (rows // tile,),
        [spec, spec, whole((8, width))] + [whole(p.shape) for p in flat],
        (spec,) * 3 + (whole((width, width)),),
    )(scalars, attended, inputs, gains, *flat)


def join_back(branch, far_branch, fgrad, far_fgrad, middle, cotangent, attended, weights, gains, scalars):
    rows, width = middle.shape
    tile = min(TILE, rows)
    steps = rows // tile

    def body(
        s_ref, b_ref, fb_ref, f_ref, ff_ref, m_ref, c_ref, a_ref, w_ref, g_ref,
        out_ref, mg_ref, ml_ref, ag_ref,
    ):
        step = pl.program_id(0)
        places = lax.broadcasted_iota(jnp.int32, (tile, 1), 0) + (step * tile + s_ref[1] * rows)
        kept = (places < s_ref[2]).astype(F32)
        middle = m_ref[...]
        branch = b_ref[...].astype(F32) + fb_ref[...].astype(F32)
        out_ref[...] = (kept * (middle + branch)).astype(BF16)
        hat, inverse = norm_stats(middle)
        grad = f_ref[...].astype(F32) + ff_ref[...].astype(F32)
        middle_grad = c_ref[...].astype(F32) * kept + norm_back(grad, g_ref[2:3, :], hat, inverse)
        mg_ref[...] = middle_grad
        low = middle_grad.astype(BF16)
        ml_ref[...] = low
        sub_grad = mm_tail(low, w_ref[...])
        hat, inverse = norm_stats(a_ref[...])
        ag_ref[...] = norm_back(sub_grad, g_ref[1:2, :], hat, inverse).astype(BF16)

    spec = rows_of((tile, width))
    return call(
        body,
        "join_back",
        (
            shaped((rows, width), BF16),
            shaped((rows, width), F32),
            shaped((rows, width), BF16),
            shaped((rows, width), BF16),
        ),
        (steps,),
        [spec] * 7 + [whole((width, width)), whole((8, width))],
        (spec,) * 4,
    )(scalars, branch, far_branch, fgrad, far_fgrad, middle, cotangent, attended, weights, gains)


def two_sided(tile, width, steps):
    near = pl.BlockSpec((tile, width), lambda i, s: (jnp.minimum(i, steps - 1), 0))
    far = pl.BlockSpec((tile, width), lambda i, s: (jnp.maximum(i - steps, 0), 0))
    return near, far


def stat_rows(first, second):
    lanes = lax.broadcasted_iota(jnp.int32, (first.shape[0], 128), 1)
    return jnp.transpose(jnp.where(lanes == 0, first, jnp.where(lanes == 1, second, 0.0)))[0:8]


def stat_columns(mine, other):
    both = jnp.transpose(mine + other)
    return both[:, 0:1], both[:, 1:2]


def unit_norm(mine, other, total):
    sums, squares = stat_columns(mine, other)
    center = sums / total
    return center, lax.rsqrt(squares / total - center * center + EPSILON)


def fold(value):
    out = value[:, 0:128]
    for at in range(128, value.shape[1], 128):
        out = out + value[:, at : at + 128]
    return out


def to_side(near, near_ref, far_ref, value):
    low = value.astype(BF16)

    @pl.when(near)
    def _():
        near_ref[...] = low

    @pl.when(jnp.logical_not(near))
    def _():
        far_ref[...] = low


def stats_of(tile):
    return pl.BlockSpec((8, tile), lambda i, s: (0, i))


def other_stats(tile, steps):
    return pl.BlockSpec((8, tile), lambda i, s: (0, lax.rem(i + steps, 2 * steps)))


def ffn_in(near, far, parts, places, units, scalars):
    rows, width = near.shape
    pieces = [piece for part in parts for piece in part]
    cuts = [part[0].shape[2] for part in parts]
    cuts[-1] = units - sum(cuts[:-1])
    tile = min(TILE, rows)
    steps = rows // tile
    chunk = 256

    def body(s_ref, n_ref, f_ref, *refs):
        blocks, (act_ref, slope_ref, stat_ref, w_ref) = refs[: len(pieces)], refs[len(pieces) :]

        @pl.when(pl.program_id(0) == 0)
        def _():
            at = 0
            for k, part in enumerate(parts):
                put_blocks(s_ref, blocks[at : at + len(part)], places[k], w_ref, sum(cuts[:k]), cuts[k])
                at += len(part)

        low = jnp.where(pl.program_id(0) < steps, n_ref[...], f_ref[...])
        sums = jnp.zeros((tile, 128), F32)
        squares = jnp.zeros((tile, 128), F32)
        for at in range(0, units, chunk):
            pre = mm(low, w_ref[:, at : at + chunk])
            cdf = 0.5 * (1.0 + lax.erf(pre * 0.7071067811865476))
            pdf = 0.3989422804014327 * jnp.exp(-0.5 * pre * pre)
            act = pre * cdf
            act_ref[:, at : at + chunk] = act
            slope_ref[:, at : at + chunk] = (cdf + pre * pdf).astype(slope_ref.dtype)
            sums = sums + fold(act)
            squares = squares + fold(act * act)
        stat_ref[...] = stat_rows(
            jnp.sum(sums, -1, keepdims=True), jnp.sum(squares, -1, keepdims=True)
        )

    near_spec, far_spec = two_sided(tile, width, steps)
    return call(
        body,
        "ffn_in",
        (
            shaped((2 * rows, units), F32),
            shaped((2 * rows, units), BF16),
            shaped((8, 2 * rows), F32),
            shaped((width, units), BF16),
        ),
        (2 * steps,),
        [near_spec, far_spec] + [whole(p.shape) for p in pieces],
        (rows_of((tile, units)), rows_of((tile, units)), stats_of(tile), whole((width, units))),
    )(scalars, near, far, *pieces)


def ffn_out(act, stats, far_stats, gain, near_grad, far_grad, weights, scalars, order):
    rows, width = near_grad.shape
    units = act.shape[1]
    tile = min(TILE, rows)
    steps = rows // tile
    depth = width // len(order)
    chunk = 256

    def body(s_ref, a_ref, st_ref, fs_ref, g_ref, n_ref, f_ref, w_ref, b_ref, fb_ref, stat_ref, out_ref, stash, tilt):
        step = pl.program_id(0)
        weight = w_ref.at[0]

        @pl.when(step == 0)
        def _():
            tilt[...] = mm_tail(jnp.broadcast_to(g_ref[...], (8, units)).astype(BF16), weight[...])

        center, inverse = unit_norm(st_ref[...], fs_ref[...], 2 * units)
        at_row = pl.multiple_of(step * tile, tile)
        for at in range(0, units, chunk):
            hat = (a_ref[:, at : at + chunk] - center) * inverse
            stash[pl.ds(at_row, tile), at : at + chunk] = (hat * g_ref[:, at : at + chunk]).astype(BF16)
        branch = mm_tail(stash[pl.ds(at_row, tile), :], weight[...])
        to_side(step < steps, b_ref, fb_ref, branch)
        inside = pl.multiple_of(lax.rem(step, steps) * tile, tile)
        grad = jnp.where(step < steps, n_ref[pl.ds(inside, tile)], f_ref[pl.ds(inside, tile)]).astype(F32)
        stat_ref[...] = stat_rows(
            jnp.sum(fold(grad * tilt[0:1, :]), -1, keepdims=True),
            jnp.sum(fold(grad * branch), -1, keepdims=True),
        )

        @pl.when(step == 2 * steps - 1)
        def _():
            near_turned, far_turned = jnp.transpose(n_ref[...]), jnp.transpose(f_ref[...])
            for at in range(0, units, 512):
                part = mm(near_turned, stash[0:rows, at : at + 512]) + mm(far_turned, stash[rows:, at : at + 512])
                for to, block in enumerate(order):
                    out_ref[to * depth : (to + 1) * depth, at : at + 512] = part[
                        block * depth : (block + 1) * depth
                    ].astype(BF16)

    return call(
        body,
        "ffn_out",
        (
            shaped((rows, width), BF16),
            shaped((rows, width), BF16),
            shaped((8, 2 * rows), F32),
            shaped((width, units), BF16),
        ),
        (2 * steps,),
        [
            rows_of((tile, units)),
            stats_of(tile),
            other_stats(tile, steps),
            whole((1, units)),
            whole((rows, width)),
            whole((rows, width)),
            whole((1, width, units)),
        ],
        two_sided(tile, width, steps) + (stats_of(tile), whole((width, units))),
        scratch=[pltpu.VMEM((2 * rows, units), BF16), pltpu.VMEM((8, width), F32)],
    )(scalars, act, stats, far_stats, gain, near_grad, far_grad, weights)


def ffn_back(
    act, slope, stats, far_stats, grads, far_grads, gain, near_grad, far_grad, near, far, out_weights, in_weights, scalars, blocks
):
    rows, width = near.shape
    units = act.shape[1]
    tile = min(TILE, rows)
    steps = rows // tile
    depth = width // blocks
    chunk = 256
    piece = units // 4

    def body(
        s_ref, a_ref, sl_ref, st_ref, fs_ref, gt_ref, fg_ref, g_ref, ng_ref, fgr_ref, n_ref, f_ref, wo_ref, wi_ref,
        b_ref, fb_ref, four_ref, *rest,
    ):
        outs, (stash, fourth, total) = rest[:-3], rest[-3:]
        step = pl.program_id(0)
        center, inverse = unit_norm(st_ref[...], fs_ref[...], 2 * units)
        first, second = stat_columns(gt_ref[...], fg_ref[...])
        first, second = first / (2 * units), second / (2 * units)
        at_row = pl.multiple_of(step * tile, tile)
        inside = pl.multiple_of(lax.rem(step, steps) * tile, tile)
        grad = jnp.where(step < steps, ng_ref[pl.ds(inside, tile)], fgr_ref[pl.ds(inside, tile)])

        @pl.when(step == 0)
        def _():
            fourth[...] = jnp.zeros_like(fourth)

        for at in range(0, units, chunk):
            normed = mm(grad, wo_ref[0, :, at : at + chunk])
            hat = (a_ref[:, at : at + chunk] - center) * inverse
            fourth[:, at : at + chunk] += jnp.sum((normed * hat).reshape(tile // 8, 8, chunk), 0)
            act_grad = inverse * (normed * g_ref[:, at : at + chunk] - first - hat * second)
            stash[pl.ds(at_row, tile), at : at + chunk] = (
                act_grad * sl_ref[:, at : at + chunk].astype(F32)
            ).astype(BF16)
        to_side(step < steps, b_ref, fb_ref, mm_tail(stash[pl.ds(at_row, tile), :], wi_ref[...]))

        @pl.when(step == 2 * steps - 1)
        def _():
            value = jnp.sum(fourth[...], 0, keepdims=True)
            four_ref[...] = jnp.broadcast_to(value, four_ref.shape)
            near_turned, far_turned = jnp.transpose(n_ref[...]), jnp.transpose(f_ref[...])
            for at in range(0, units, piece):
                part = mm(near_turned, stash[0:rows, at : at + piece]) + mm(far_turned, stash[rows:, at : at + piece])
                if blocks == 1:
                    outs[0][:, at : at + piece] = part.astype(BF16)
                else:
                    total[...] = part
                    order = 0 if at < units // 2 else 1
                    inside = at - order * (units // 2)
                    for block in range(blocks):
                        slot = slot_of(block ^ s_ref[0], order, blocks)
                        low = total[block * depth : (block + 1) * depth].astype(BF16)

                        @pl.when(slot < blocks // 2)
                        def _():
                            outs[0][pl.ds(pl.multiple_of(slot * depth, 16), depth), at : at + piece] = low

                        @pl.when(slot >= blocks // 2)
                        def _():
                            row = pl.multiple_of((slot - blocks // 2) * depth, 16)
                            outs[1 + order][pl.ds(row, depth), inside : inside + piece] = low
            if blocks > 1:
                high = value.astype(BF16)
                rest_of = (value - high.astype(F32)).astype(BF16)
                at_line = lax.broadcasted_iota(jnp.int32, (EXTRA, units), 0)
                extra = jnp.where(at_line == 0, high.astype(F32), jnp.where(at_line == 1, rest_of.astype(F32), 0.0))
                extra = extra.astype(BF16)
                outs[1][width // 2 : width // 2 + EXTRA] = extra[:, : units // 2]
                outs[2][width // 2 : width // 2 + EXTRA] = extra[:, units // 2 :]

    wide = rows_of((tile, units))
    crossing = (width // 2 + EXTRA, units // 2)
    shapes = ((width, units),) if blocks == 1 else ((width // 2, units), crossing, crossing)
    return call(
        body,
        "ffn_back",
        (shaped((rows, width), BF16), shaped((rows, width), BF16), shaped((8, units), F32))
        + tuple(shaped(shape, BF16) for shape in shapes),
        (2 * steps,),
        [
            wide, wide, stats_of(tile), other_stats(tile, steps), stats_of(tile), other_stats(tile, steps),
            whole((1, units)),
        ]
        + [whole((rows, width))] * 4
        + [whole((1, width, units)), whole((width, units))],
        two_sided(tile, width, steps) + (whole((8, units)),) + tuple(whole(shape) for shape in shapes),
        scratch=[
            pltpu.VMEM((2 * rows, units), BF16),
            pltpu.VMEM((8, units), F32),
            pltpu.VMEM((width, piece), F32),
        ],
    )(
        scalars, act, slope, stats, far_stats, grads, far_grads, gain, near_grad, far_grad, near, far, out_weights,
        in_weights,
    )


def slot_of(position, order, blocks):
    if blocks < 4:
        return position
    low = (position >> order) & 1
    high = (position >> (1 - order)) & 1
    return low * (blocks // 2) + high * (blocks // 4) + (position >> 2)


def project_grads(normed, dq, dkv, far_dkv, extra, parts, scalars, blocks):
    rows, width = normed.shape
    cols = dq.shape[1]
    depth = width // blocks
    own = depth // 2
    total = 3 * cols + (width if extra else 0)
    pairs = cols // PAIR
    shape = (blocks, own, total) if blocks > 1 else (1, width, total)

    def body(s_ref, n_ref, q_ref, kv_ref, fkv_ref, *refs):
        if extra:
            left_ref, right_ref = refs[:2]
            refs = refs[2:]
        low_ref, *outs, grad_ref = refs
        me, core = s_ref[0], s_ref[1]
        near = core == 0
        both = kv_ref[...] + jnp.where(near, fkv_ref[...].astype(F32), 0.0)
        low_ref[:, 0:cols] = q_ref[...]
        for pair in range(pairs):
            for which in range(2):
                to = (1 + which) * cols + pair * PAIR
                at = (2 * pair + which) * PAIR
                low_ref[:, to : to + PAIR] = both[:, at : at + PAIR].astype(BF16)
        turned = jnp.transpose(n_ref[...])
        grad_ref[:, 0 : 3 * cols] = mm(turned, low_ref[...])
        if extra:
            grad_ref[:, 3 * cols : total] = mm_lead(left_ref[...], right_ref[...])
        if blocks == 1:
            outs[0][0] = grad_ref[...].astype(BF16)
            return
        for side, out in ((0, outs[0]), (1, outs[1])):
            owner = core if side == 0 else 1 - core
            for block in range(blocks):
                position = block ^ me
                row = pl.multiple_of(block * depth + owner * own, 8)
                for order, start, end in parts:
                    slot = slot_of(position, order, blocks)
                    out[slot, :, start:end] = grad_ref[pl.ds(row, own), start:end].astype(BF16)

    more = list(extra) if extra else []
    pieces = 1 if blocks == 1 else 2
    return call(
        body,
        "project_grads",
        (shaped((rows, 3 * cols), BF16),) + (shaped(shape, BF16),) * pieces,
        (1,),
        [whole((rows, width)), whole((rows, cols)), whole((rows, 2 * cols)), whole((rows, 2 * cols))]
        + [whole((rows, width))] * len(more),
        (whole((rows, 3 * cols)),) + (whole(shape),) * pieces,
        scratch=[pltpu.VMEM((width, total), F32)],
    )(scalars, normed, dq, dkv, far_dkv, *more)


def project_back(lows, inputs, middle_grad, weights, gains, scalars):
    rows, width = inputs.shape
    tile = min(TILE, rows)
    sizes = [low.shape[1] // 3 for low in lows]

    def body(s_ref, *refs):
        low_refs, (x_ref, m_ref, w_ref, g_ref, out_ref) = refs[: len(lows)], refs[len(lows) :]
        hat, inverse = norm_stats(x_ref[...].astype(F32))
        grad = jnp.zeros((tile, width), F32)
        at = 0
        for low_ref, size in zip(low_refs, sizes):
            for which in range(3):
                base = which * width + at
                grad = grad + mm_tail(
                    low_ref[:, which * size : (which + 1) * size], w_ref[:, base : base + size]
                )
            at += size
        out_ref[...] = (m_ref[...] + norm_back(grad, g_ref[0:1, :], hat, inverse)).astype(BF16)

    spec = rows_of((tile, width))
    return call(
        body,
        "project_back",
        shaped((rows, width), BF16),
        (rows // tile,),
        [rows_of((tile, 3 * size)) for size in sizes]
        + [spec, spec, whole((width, 3 * width)), whole((8, width))],
        spec,
    )(scalars, *lows, inputs, middle_grad, weights, gains)


CHIPS = ("outer", "inner")
CORES = "tensor"


def other_core(array):
    return lax.ppermute(array, CORES, [(0, 1), (1, 0)])


def exchange(array, mask, chips):
    return lax.ppermute(array, CHIPS, [(i, i ^ mask) for i in range(chips)])


def bit_count(chips):
    return chips.bit_length() - 1


def by_core(mine, other, axis):
    core = lax.axis_index(CORES)
    return jnp.where(
        core == 0,
        jnp.concatenate([mine, other], axis),
        jnp.concatenate([other, mine], axis),
    )


def after(value, *others):
    return lax.optimization_barrier((value,) + others)[0]


def gather_outer(shard, chips):
    places = list(range(0, chips, 4))
    return jnp.stack([shard] + [exchange(shard, mask, chips) for mask in places[1:]], 0), places


def widen(pieces, places, mask, chips):
    held = pieces[0] if len(pieces) == 1 else jnp.concatenate(pieces, 0)
    return pieces + [exchange(held, mask, chips)], places + [p | mask for p in places]


def on_device(
    inputs,
    cotangent,
    lengths,
    query_key,
    value_proj,
    output_proj,
    hidden_in,
    hidden_out,
    first_gain,
    second_gain,
    third_gain,
    fourth_gain,
):
    rows, width = inputs.shape[1:]
    chips = lax.axis_size(CHIPS)
    inner = lax.axis_size("inner")
    chip = lax.axis_index(CHIPS)
    core = lax.axis_index(CORES)
    barrier = lax.optimization_barrier
    depth = width // chips
    pairwise = chips & (chips - 1) == 0 and chips >= 4 and depth % 16 == 0
    series = inputs[0]
    scalars = jnp.stack([chip if pairwise else jnp.zeros_like(chip), core, lengths[0]]).astype(jnp.int32)
    scalars = jnp.concatenate([scalars, jnp.zeros((5,), jnp.int32)])

    gain_columns = jnp.stack([first_gain, second_gain, third_gain], 1)
    gain_columns = jnp.pad(gain_columns, ((0, 0), (0, 256 - 3)))
    shard = jnp.concatenate([query_key, value_proj, gain_columns], 1)
    half = shard.shape[1]
    units = hidden_in.shape[1]
    if pairwise:
        stack, places = gather_outer(shard, chips)
        cut = -(-half // 256) * 128
        o_folded = jnp.concatenate([output_proj[:, : width // 2], output_proj[:, width // 2 :]], 0)
        late_shard = jnp.concatenate([hidden_in, o_folded], 1)
        late_out = hidden_out.T
        stack, late_shard = barrier((stack, late_shard))
        out_weights_ff = lax.all_gather(late_out, CHIPS, axis=0, tiled=True)[None]
        first, first_places = widen([stack[:, :, :cut]], places, 2, chips)
        second, second_places = widen([stack[:, :, cut:]], places, 1, chips)
        late, late_places = gather_outer(late_shard, chips)
        first[-1], second[-1] = barrier((first[-1], second[-1]))
        first, first_places = widen(first, first_places, 1, chips)
        second, second_places = widen(second, second_places, 2, chips)
        first[-1], second[-1], late = barrier((first[-1], second[-1], late))
        late_cut = -(-late.shape[2] // 256) * 128
        in_first, in_first_places = widen([late[:, :, :late_cut]], late_places, 1, chips)
        in_second, in_second_places = widen([late[:, :, late_cut:]], late_places, 2, chips)
        mine = [jnp.concatenate(first, 0), jnp.concatenate(second, 0)]
        parts = [[p, other_core(p)] for p in mine]
        part_places = [first_places, second_places]
    else:
        gathered = lax.all_gather(shard, CHIPS + (CORES,), axis=0, tiled=True)
        parts, part_places = [[gathered[None]]], [[0]]
        in_parts = [[lax.all_gather(hidden_in, CHIPS, axis=0, tiled=True)[None]]]
        in_part_places = [[0]]
        out_weights = lax.all_gather(output_proj, CHIPS + (CORES,), axis=0, tiled=True)
        out_weights_ff = lax.all_gather(hidden_out.T, CHIPS, axis=0, tiled=True)[None]

    kept = (core * rows + jnp.arange(rows) < lengths[0])[:, None]
    near_grad = jnp.where(kept, cotangent[0], jnp.zeros((), BF16))
    far_grad = other_core(near_grad)

    if pairwise:
        series, in_first[0], in_second[0] = barrier((series, in_first[0], in_second[0]))
    queries, near_kv, normed, weights, gains = project(series, parts, part_places, scalars)
    if pairwise:
        near_kv, in_first[-1], in_second[-1] = barrier((near_kv, in_first[-1], in_second[-1]))
    far_kv = lax.ppermute(near_kv, CORES, [(0, 1)])
    if pairwise:
        in_first, in_first_places = widen(in_first, in_first_places, 2, chips)
        in_second, in_second_places = widen(in_second, in_second_places, 1, chips)
    attended, logs = attend(queries, near_kv, far_kv, scalars)
    if pairwise:
        attended, in_first[-1], in_second[-1] = barrier((attended, in_first[-1], in_second[-1]))
        in_parts = [in_first, in_second]
        in_part_places = [in_first_places, in_second_places]
        extra_columns = units - late_cut
        o_mine = jnp.concatenate(in_second, 0)[:, :, extra_columns:]
        out_parts = [o_mine, other_core(o_mine)]
        sub_low, middle, near, out_weights = join(attended, series, out_parts, in_second_places, gains, scalars)
    else:
        sub_low, middle, near, out_weights = join(attended, series, [out_weights[None]], [0], gains, scalars)
    far = other_core(near)

    if pairwise:
        far, out_weights_ff = barrier((far, out_weights_ff))
    act, slope, stats, in_weights = ffn_in(near, far, in_parts, in_part_places, units, scalars)
    far_stats = other_core(stats)
    outer = chips // inner
    order = list(range(chips))
    if pairwise:
        order = [o * inner + i for i in range(inner) for o in range(outer)]
    gain_four = fourth_gain.astype(F32)[None, :]
    branch, branch_sent, grad_stats, out_payload = ffn_out(
        act, stats, far_stats, gain_four, near_grad, far_grad, out_weights_ff, scalars, order
    )
    if pairwise:
        out_payload = lax.psum_scatter(out_payload, "inner", scatter_dimension=0, tiled=True)
    else:
        out_payload = lax.psum_scatter(out_payload, CHIPS, scatter_dimension=0, tiled=True)
    far_grad_stats = other_core(grad_stats)
    far_branch = other_core(branch_sent)
    blocks = chips if pairwise else 1
    ffn_grad, ffn_grad_sent, fourth_term, *in_payload = ffn_back(
        act, slope, stats, far_stats, grad_stats, far_grad_stats, gain_four, near_grad, far_grad, near, far,
        out_weights_ff, in_weights, scalars, blocks,
    )
    far_ffn_grad = other_core(ffn_grad_sent)
    if pairwise:
        got = [exchange(in_payload[1], 1, chips), exchange(in_payload[2], 2, chips)]
    outputs, middle_grad, middle_low, attended_low = join_back(
        branch, far_branch, ffn_grad, far_ffn_grad, middle, near_grad, attended, out_weights, gains, scalars
    )

    pairs = width // PAIR
    extra = (sub_low, middle_low)
    if pairwise:
        columns = 4 * width
        cut = columns // 2
        middle, lower = chips // 2, chips // 4
        count = width // 2
        dq, dkv, far_dkv = attend_back(queries, near_kv, far_kv, attended_low, attended, logs, scalars, 0, pairs)
        got[0], got[1], out_payload, far_dkv = barrier((got[0], got[1], out_payload, far_dkv))
        far_dkv = lax.ppermute(far_dkv, CORES, [(1, 0)])
        out_payload = lax.psum_scatter(out_payload, "outer", scatter_dimension=0, tiled=True)
        in_kept, fourth = add_parts(in_payload[0][: count // 2], fourth_term[0:1], got, 0, count)
        in_sent, _ = add_parts(in_payload[0][count // 2 :], fourth_term[0:1], got, count // 2, count)
        rows_low = low_rows(fourth)
        sent = [
            jnp.concatenate([in_sent[:, : units // 2], rows_low[:, : units // 2]], 0),
            jnp.concatenate([in_sent[:, units // 2 :], rows_low[:, units // 2 :]], 0),
        ]
        far_dkv, sent[0], sent[1], in_kept = barrier((far_dkv, sent[0], sent[1], in_kept))
        got = [exchange(sent[0], 2, chips), exchange(sent[1], 1, chips)]
        low, keep, send = project_grads(
            normed, dq, dkv, far_dkv, extra, ((0, 0, cut), (1, cut, columns)), scalars, chips
        )
        middle_grad, keep, send = barrier((middle_grad, keep, send))
        other = other_core(send)
        inputs_grad = project_back([low], series, middle_grad, weights, gains, scalars)
        inputs_grad, other, got[0], got[1] = barrier((inputs_grad, other, got[0], got[1]))
        upper_one = add_low(keep[middle:, :, :cut], other[middle:, :, :cut])
        upper_two = add_low(keep[middle:, :, cut:], other[middle:, :, cut:])
        upper_one, upper_two = barrier((upper_one, upper_two))
        got_one, got_two = exchange(upper_one, 1, chips), exchange(upper_two, 2, chips)
        in_held, fourth = add_parts(in_kept, fourth, got, 0, count // 2)
        in_held = in_held.reshape(chips // 4, depth, units)
        sends = barrier(tuple(outer_sends(in_held, fourth)))
        got_one, got_two, *sends = barrier((got_one, got_two, *sends))
        in_got = exchange_outer(sends, chips)
        sent_first = sum_low(keep[lower:middle, :, :cut], other[lower:middle, :, :cut], got_one[lower:])
        sent_second = sum_low(keep[lower:middle, :, cut:], other[lower:middle, :, cut:], got_two[lower:])
        sent_first, sent_second = barrier((sent_first, sent_second))
        got_first, got_second = exchange(sent_first, 2, chips), exchange(sent_second, 1, chips)
        kept = sum_low(keep[:lower], other[:lower], jnp.concatenate([got_one[:lower], got_two[:lower]], -1))
        got_first, got_second, kept, out_payload = barrier((got_first, got_second, kept, out_payload))
        both = add_low(kept, jnp.concatenate([got_first, got_second], -1))
        both_sends = barrier(tuple(outer_sends(both, None)))
        both_got = exchange_outer(both_sends, chips)
        both_got[0], *in_got = barrier((both_got[0], *in_got))
        in_payload = in_held[0].astype(F32)
        for piece in in_got:
            in_payload = in_payload + piece[:depth].astype(F32)
            fourth = add_rows(fourth, piece[depth:])
        third_part = jnp.sum(hidden_in.astype(F32) * in_payload, 1, keepdims=True)
        third_part = jnp.broadcast_to(third_part, (depth, 128))
        third_part = third_part + other_core(third_part)
        *both_got, third_part = barrier((*both_got, third_part))
        total = both[0].astype(F32)
        for piece in both_got:
            total = total + piece.astype(F32)
        large = total
    else:
        dq, dkv, far_dkv = attend_back(queries, near_kv, far_kv, attended_low, attended, logs, scalars, 0, pairs)
        far_dkv = lax.ppermute(far_dkv, CORES, [(1, 0)])
        low, mine = project_grads(normed, dq, dkv, far_dkv, extra, None, scalars, 1)
        mine = lax.psum_scatter(mine[0], CHIPS, scatter_dimension=0, tiled=True).astype(F32)
        mine = lax.psum(mine, CORES)
        inputs_grad = project_back([low], series, middle_grad, weights, gains, scalars)
        in_payload = lax.psum_scatter(in_payload[0], CHIPS, scatter_dimension=0, tiled=True).astype(F32)
        fourth = lax.psum(fourth_term[0:1], CHIPS)
        large = lax.dynamic_slice_in_dim(mine, core * (depth // 2), depth // 2, 0)
        third_part = lax.psum(jnp.sum(hidden_in.astype(F32) * in_payload, 1, keepdims=True), CORES)
    hidden_out_sum = out_payload.astype(F32).T
    hidden_in_sum = in_payload
    third_sum = lax.dynamic_slice_in_dim(third_part[:, 0], core * (depth // 2), depth // 2) / third_gain.astype(F32)
    qk_sum, value_sum, output_sum = large[:, : 2 * width], large[:, 2 * width : 3 * width], large[:, 3 * width :]
    first_sum = (
        jnp.sum(query_key.astype(F32) * qk_sum, 1) + jnp.sum(value_proj.astype(F32) * value_sum, 1)
    ) / first_gain.astype(F32)
    second_sum = jnp.sum(output_proj.astype(F32) * output_sum, 1) / second_gain.astype(F32)
    return (
        outputs[None],
        inputs_grad[None],
        qk_sum,
        value_sum,
        output_sum,
        hidden_in_sum,
        hidden_out_sum,
        first_sum,
        second_sum,
        third_sum,
        fourth[0],
    )


def add_low(kept, got):
    return (kept.astype(F32) + got.astype(F32)).astype(BF16)


def add_rows(value, rows):
    return value + (rows[0:1].astype(F32) + rows[1:2].astype(F32))


def low_rows(vector):
    high = lax.reduce_precision(vector, 8, 7)
    rest = lax.reduce_precision(vector - high, 8, 7)
    return jnp.concatenate([high, rest, jnp.zeros((EXTRA - 2, vector.shape[1]), F32)], 0).astype(BF16)


def outer_sends(held, vector):
    rows = [] if vector is None else [low_rows(vector)]
    return [jnp.concatenate([held[at]] + rows, 0) if rows else held[at] for at in range(1, held.shape[0])]


def exchange_outer(sends, chips):
    return [exchange(send, 4 * (at + 1), chips) for at, send in enumerate(sends)]


def add_parts(kept, vector, got, start, count):
    part = jnp.concatenate([piece[start : start + kept.shape[0]] for piece in got], 1)
    rows = jnp.concatenate([piece[count:] for piece in got], 1)
    return add_low(kept, part), add_rows(vector, rows)


def sum_low(*arrays):
    total = arrays[0].astype(F32)
    for array in arrays[1:]:
        total = total + array.astype(F32)
    return total.astype(BF16)


def solution(mesh):
    chips, cores = mesh.devices.shape
    inner = 4 if chips % 4 == 0 else 1
    split = Mesh(mesh.devices.reshape(chips // inner, inner, cores), CHIPS + (CORES,))
    every = CHIPS + (CORES,)
    return jax.shard_map(
        on_device,
        mesh=split,
        in_specs=(
            P(CHIPS, CORES, None),
            P(CHIPS, CORES, None),
            P(CHIPS),
            P(every, None),
            P(every, None),
            P(every, None),
            P(CHIPS, CORES),
            P(CORES, CHIPS),
            P(every),
            P(every),
            P(every),
            P(CORES),
        ),
        out_specs=(
            P(CHIPS, CORES, None),
            P(CHIPS, CORES, None),
            P(every, None),
            P(every, None),
            P(every, None),
            P(CHIPS, CORES),
            P(CORES, CHIPS),
            P(every),
            P(every),
            P(every),
            P(CORES),
        ),
        check_vma=False,
    )
```

```python
import jax
import jax.numpy as jnp
from jax import lax
from jax.experimental import pallas as pl
from jax.experimental.pallas import tpu as pltpu
from jax.sharding import Mesh
from jax.sharding import PartitionSpec as P

HEAD_DIM = 64
PAIR = 2 * HEAD_DIM
EPSILON = 1e-05
MASKED = -1000000000.0
F32 = jnp.float32
BF16 = jnp.bfloat16
VMEM_LIMIT = 60 * 1024 * 1024
TILE = 256
EXTRA = 16
COST_SCALE = 0.05
COSTS = {
    "project": 8,
    "attend": 15,
    "join": 5,
    "ffn_in": 10,
    "ffn_out": 10,
    "ffn_back": 14,
    "join_back": 7,
    "attend_back": 20,
    "project_grads": 11,
    "project_back": 7,
    "finish": 2,
}


def mm(former, latter):
    return jnp.dot(former, latter, preferred_element_type=F32)


def mm_tail(former, latter):
    return lax.dot_general(former, latter, (((1,), (1,)), ((), ())), preferred_element_type=F32)


def mm_lead(former, latter):
    return lax.dot_general(former, latter, (((0,), (0,)), ((), ())), preferred_element_type=F32)


def call(body, name, out_shape, grid, in_specs, out_specs, scratch=(), aliases=None):
    return pl.pallas_call(
        body,
        name=name,
        out_shape=out_shape,
        grid_spec=pltpu.PrefetchScalarGridSpec(
            num_scalar_prefetch=1,
            grid=grid,
            in_specs=in_specs,
            out_specs=out_specs,
            scratch_shapes=list(scratch),
        ),
        input_output_aliases=aliases or {},
        compiler_params=pltpu.CompilerParams(vmem_limit_bytes=VMEM_LIMIT),
        cost_estimate=pl.CostEstimate(
            flops=1, bytes_accessed=int(COST_SCALE * COSTS[name] * 3690000), transcendentals=0
        ),
    )


def shaped(shape, kind):
    return jax.ShapeDtypeStruct(shape, kind)


def whole(shape):
    return pl.BlockSpec(shape, lambda i, s: (0,) * len(shape), pipeline_mode=pl.Buffered(1))


def rows_of(shape):
    return pl.BlockSpec(shape, lambda i, s: (i, 0))


def norm_stats(series):
    center = jnp.mean(series, -1, keepdims=True)
    spread = jnp.mean(series * series, -1, keepdims=True) - center * center
    inverse = lax.rsqrt(spread + EPSILON)
    return (series - center) * inverse, inverse


def norm_back(grad, gain, hat, inverse):
    scaled = grad * gain
    first = jnp.mean(scaled, -1, keepdims=True)
    second = jnp.mean(scaled * hat, -1, keepdims=True)
    return inverse * (scaled - first - hat * second)


def put_blocks(s_ref, pieces, places, target, column, width):
    at = 0
    for piece in pieces:
        depth = piece.shape[1]
        for block in range(piece.shape[0]):
            row = (s_ref[0] ^ places[at]) * depth
            if depth % 16 == 0:
                row = pl.multiple_of(row, 16)
            target[pl.ds(row, depth), pl.ds(column, width)] = piece[block, :, 0:width]
            at += 1


def put_rows(s_ref, mine, other, places, target, column, folds):
    near = s_ref[1] == 0
    own = mine.shape[1] // folds
    width = mine.shape[2]
    for block in range(mine.shape[0]):
        row = pl.multiple_of((s_ref[0] ^ places[block]) * (2 * own), 16)
        one, two = mine[block].astype(F32), other[block].astype(F32)
        upper, lower = jnp.where(near, one, two), jnp.where(near, two, one)
        for at in range(folds):
            rows = slice(at * own, (at + 1) * own)
            target[pl.ds(row, 2 * own), column + at * width : column + (at + 1) * width] = jnp.concatenate(
                [upper[rows], lower[rows]], 0
            ).astype(BF16)


def project(inputs, parts, places, scalars):
    rows, width = inputs.shape
    tile = min(TILE, rows)
    flat = [piece for part in parts for piece in part]
    cuts = [part[0].shape[2] for part in parts]
    columns = sum(cuts)

    def body(s_ref, x_ref, *refs):
        pieces, (q_ref, kv_ref, n_ref, w_ref, g_ref, full) = refs[: len(flat)], refs[len(flat) :]

        @pl.when(pl.program_id(0) == 0)
        def _():
            at = 0
            for k, part in enumerate(parts):
                column = sum(cuts[:k])
                if len(part) == 2:
                    put_rows(s_ref, pieces[at], pieces[at + 1], places[k], full, column, 1)
                else:
                    put_blocks(s_ref, pieces[at : at + 1], places[k], full, column, cuts[k])
                at += len(part)
            w_ref[...] = full[:, 0 : 3 * width]
            g_ref[...] = jnp.transpose(full[:, 3 * width : 3 * width + 128].astype(F32))[0:8]

        hat, _ = norm_stats(x_ref[...].astype(F32))
        low = (hat * g_ref[0:1, :]).astype(BF16)
        n_ref[...] = low
        q_ref[...] = mm(low, full[:, 0:width]).astype(BF16)
        for which in range(2):
            part = mm(low, full[:, (1 + which) * width : (2 + which) * width]).astype(BF16)
            for pair in range(width // PAIR):
                at = (2 * pair + which) * PAIR
                kv_ref[:, at : at + PAIR] = part[:, pair * PAIR : (pair + 1) * PAIR]

    spec = rows_of((tile, width))
    return call(
        body,
        "project",
        (
            shaped((rows, width), BF16),
            shaped((rows, 2 * width), BF16),
            shaped((rows, width), BF16),
            shaped((width, 3 * width), BF16),
            shaped((8, width), F32),
        ),
        (rows // tile,),
        [spec] + [whole(p.shape) for p in flat],
        (spec, rows_of((tile, 2 * width)), spec, whole((width, 3 * width)), whole((8, width))),
        scratch=[pltpu.VMEM((width, columns), BF16)],
    )(scalars, inputs, *flat)


def lane_of(head):
    lanes = lax.broadcasted_iota(jnp.int32, (1, PAIR), 1)
    return (lanes >= head * HEAD_DIM) & (lanes < (head + 1) * HEAD_DIM)


def attend(queries, near, far_side, scalars):
    rows, width = queries.shape
    tile = min(TILE, rows)
    pairs = width // PAIR

    def body(s_ref, q_ref, kv_ref, fkv_ref, o_ref, l_ref):
        offset = s_ref[1] * rows
        length = s_ref[2]

        def run(far):
            query = q_ref[...] * jnp.asarray(0.125, BF16)
            for t in range(rows // tile):
                end = (t + 1) * tile
                place = lax.broadcasted_iota(jnp.int32, (tile, end), 0) + t * tile
                key_at = lax.broadcasted_iota(jnp.int32, (tile, end), 1)
                allowed = (key_at <= place) & (key_at + offset < length)
                sums = []
                logs = []
                for head in range(2):
                    mine = jnp.where(
                        lane_of(head), query[t * tile : end], jnp.zeros((), BF16)
                    )
                    scores = jnp.where(allowed, mm_tail(mine, kv_ref[0:end, 0:PAIR]), MASKED)
                    highest = jnp.max(scores, -1, keepdims=True)
                    if far:
                        beyond = mm_tail(mine, fkv_ref[:, 0:PAIR])
                        highest = jnp.maximum(highest, jnp.max(beyond, -1, keepdims=True))
                        beyond = jnp.exp(beyond - highest)
                    scores = jnp.exp(scores - highest)
                    total = jnp.sum(scores, -1, keepdims=True)
                    mixed = mm(scores.astype(BF16), kv_ref[0:end, PAIR : 2 * PAIR])
                    if far:
                        total = total + jnp.sum(beyond, -1, keepdims=True)
                        mixed = mixed + mm(beyond.astype(BF16), fkv_ref[:, PAIR : 2 * PAIR])
                    sums.append(mixed / total)
                    logs.append(jnp.broadcast_to(highest + jnp.log(total), (tile, PAIR)))
                o_ref[t * tile : end] = jnp.where(lane_of(0), sums[0], sums[1]).astype(BF16)
                turned = jnp.transpose(jnp.where(lane_of(0), logs[0], logs[1]))
                upper = lax.broadcasted_iota(jnp.int32, (8, tile), 0) < 4
                l_ref[0, :, t * tile : end] = jnp.where(upper, turned[0:8], turned[HEAD_DIM : HEAD_DIM + 8])

        @pl.when(s_ref[1] == 0)
        def _():
            run(False)

        @pl.when(s_ref[1] != 0)
        def _():
            run(True)

    spec = pl.BlockSpec((rows, PAIR), lambda i, s: (0, i))
    both = pl.BlockSpec((rows, 2 * PAIR), lambda i, s: (0, i))
    log_spec = pl.BlockSpec((1, 8, rows), lambda i, s: (i, 0, 0))
    return call(
        body,
        "attend",
        (shaped((rows, width), BF16), shaped((pairs, 8, rows), F32)),
        (pairs,),
        [spec, both, both],
        (spec, log_spec),
    )(scalars, queries, near, far_side)


def attend_back(queries, near, far_side, grads, attended, logs, scalars, first, pairs):
    rows = queries.shape[0]
    tile = min(TILE, rows)
    width = pairs * PAIR

    def body(
        s_ref, q_ref, kv_ref, fkv_ref, d_ref, o_ref, l_ref,
        dq_ref, dkv_ref, fdkv_ref,
    ):
        offset = s_ref[1] * rows
        length = s_ref[2]

        def run(far):
            query = q_ref[...] * jnp.asarray(0.125, BF16)
            grad = d_ref[...]
            picker = jnp.where(
                lax.broadcasted_iota(jnp.int32, (8, PAIR), 1) // HEAD_DIM
                == lax.broadcasted_iota(jnp.int32, (8, PAIR), 0),
                1.0,
                0.0,
            ).astype(F32)
            dots = lax.dot_general(
                picker,
                grad.astype(F32) * o_ref[...].astype(F32),
                (((1,), (1,)), ((), ())),
                precision=lax.Precision.HIGHEST,
                preferred_element_type=F32,
            )
            blocks = [
                (kv_ref, dkv_ref, t * tile, t * tile, True)
                for t in range(rows // tile)
            ]
            if far:
                blocks += [
                    (fkv_ref, fdkv_ref, t * tile, 0, False)
                    for t in range(rows // tile)
                ]
            turned = [[jnp.zeros((HEAD_DIM, tile), F32) for _ in range(rows // tile)] for _ in range(2)]
            for pair_ref, dpair_ref, at, low, masked in blocks:
                key = pair_ref[at : at + tile, 0:PAIR]
                value = pair_ref[at : at + tile, PAIR : 2 * PAIR]
                key_turned = jnp.transpose(key)
                count = rows - low
                kgrads, vgrads = [], []
                if masked:
                    key_at = lax.broadcasted_iota(jnp.int32, (tile, count), 0) + at
                    place = lax.broadcasted_iota(jnp.int32, (tile, count), 1) + low
                    allowed = (key_at <= place) & (key_at + offset < length)
                for head in range(2):
                    lanes = lane_of(head)
                    mine = jnp.where(lanes, query[low:rows], jnp.zeros((), BF16))
                    mine_grad = jnp.where(lanes, grad[low:rows], jnp.zeros((), BF16))
                    scores = mm_tail(key, mine)
                    if masked:
                        scores = jnp.where(allowed, scores, MASKED)
                    base = head * HEAD_DIM
                    probs = jnp.exp(scores - l_ref[0, 4 * head : 4 * head + 1, low:rows])
                    prob_grad = mm_tail(value, mine_grad)
                    score_grad = (probs * (prob_grad - dots[head : head + 1, low:rows])).astype(BF16)
                    vgrads.append(mm(probs.astype(BF16), grad[low:rows]))
                    kgrads.append(mm(score_grad, query[low:rows]))
                    part = mm(key_turned[base : base + HEAD_DIM], score_grad)
                    for t in range(low // tile, rows // tile):
                        turned[head][t] = turned[head][t] + part[:, t * tile - low : (t + 1) * tile - low]
                dpair_ref[at : at + tile, 0:PAIR] = jnp.where(lane_of(0), kgrads[0], kgrads[1]).astype(dpair_ref.dtype)
                dpair_ref[at : at + tile, PAIR : 2 * PAIR] = jnp.where(lane_of(0), vgrads[0], vgrads[1]).astype(dpair_ref.dtype)
            for t in range(rows // tile):
                both = jnp.concatenate([turned[0][t], turned[1][t]], 0)
                dq_ref[t * tile : (t + 1) * tile] = (jnp.transpose(both) * 0.125).astype(BF16)

        @pl.when(s_ref[1] == 0)
        def _():
            run(False)
            fdkv_ref[...] = jnp.zeros_like(fdkv_ref)

        @pl.when(s_ref[1] != 0)
        def _():
            run(True)

    spec = pl.BlockSpec((rows, PAIR), lambda i, s: (0, i + first))
    both = pl.BlockSpec((rows, 2 * PAIR), lambda i, s: (0, i + first))
    own = pl.BlockSpec((rows, PAIR), lambda i, s: (0, i))
    own_both = pl.BlockSpec((rows, 2 * PAIR), lambda i, s: (0, i))
    log_spec = pl.BlockSpec((1, 8, rows), lambda i, s: (i + first, 0, 0))
    return call(
        body,
        "attend_back",
        (shaped((rows, width), BF16), shaped((rows, 2 * width), BF16), shaped((rows, 2 * width), BF16)),
        (pairs,),
        [spec, both, both, spec, spec, log_spec],
        (own, own_both, own_both),
    )(scalars, queries, near, far_side, grads, attended, logs)


def join(attended, inputs, parts, places, gains, scalars):
    rows, width = attended.shape
    tile = min(TILE, rows)
    flat = parts

    def body(s_ref, a_ref, x_ref, g_ref, *refs):
        pieces, (sub_ref, mid_ref, ffn_ref, w_ref) = refs[: len(flat)], refs[len(flat) :]

        @pl.when(pl.program_id(0) == 0)
        def _():
            if len(parts) == 2:
                put_rows(s_ref, pieces[0], pieces[1], places, w_ref, 0, width // pieces[0].shape[2])
            else:
                put_blocks(s_ref, pieces, places, w_ref, 0, width)

        hat, _ = norm_stats(a_ref[...].astype(F32))
        low = (hat * g_ref[1:2, :]).astype(BF16)
        sub_ref[...] = low
        middle = x_ref[...].astype(F32) + mm(low, w_ref[...])
        mid_ref[...] = middle
        hat, _ = norm_stats(middle)
        ffn_ref[...] = (hat * g_ref[2:3, :]).astype(BF16)

    spec = rows_of((tile, width))
    return call(
        body,
        "join",
        (
            shaped((rows, width), BF16),
            shaped((rows, width), F32),
            shaped((rows, width), BF16),
            shaped((width, width), BF16),
        ),
        (rows // tile,),
        [spec, spec, whole((8, width))] + [whole(p.shape) for p in flat],
        (spec,) * 3 + (whole((width, width)),),
    )(scalars, attended, inputs, gains, *flat)


def join_back(branch, far_branch, fgrad, far_fgrad, middle, cotangent, attended, weights, gains, scalars):
    rows, width = middle.shape
    tile = min(TILE, rows)
    steps = rows // tile

    def body(
        s_ref, b_ref, fb_ref, f_ref, ff_ref, m_ref, c_ref, a_ref, w_ref, g_ref,
        out_ref, mg_ref, ml_ref, ag_ref,
    ):
        step = pl.program_id(0)
        places = lax.broadcasted_iota(jnp.int32, (tile, 1), 0) + (step * tile + s_ref[1] * rows)
        kept = (places < s_ref[2]).astype(F32)
        middle = m_ref[...]
        branch = b_ref[...].astype(F32) + fb_ref[...].astype(F32)
        out_ref[...] = (kept * (middle + branch)).astype(BF16)
        hat, inverse = norm_stats(middle)
        grad = f_ref[...].astype(F32) + ff_ref[...].astype(F32)
        middle_grad = c_ref[...].astype(F32) * kept + norm_back(grad, g_ref[2:3, :], hat, inverse)
        mg_ref[...] = middle_grad
        low = middle_grad.astype(BF16)
        ml_ref[...] = low
        sub_grad = mm_tail(low, w_ref[...])
        hat, inverse = norm_stats(a_ref[...].astype(F32))
        ag_ref[...] = norm_back(sub_grad, g_ref[1:2, :], hat, inverse).astype(BF16)

    spec = rows_of((tile, width))
    return call(
        body,
        "join_back",
        (
            shaped((rows, width), BF16),
            shaped((rows, width), F32),
            shaped((rows, width), BF16),
            shaped((rows, width), BF16),
        ),
        (steps,),
        [spec] * 7 + [whole((width, width)), whole((8, width))],
        (spec,) * 4,
    )(scalars, branch, far_branch, fgrad, far_fgrad, middle, cotangent, attended, weights, gains)


def two_sided(tile, width, steps):
    near = pl.BlockSpec((tile, width), lambda i, s: (jnp.minimum(i, steps - 1), 0))
    far = pl.BlockSpec((tile, width), lambda i, s: (jnp.maximum(i - steps, 0), 0))
    return near, far


def stat_rows(first, second):
    lanes = lax.broadcasted_iota(jnp.int32, (first.shape[0], 128), 1)
    return jnp.transpose(jnp.where(lanes == 0, first, jnp.where(lanes == 1, second, 0.0)))[0:8]


def stat_columns(mine, other):
    both = jnp.transpose(mine + other)
    return both[:, 0:1], both[:, 1:2]


def unit_norm(mine, other, total):
    sums, squares = stat_columns(mine, other)
    center = sums / total
    return center, lax.rsqrt(squares / total - center * center + EPSILON)


def fold(value):
    out = value[:, 0:128]
    for at in range(128, value.shape[1], 128):
        out = out + value[:, at : at + 128]
    return out


def to_side(near, near_ref, far_ref, value):
    low = value.astype(BF16)

    @pl.when(near)
    def _():
        near_ref[...] = low

    @pl.when(jnp.logical_not(near))
    def _():
        far_ref[...] = low


def stats_of(tile):
    return pl.BlockSpec((8, tile), lambda i, s: (0, i))


def other_stats(tile, steps):
    return pl.BlockSpec((8, tile), lambda i, s: (0, lax.rem(i + steps, 2 * steps)))


def ffn_in(near, far, parts, places, units, scalars):
    rows, width = near.shape
    pieces = [piece for part in parts for piece in part]
    cuts = [part[0].shape[2] for part in parts]
    cuts[-1] = units - sum(cuts[:-1])
    tile = min(TILE, rows)
    steps = rows // tile
    chunk = 256

    def body(s_ref, n_ref, f_ref, *refs):
        blocks, (act_ref, slope_ref, stat_ref, w_ref) = refs[: len(pieces)], refs[len(pieces) :]

        @pl.when(pl.program_id(0) == 0)
        def _():
            at = 0
            for k, part in enumerate(parts):
                put_blocks(s_ref, blocks[at : at + len(part)], places[k], w_ref, sum(cuts[:k]), cuts[k])
                at += len(part)

        low = jnp.where(pl.program_id(0) < steps, n_ref[...], f_ref[...])
        sums = jnp.zeros((tile, 128), F32)
        squares = jnp.zeros((tile, 128), F32)
        for at in range(0, units, chunk):
            pre = mm(low, w_ref[:, at : at + chunk])
            cdf = 0.5 * (1.0 + lax.erf(pre * 0.7071067811865476))
            pdf = 0.3989422804014327 * jnp.exp(-0.5 * pre * pre)
            act = pre * cdf
            act_ref[:, at : at + chunk] = act.astype(BF16)
            slope_ref[:, at : at + chunk] = (cdf + pre * pdf).astype(slope_ref.dtype)
            sums = sums + fold(act)
            squares = squares + fold(act * act)
        stat_ref[...] = stat_rows(
            jnp.sum(sums, -1, keepdims=True), jnp.sum(squares, -1, keepdims=True)
        )

    near_spec, far_spec = two_sided(tile, width, steps)
    return call(
        body,
        "ffn_in",
        (
            shaped((2 * rows, units), BF16),
            shaped((2 * rows, units), BF16),
            shaped((8, 2 * rows), F32),
            shaped((width, units), BF16),
        ),
        (2 * steps,),
        [near_spec, far_spec] + [whole(p.shape) for p in pieces],
        (rows_of((tile, units)), rows_of((tile, units)), stats_of(tile), whole((width, units))),
    )(scalars, near, far, *pieces)


def ffn_out(act, stats, far_stats, gain, near_grad, far_grad, weights, scalars, order):
    rows, width = near_grad.shape
    units = act.shape[1]
    tile = min(TILE, rows)
    steps = rows // tile
    depth = width // len(order)
    chunk = 256

    def body(s_ref, a_ref, st_ref, fs_ref, g_ref, n_ref, f_ref, w_ref, b_ref, fb_ref, stat_ref, out_ref, stash, tilt):
        step = pl.program_id(0)
        weight = w_ref.at[0]

        @pl.when(step == 0)
        def _():
            tilt[...] = mm_tail(jnp.broadcast_to(g_ref[...], (8, units)).astype(BF16), weight[...])

        center, inverse = unit_norm(st_ref[...], fs_ref[...], 2 * units)
        at_row = pl.multiple_of(step * tile, tile)
        for at in range(0, units, chunk):
            hat = (a_ref[:, at : at + chunk].astype(F32) - center) * inverse
            stash[pl.ds(at_row, tile), at : at + chunk] = (hat * g_ref[:, at : at + chunk]).astype(BF16)
        branch = mm_tail(stash[pl.ds(at_row, tile), :], weight[...])
        to_side(step < steps, b_ref, fb_ref, branch)
        inside = pl.multiple_of(lax.rem(step, steps) * tile, tile)
        grad = jnp.where(step < steps, n_ref[pl.ds(inside, tile)], f_ref[pl.ds(inside, tile)]).astype(F32)
        stat_ref[...] = stat_rows(
            jnp.sum(fold(grad * tilt[0:1, :]), -1, keepdims=True),
            jnp.sum(fold(grad * branch), -1, keepdims=True),
        )

        @pl.when(step == 2 * steps - 1)
        def _():
            near_turned, far_turned = jnp.transpose(n_ref[...]), jnp.transpose(f_ref[...])
            for at in range(0, units, 512):
                part = mm(near_turned, stash[0:rows, at : at + 512]) + mm(far_turned, stash[rows:, at : at + 512])
                for to, block in enumerate(order):
                    out_ref[to * depth : (to + 1) * depth, at : at + 512] = part[
                        block * depth : (block + 1) * depth
                    ].astype(BF16)

    return call(
        body,
        "ffn_out",
        (
            shaped((rows, width), BF16),
            shaped((rows, width), BF16),
            shaped((8, 2 * rows), F32),
            shaped((width, units), BF16),
        ),
        (2 * steps,),
        [
            rows_of((tile, units)),
            stats_of(tile),
            other_stats(tile, steps),
            whole((1, units)),
            whole((rows, width)),
            whole((rows, width)),
            whole((1, width, units)),
        ],
        two_sided(tile, width, steps) + (stats_of(tile), whole((width, units))),
        scratch=[pltpu.VMEM((2 * rows, units), BF16), pltpu.VMEM((8, width), F32)],
    )(scalars, act, stats, far_stats, gain, near_grad, far_grad, weights)


def ffn_back(
    act, slope, stats, far_stats, grads, far_grads, gain, near_grad, far_grad, near, far, out_weights, in_weights, scalars, blocks
):
    rows, width = near.shape
    units = act.shape[1]
    tile = min(TILE, rows)
    steps = rows // tile
    depth = width // blocks
    chunk = 256
    piece = units // 4

    def body(
        s_ref, a_ref, sl_ref, st_ref, fs_ref, gt_ref, fg_ref, g_ref, ng_ref, fgr_ref, n_ref, f_ref, wo_ref, wi_ref,
        b_ref, fb_ref, four_ref, *rest,
    ):
        outs, (stash, fourth, total) = rest[:-3], rest[-3:]
        step = pl.program_id(0)
        center, inverse = unit_norm(st_ref[...], fs_ref[...], 2 * units)
        first, second = stat_columns(gt_ref[...], fg_ref[...])
        first, second = first / (2 * units), second / (2 * units)
        at_row = pl.multiple_of(step * tile, tile)
        inside = pl.multiple_of(lax.rem(step, steps) * tile, tile)
        grad = jnp.where(step < steps, ng_ref[pl.ds(inside, tile)], fgr_ref[pl.ds(inside, tile)])

        @pl.when(step == 0)
        def _():
            fourth[...] = jnp.zeros_like(fourth)

        for at in range(0, units, chunk):
            normed = mm(grad, wo_ref[0, :, at : at + chunk])
            hat = (a_ref[:, at : at + chunk].astype(F32) - center) * inverse
            fourth[:, at : at + chunk] += jnp.sum((normed * hat).reshape(tile // 8, 8, chunk), 0)
            act_grad = inverse * (normed * g_ref[:, at : at + chunk] - first - hat * second)
            stash[pl.ds(at_row, tile), at : at + chunk] = (
                act_grad * sl_ref[:, at : at + chunk].astype(F32)
            ).astype(BF16)
        to_side(step < steps, b_ref, fb_ref, mm_tail(stash[pl.ds(at_row, tile), :], wi_ref[...]))

        @pl.when(step == 2 * steps - 1)
        def _():
            value = jnp.sum(fourth[...], 0, keepdims=True)
            four_ref[...] = jnp.broadcast_to(value, four_ref.shape)
            near_turned, far_turned = jnp.transpose(n_ref[...]), jnp.transpose(f_ref[...])
            for at in range(0, units, piece):
                part = mm(near_turned, stash[0:rows, at : at + piece]) + mm(far_turned, stash[rows:, at : at + piece])
                if blocks == 1:
                    outs[0][:, at : at + piece] = part.astype(BF16)
                else:
                    total[...] = part
                    order = 0 if at < units // 2 else 1
                    inside = at - order * (units // 2)
                    for block in range(blocks):
                        slot = slot_of(block ^ s_ref[0], order, blocks)
                        low = total[block * depth : (block + 1) * depth].astype(BF16)

                        @pl.when(slot < blocks // 2)
                        def _():
                            outs[0][pl.ds(pl.multiple_of(slot * depth, 16), depth), at : at + piece] = low

                        @pl.when(slot >= blocks // 2)
                        def _():
                            row = pl.multiple_of((slot - blocks // 2) * depth, 16)
                            outs[1 + order][pl.ds(row, depth), inside : inside + piece] = low
            if blocks > 1:
                high = value.astype(BF16)
                rest_of = (value - high.astype(F32)).astype(BF16)
                at_line = lax.broadcasted_iota(jnp.int32, (EXTRA, units), 0)
                extra = jnp.where(at_line == 0, high.astype(F32), jnp.where(at_line == 1, rest_of.astype(F32), 0.0))
                extra = extra.astype(BF16)
                outs[1][width // 2 : width // 2 + EXTRA] = extra[:, : units // 2]
                outs[2][width // 2 : width // 2 + EXTRA] = extra[:, units // 2 :]

    wide = rows_of((tile, units))
    crossing = (width // 2 + EXTRA, units // 2)
    shapes = ((width, units),) if blocks == 1 else ((width // 2, units), crossing, crossing)
    return call(
        body,
        "ffn_back",
        (shaped((rows, width), BF16), shaped((rows, width), BF16), shaped((8, units), F32))
        + tuple(shaped(shape, BF16) for shape in shapes),
        (2 * steps,),
        [
            wide, wide, stats_of(tile), other_stats(tile, steps), stats_of(tile), other_stats(tile, steps),
            whole((1, units)),
        ]
        + [whole((rows, width))] * 4
        + [whole((1, width, units)), whole((width, units))],
        two_sided(tile, width, steps) + (whole((8, units)),) + tuple(whole(shape) for shape in shapes),
        scratch=[
            pltpu.VMEM((2 * rows, units), BF16),
            pltpu.VMEM((8, units), F32),
            pltpu.VMEM((width, piece), F32),
        ],
    )(
        scalars, act, slope, stats, far_stats, grads, far_grads, gain, near_grad, far_grad, near, far, out_weights,
        in_weights,
    )


def slot_of(position, order, blocks):
    if blocks < 4:
        return position
    low = (position >> order) & 1
    high = (position >> (1 - order)) & 1
    return low * (blocks // 2) + high * (blocks // 4) + (position >> 2)


def project_grads(normed, dq, dkv, far_dkv, extra, parts, scalars, blocks):
    rows, width = normed.shape
    cols = dq.shape[1]
    depth = width // blocks
    own = depth // 2
    total = 3 * cols + (width if extra else 0)
    pairs = cols // PAIR
    shape = (blocks, own, total) if blocks > 1 else (1, width, total)

    def body(s_ref, n_ref, q_ref, kv_ref, fkv_ref, *refs):
        if extra:
            left_ref, right_ref = refs[:2]
            refs = refs[2:]
        low_ref, *outs, grad_ref = refs
        me, core = s_ref[0], s_ref[1]
        near = core == 0
        both = kv_ref[...].astype(F32) + jnp.where(near, fkv_ref[...].astype(F32), 0.0)
        low_ref[:, 0:cols] = q_ref[...]
        for pair in range(pairs):
            for which in range(2):
                to = (1 + which) * cols + pair * PAIR
                at = (2 * pair + which) * PAIR
                low_ref[:, to : to + PAIR] = both[:, at : at + PAIR].astype(BF16)
        turned = jnp.transpose(n_ref[...])
        grad_ref[:, 0 : 3 * cols] = mm(turned, low_ref[...])
        if extra:
            grad_ref[:, 3 * cols : total] = mm_lead(left_ref[...], right_ref[...])
        if blocks == 1:
            outs[0][0] = grad_ref[...].astype(BF16)
            return
        for side in range(2):
            owner = core if side == 0 else 1 - core
            later, *firsts = outs[3 * side : 3 * side + 3]
            for block in range(blocks):
                position = block ^ me
                row = pl.multiple_of(block * depth + owner * own, 8)
                for order, start, end in parts:
                    slot = slot_of(position, order, blocks)
                    low = grad_ref[pl.ds(row, own), start:end].astype(BF16)

                    @pl.when(slot < blocks // 2)
                    def _():
                        later[slot, :, start:end] = low

                    @pl.when(slot >= blocks // 2)
                    def _():
                        firsts[order][slot - blocks // 2] = low

    more = list(extra) if extra else []
    shapes = [shape]
    if blocks > 1:
        shapes = [(blocks // 2, own, total)] + [(blocks // 2, own, end - start) for _, start, end in parts]
        shapes = shapes * 2
    return call(
        body,
        "project_grads",
        (shaped((rows, 3 * cols), BF16),) + tuple(shaped(each, BF16) for each in shapes),
        (1,),
        [whole((rows, width)), whole((rows, cols)), whole((rows, 2 * cols)), whole((rows, 2 * cols))]
        + [whole((rows, width))] * len(more),
        (whole((rows, 3 * cols)),) + tuple(whole(each) for each in shapes),
        scratch=[pltpu.VMEM((width, total), F32)],
    )(scalars, normed, dq, dkv, far_dkv, *more)


def finish(pieces, query_key, value_proj, output_proj, gains, scalars):
    rows, columns = pieces[0].shape
    width = columns // 4

    def body(s_ref, *refs):
        ins = refs[: len(pieces)]
        qk_ref, v_ref, o_ref, one_ref, two_ref, qk_out, v_out, o_out, one_out, two_out = refs[len(pieces) :]

        def total(start, end):
            value = ins[0][:, start:end].astype(F32)
            for piece in ins[1:]:
                value = value + piece[:, start:end].astype(F32)
            return value

        qk, v, o = total(0, 2 * width), total(2 * width, 3 * width), total(3 * width, columns)
        qk_out[...] = qk
        v_out[...] = v
        o_out[...] = o
        one = fold(qk * qk_ref[...].astype(F32)) + fold(v * v_ref[...].astype(F32))
        two = fold(o * o_ref[...].astype(F32))
        for sums, gain_ref, out in ((one, one_ref, one_out), (two, two_ref, two_out)):
            turned = lax.dot_general(
                jnp.ones((8, 128), F32),
                sums,
                (((1,), (1,)), ((), ())),
                precision=lax.Precision.HIGHEST,
                preferred_element_type=F32,
            )
            out[...] = turned[0:1] / gain_ref[...]

    shapes = ((rows, 2 * width), (rows, width), (rows, width), (1, rows), (1, rows))
    return call(
        body,
        "finish",
        tuple(shaped(shape, F32) for shape in shapes),
        (1,),
        [whole(p.shape) for p in pieces] + [whole(shape) for shape in shapes],
        tuple(whole(shape) for shape in shapes),
    )(scalars, *pieces, query_key, value_proj, output_proj, *gains)


def project_back(lows, inputs, middle_grad, weights, gains, scalars):
    rows, width = inputs.shape
    tile = min(TILE, rows)
    sizes = [low.shape[1] // 3 for low in lows]

    def body(s_ref, *refs):
        low_refs, (x_ref, m_ref, w_ref, g_ref, out_ref) = refs[: len(lows)], refs[len(lows) :]
        hat, inverse = norm_stats(x_ref[...].astype(F32))
        grad = jnp.zeros((tile, width), F32)
        at = 0
        for low_ref, size in zip(low_refs, sizes):
            for which in range(3):
                base = which * width + at
                grad = grad + mm_tail(
                    low_ref[:, which * size : (which + 1) * size], w_ref[:, base : base + size]
                )
            at += size
        out_ref[...] = (m_ref[...] + norm_back(grad, g_ref[0:1, :], hat, inverse)).astype(BF16)

    spec = rows_of((tile, width))
    return call(
        body,
        "project_back",
        shaped((rows, width), BF16),
        (rows // tile,),
        [rows_of((tile, 3 * size)) for size in sizes]
        + [spec, spec, whole((width, 3 * width)), whole((8, width))],
        spec,
    )(scalars, *lows, inputs, middle_grad, weights, gains)


CHIPS = ("outer", "inner")
CORES = "tensor"


def other_core(array):
    return lax.ppermute(array, CORES, [(0, 1), (1, 0)])


def exchange(array, mask, chips):
    return lax.ppermute(array, CHIPS, [(i, i ^ mask) for i in range(chips)])


def bit_count(chips):
    return chips.bit_length() - 1


def by_core(mine, other, axis):
    core = lax.axis_index(CORES)
    return jnp.where(
        core == 0,
        jnp.concatenate([mine, other], axis),
        jnp.concatenate([other, mine], axis),
    )


def after(value, *others):
    return lax.optimization_barrier((value,) + others)[0]


def gather_outer(shard, chips):
    places = list(range(0, chips, 4))
    return jnp.stack([shard] + [exchange(shard, mask, chips) for mask in places[1:]], 0), places


def widen(pieces, places, mask, chips):
    held = pieces[0] if len(pieces) == 1 else jnp.concatenate(pieces, 0)
    return pieces + [exchange(held, mask, chips)], places + [p | mask for p in places]


def on_device(
    inputs,
    cotangent,
    lengths,
    query_key,
    value_proj,
    output_proj,
    hidden_in,
    hidden_out,
    first_gain,
    second_gain,
    third_gain,
    fourth_gain,
):
    rows, width = inputs.shape[1:]
    chips = lax.axis_size(CHIPS)
    inner = lax.axis_size("inner")
    chip = lax.axis_index(CHIPS)
    core = lax.axis_index(CORES)
    barrier = lax.optimization_barrier
    depth = width // chips
    pairwise = chips & (chips - 1) == 0 and chips >= 4 and depth % 16 == 0
    series = inputs[0]
    scalars = jnp.stack([chip if pairwise else jnp.zeros_like(chip), core, lengths[0]]).astype(jnp.int32)
    scalars = jnp.concatenate([scalars, jnp.zeros((5,), jnp.int32)])

    gain_columns = jnp.stack([first_gain, second_gain, third_gain], 1)
    gain_columns = jnp.pad(gain_columns, ((0, 0), (0, 256 - 3)))
    shard = jnp.concatenate([query_key, value_proj, gain_columns], 1)
    half = shard.shape[1]
    units = hidden_in.shape[1]
    if pairwise:
        stack, places = gather_outer(shard, chips)
        cut = -(-half // 256) * 128
        o_folded = jnp.concatenate([output_proj[:, : width // 2], output_proj[:, width // 2 :]], 0)
        late_shard = jnp.concatenate([hidden_in, o_folded], 1)
        late_out = hidden_out.T
        stack, late_shard = barrier((stack, late_shard))
        out_weights_ff = lax.all_gather(late_out, CHIPS, axis=0, tiled=True)[None]
        first, first_places = widen([stack[:, :, :cut]], places, 2, chips)
        second, second_places = widen([stack[:, :, cut:]], places, 1, chips)
        late, late_places = gather_outer(late_shard, chips)
        first[-1], second[-1] = barrier((first[-1], second[-1]))
        first, first_places = widen(first, first_places, 1, chips)
        second, second_places = widen(second, second_places, 2, chips)
        first[-1], second[-1], late = barrier((first[-1], second[-1], late))
        late_cut = -(-late.shape[2] // 256) * 128
        in_first, in_first_places = widen([late[:, :, :late_cut]], late_places, 1, chips)
        in_second, in_second_places = widen([late[:, :, late_cut:]], late_places, 2, chips)
        mine = [jnp.concatenate(first, 0), jnp.concatenate(second, 0)]
        parts = [[p, other_core(p)] for p in mine]
        part_places = [first_places, second_places]
    else:
        gathered = lax.all_gather(shard, CHIPS + (CORES,), axis=0, tiled=True)
        parts, part_places = [[gathered[None]]], [[0]]
        in_parts = [[lax.all_gather(hidden_in, CHIPS, axis=0, tiled=True)[None]]]
        in_part_places = [[0]]
        out_weights = lax.all_gather(output_proj, CHIPS + (CORES,), axis=0, tiled=True)
        out_weights_ff = lax.all_gather(hidden_out.T, CHIPS, axis=0, tiled=True)[None]

    kept = (core * rows + jnp.arange(rows) < lengths[0])[:, None]
    near_grad = jnp.where(kept, cotangent[0], jnp.zeros((), BF16))
    far_grad = other_core(near_grad)

    if pairwise:
        series, in_first[0], in_second[0] = barrier((series, in_first[0], in_second[0]))
    queries, near_kv, normed, weights, gains = project(series, parts, part_places, scalars)
    if pairwise:
        near_kv, in_first[-1], in_second[-1] = barrier((near_kv, in_first[-1], in_second[-1]))
    far_kv = lax.ppermute(near_kv, CORES, [(0, 1)])
    if pairwise:
        in_first, in_first_places = widen(in_first, in_first_places, 2, chips)
        in_second, in_second_places = widen(in_second, in_second_places, 1, chips)
    attended, logs = attend(queries, near_kv, far_kv, scalars)
    if pairwise:
        attended, in_first[-1], in_second[-1] = barrier((attended, in_first[-1], in_second[-1]))
        in_parts = [in_first, in_second]
        in_part_places = [in_first_places, in_second_places]
        extra_columns = units - late_cut
        o_mine = jnp.concatenate(in_second, 0)[:, :, extra_columns:]
        out_parts = [o_mine, other_core(o_mine)]
        sub_low, middle, near, out_weights = join(attended, series, out_parts, in_second_places, gains, scalars)
    else:
        sub_low, middle, near, out_weights = join(attended, series, [out_weights[None]], [0], gains, scalars)
    far = other_core(near)

    if pairwise:
        far, out_weights_ff = barrier((far, out_weights_ff))
    act, slope, stats, in_weights = ffn_in(near, far, in_parts, in_part_places, units, scalars)
    far_stats = other_core(stats)
    outer = chips // inner
    order = list(range(chips))
    if pairwise:
        order = [o * inner + i for i in range(inner) for o in range(outer)]
    gain_four = fourth_gain.astype(F32)[None, :]
    branch, branch_sent, grad_stats, out_payload = ffn_out(
        act, stats, far_stats, gain_four, near_grad, far_grad, out_weights_ff, scalars, order
    )
    if pairwise:
        out_payload = lax.psum_scatter(out_payload, "inner", scatter_dimension=0, tiled=True)
    else:
        out_payload = lax.psum_scatter(out_payload, CHIPS, scatter_dimension=0, tiled=True)
    far_grad_stats = other_core(grad_stats)
    far_branch = other_core(branch_sent)
    blocks = chips if pairwise else 1
    ffn_grad, ffn_grad_sent, fourth_term, *in_payload = ffn_back(
        act, slope, stats, far_stats, grad_stats, far_grad_stats, gain_four, near_grad, far_grad, near, far,
        out_weights_ff, in_weights, scalars, blocks,
    )
    far_ffn_grad = other_core(ffn_grad_sent)
    if pairwise:
        got = [exchange(in_payload[1], 1, chips), exchange(in_payload[2], 2, chips)]
    outputs, middle_grad, middle_low, attended_low = join_back(
        branch, far_branch, ffn_grad, far_ffn_grad, middle, near_grad, attended, out_weights, gains, scalars
    )

    pairs = width // PAIR
    extra = (sub_low, middle_low)
    if pairwise:
        columns = 4 * width
        cut = columns // 2
        middle, lower = chips // 2, chips // 4
        count = width // 2
        dq, dkv, far_dkv = attend_back(queries, near_kv, far_kv, attended_low, attended, logs, scalars, 0, pairs)
        got[0], got[1], out_payload, far_dkv = barrier((got[0], got[1], out_payload, far_dkv))
        far_dkv = lax.ppermute(far_dkv, CORES, [(1, 0)])
        out_payload = lax.psum_scatter(out_payload, "outer", scatter_dimension=0, tiled=True)
        in_kept, fourth = add_parts(in_payload[0][: count // 2], fourth_term[0:1], got, 0, count)
        in_sent, _ = add_parts(in_payload[0][count // 2 :], fourth_term[0:1], got, count // 2, count)
        rows_low = low_rows(fourth)
        sent = [
            jnp.concatenate([in_sent[:, : units // 2], rows_low[:, : units // 2]], 0),
            jnp.concatenate([in_sent[:, units // 2 :], rows_low[:, units // 2 :]], 0),
        ]
        far_dkv, sent[0], sent[1], in_kept = barrier((far_dkv, sent[0], sent[1], in_kept))
        got = [exchange(sent[0], 2, chips), exchange(sent[1], 1, chips)]
        low, keep, keep_one, keep_two, send, send_one, send_two = project_grads(
            normed, dq, dkv, far_dkv, extra, ((0, 0, cut), (1, cut, columns)), scalars, chips
        )
        middle_grad, send, send_one, send_two = barrier((middle_grad, send, send_one, send_two))
        other_one, other_two, other = other_core(send_one), other_core(send_two), other_core(send)
        inputs_grad = project_back([low], series, middle_grad, weights, gains, scalars)
        inputs_grad, other_one, other_two, other, got[0], got[1] = barrier(
            (inputs_grad, other_one, other_two, other, got[0], got[1])
        )
        upper_one, upper_two = add_low(keep_one, other_one), add_low(keep_two, other_two)
        upper_one, upper_two = barrier((upper_one, upper_two))
        got_one, got_two = exchange(upper_one, 1, chips), exchange(upper_two, 2, chips)
        in_held, fourth = add_parts(in_kept, fourth, got, 0, count // 2)
        in_held = in_held.reshape(chips // 4, depth, units)
        sends = barrier(tuple(outer_sends(in_held, fourth)))
        in_got = exchange_outer(sends, chips)
        sent_first = sum_low(keep[lower:, :, :cut], other[lower:, :, :cut], got_one[lower:])
        sent_second = sum_low(keep[lower:, :, cut:], other[lower:, :, cut:], got_two[lower:])
        sent_first, sent_second = barrier((sent_first, sent_second))
        got_first, got_second = exchange(sent_first, 2, chips), exchange(sent_second, 1, chips)
        kept = sum_low(keep[:lower], other[:lower], jnp.concatenate([got_one[:lower], got_two[:lower]], -1))
        got_first, got_second, kept, out_payload = barrier((got_first, got_second, kept, out_payload))
        both = add_low(kept, jnp.concatenate([got_first, got_second], -1))
        both_sends = barrier(tuple(outer_sends(both, None)))
        both_got = exchange_outer(both_sends, chips)
        both_got[0], *in_got = barrier((both_got[0], *in_got))
        in_payload = in_held[0].astype(F32)
        for piece in in_got:
            in_payload = in_payload + piece[:depth].astype(F32)
            fourth = add_rows(fourth, piece[depth:])
        third_part = jnp.sum(hidden_in.astype(F32) * in_payload, 1, keepdims=True)
        third_part = jnp.broadcast_to(third_part, (depth, 128))
        third_part = third_part + other_core(third_part)
        *both_got, third_part = barrier((*both_got, third_part))
        last = [both[0], *both_got]
    else:
        dq, dkv, far_dkv = attend_back(queries, near_kv, far_kv, attended_low, attended, logs, scalars, 0, pairs)
        far_dkv = lax.ppermute(far_dkv, CORES, [(1, 0)])
        low, mine = project_grads(normed, dq, dkv, far_dkv, extra, None, scalars, 1)
        mine = lax.psum_scatter(mine[0], CHIPS, scatter_dimension=0, tiled=True).astype(F32)
        mine = lax.psum(mine, CORES)
        inputs_grad = project_back([low], series, middle_grad, weights, gains, scalars)
        in_payload = lax.psum_scatter(in_payload[0], CHIPS, scatter_dimension=0, tiled=True).astype(F32)
        fourth = lax.psum(fourth_term[0:1], CHIPS)
        last = [lax.dynamic_slice_in_dim(mine, core * (depth // 2), depth // 2, 0)]
        third_part = lax.psum(jnp.sum(hidden_in.astype(F32) * in_payload, 1, keepdims=True), CORES)
    hidden_out_sum = out_payload.astype(F32).T
    hidden_in_sum = in_payload
    third_sum = lax.dynamic_slice_in_dim(third_part[:, 0], core * (depth // 2), depth // 2) / third_gain.astype(F32)
    gain_rows = [gain.astype(F32)[None, :] for gain in (first_gain, second_gain)]
    qk_sum, value_sum, output_sum, first_sum, second_sum = finish(
        last, query_key, value_proj, output_proj, gain_rows, scalars
    )
    first_sum, second_sum = first_sum[0], second_sum[0]
    return (
        outputs[None],
        inputs_grad[None],
        qk_sum,
        value_sum,
        output_sum,
        hidden_in_sum,
        hidden_out_sum,
        first_sum,
        second_sum,
        third_sum,
        fourth[0],
    )


def add_low(kept, got):
    return (kept.astype(F32) + got.astype(F32)).astype(BF16)


def add_rows(value, rows):
    return value + (rows[0:1].astype(F32) + rows[1:2].astype(F32))


def low_rows(vector):
    high = lax.reduce_precision(vector, 8, 7)
    rest = lax.reduce_precision(vector - high, 8, 7)
    return jnp.concatenate([high, rest, jnp.zeros((EXTRA - 2, vector.shape[1]), F32)], 0).astype(BF16)


def outer_sends(held, vector):
    rows = [] if vector is None else [low_rows(vector)]
    return [jnp.concatenate([held[at]] + rows, 0) if rows else held[at] for at in range(1, held.shape[0])]


def exchange_outer(sends, chips):
    return [exchange(send, 4 * (at + 1), chips) for at, send in enumerate(sends)]


def add_parts(kept, vector, got, start, count):
    part = jnp.concatenate([piece[start : start + kept.shape[0]] for piece in got], 1)
    rows = jnp.concatenate([piece[count:] for piece in got], 1)
    return add_low(kept, part), add_rows(vector, rows)


def sum_low(*arrays):
    total = arrays[0].astype(F32)
    for array in arrays[1:]:
        total = total + array.astype(F32)
    return total.astype(BF16)


def solution(mesh):
    chips, cores = mesh.devices.shape
    inner = 4 if chips % 4 == 0 else 1
    split = Mesh(mesh.devices.reshape(chips // inner, inner, cores), CHIPS + (CORES,))
    every = CHIPS + (CORES,)
    return jax.shard_map(
        on_device,
        mesh=split,
        in_specs=(
            P(CHIPS, CORES, None),
            P(CHIPS, CORES, None),
            P(CHIPS),
            P(every, None),
            P(every, None),
            P(every, None),
            P(CHIPS, CORES),
            P(CORES, CHIPS),
            P(every),
            P(every),
            P(every),
            P(CORES),
        ),
        out_specs=(
            P(CHIPS, CORES, None),
            P(CHIPS, CORES, None),
            P(every, None),
            P(every, None),
            P(every, None),
            P(CHIPS, CORES),
            P(CORES, CHIPS),
            P(every),
            P(every),
            P(every),
            P(CORES),
        ),
        check_vma=False,
    )
```

```python
import jax
import jax.numpy as jnp
from jax import lax
from jax.experimental import pallas as pl
from jax.experimental.pallas import tpu as pltpu
from jax.sharding import Mesh
from jax.sharding import PartitionSpec as P

HEAD_DIM = 64
PAIR = 2 * HEAD_DIM
EPSILON = 1e-05
MASKED = -1000000000.0
F32 = jnp.float32
BF16 = jnp.bfloat16
VMEM_LIMIT = 60 * 1024 * 1024
VMEM_LIMITS = {"project_grads": 30 * 1024 * 1024, "finish": 30 * 1024 * 1024}
TILE = 256
EXTRA = 16
COST_SCALE = 0.05
COSTS = {
    "project": 8,
    "attend": 15,
    "join": 5,
    "ffn_in": 10,
    "ffn_out": 10,
    "ffn_back": 14,
    "join_back": 7,
    "attend_back": 20,
    "project_grads": 11,
    "project_back": 7,
    "finish": 2,
}


def mm(former, latter):
    return jnp.dot(former, latter, preferred_element_type=F32)


def mm_tail(former, latter):
    return lax.dot_general(former, latter, (((1,), (1,)), ((), ())), preferred_element_type=F32)


def mm_lead(former, latter):
    return lax.dot_general(former, latter, (((0,), (0,)), ((), ())), preferred_element_type=F32)


def call(body, name, out_shape, grid, in_specs, out_specs, scratch=(), aliases=None):
    return pl.pallas_call(
        body,
        name=name,
        out_shape=out_shape,
        grid_spec=pltpu.PrefetchScalarGridSpec(
            num_scalar_prefetch=1,
            grid=grid,
            in_specs=in_specs,
            out_specs=out_specs,
            scratch_shapes=list(scratch),
        ),
        input_output_aliases=aliases or {},
        compiler_params=pltpu.CompilerParams(vmem_limit_bytes=VMEM_LIMITS.get(name, VMEM_LIMIT)),
        cost_estimate=pl.CostEstimate(
            flops=1, bytes_accessed=int(COST_SCALE * COSTS[name] * 3690000), transcendentals=0
        ),
    )


def shaped(shape, kind):
    return jax.ShapeDtypeStruct(shape, kind)


def whole(shape):
    return pl.BlockSpec(shape, lambda i, s: (0,) * len(shape), pipeline_mode=pl.Buffered(1))


def rows_of(shape):
    return pl.BlockSpec(shape, lambda i, s: (i, 0))


def norm_stats(series):
    center = jnp.mean(series, -1, keepdims=True)
    spread = jnp.mean(series * series, -1, keepdims=True) - center * center
    inverse = lax.rsqrt(spread + EPSILON)
    return (series - center) * inverse, inverse


def norm_back(grad, gain, hat, inverse):
    scaled = grad * gain
    first = jnp.mean(scaled, -1, keepdims=True)
    second = jnp.mean(scaled * hat, -1, keepdims=True)
    return inverse * (scaled - first - hat * second)


def put_blocks(s_ref, pieces, places, target, column, width):
    at = 0
    for piece in pieces:
        depth = piece.shape[1]
        for block in range(piece.shape[0]):
            row = (s_ref[0] ^ places[at]) * depth
            if depth % 16 == 0:
                row = pl.multiple_of(row, 16)
            target[pl.ds(row, depth), pl.ds(column, width)] = piece[block, :, 0:width]
            at += 1


def put_rows(s_ref, mine, other, places, target, column, folds):
    near = s_ref[1] == 0
    own = mine.shape[1] // folds
    width = mine.shape[2]
    for block in range(mine.shape[0]):
        row = pl.multiple_of((s_ref[0] ^ places[block]) * (2 * own), 16)
        one, two = mine[block].astype(F32), other[block].astype(F32)
        upper, lower = jnp.where(near, one, two), jnp.where(near, two, one)
        for at in range(folds):
            rows = slice(at * own, (at + 1) * own)
            target[pl.ds(row, 2 * own), column + at * width : column + (at + 1) * width] = jnp.concatenate(
                [upper[rows], lower[rows]], 0
            ).astype(BF16)


def project(inputs, parts, places, scalars):
    rows, width = inputs.shape
    tile = min(TILE, rows)
    flat = [piece for part in parts for piece in part]
    cuts = [part[0].shape[2] for part in parts]
    columns = sum(cuts)

    def body(s_ref, x_ref, *refs):
        pieces, (q_ref, kv_ref, n_ref, w_ref, g_ref, full) = refs[: len(flat)], refs[len(flat) :]

        @pl.when(pl.program_id(0) == 0)
        def _():
            at = 0
            for k, part in enumerate(parts):
                column = sum(cuts[:k])
                if len(part) == 2:
                    put_rows(s_ref, pieces[at], pieces[at + 1], places[k], full, column, 1)
                else:
                    put_blocks(s_ref, pieces[at : at + 1], places[k], full, column, cuts[k])
                at += len(part)
            w_ref[...] = full[:, 0 : 3 * width]
            g_ref[...] = jnp.transpose(full[:, 3 * width : 3 * width + 128].astype(F32))[0:8]

        hat, _ = norm_stats(x_ref[...].astype(F32))
        low = (hat * g_ref[0:1, :]).astype(BF16)
        n_ref[...] = low
        q_ref[...] = mm(low, full[:, 0:width]).astype(BF16)
        for which in range(2):
            part = mm(low, full[:, (1 + which) * width : (2 + which) * width]).astype(BF16)
            for pair in range(width // PAIR):
                at = (2 * pair + which) * PAIR
                kv_ref[:, at : at + PAIR] = part[:, pair * PAIR : (pair + 1) * PAIR]

    spec = rows_of((tile, width))
    return call(
        body,
        "project",
        (
            shaped((rows, width), BF16),
            shaped((rows, 2 * width), BF16),
            shaped((rows, width), BF16),
            shaped((width, 3 * width), BF16),
            shaped((8, width), F32),
        ),
        (rows // tile,),
        [spec] + [whole(p.shape) for p in flat],
        (spec, rows_of((tile, 2 * width)), spec, whole((width, 3 * width)), whole((8, width))),
        scratch=[pltpu.VMEM((width, columns), BF16)],
    )(scalars, inputs, *flat)


def lane_of(head):
    lanes = lax.broadcasted_iota(jnp.int32, (1, PAIR), 1)
    return (lanes >= head * HEAD_DIM) & (lanes < (head + 1) * HEAD_DIM)


def attend(queries, near, far_side, scalars):
    rows, width = queries.shape
    tile = min(TILE, rows)
    pairs = width // PAIR

    def body(s_ref, q_ref, kv_ref, fkv_ref, o_ref, l_ref):
        offset = s_ref[1] * rows
        length = s_ref[2]

        def run(far):
            query = q_ref[...] * jnp.asarray(0.125, BF16)
            for t in range(rows // tile):
                end = (t + 1) * tile
                place = lax.broadcasted_iota(jnp.int32, (tile, end), 0) + t * tile
                key_at = lax.broadcasted_iota(jnp.int32, (tile, end), 1)
                allowed = (key_at <= place) & (key_at + offset < length)
                sums = []
                logs = []
                near_scores, far_scores = [], []
                for head in range(2):
                    mine = jnp.where(
                        lane_of(head), query[t * tile : end], jnp.zeros((), BF16)
                    )
                    near_scores.append(mm_tail(mine, kv_ref[0:end, 0:PAIR]))
                    if far:
                        far_scores.append(mm_tail(mine, fkv_ref[:, 0:PAIR]))
                for head in range(2):
                    scores = jnp.where(allowed, near_scores[head], MASKED)
                    highest = jnp.max(scores, -1, keepdims=True)
                    if far:
                        beyond = far_scores[head]
                        highest = jnp.maximum(highest, jnp.max(beyond, -1, keepdims=True))
                        beyond = jnp.exp(beyond - highest)
                    scores = jnp.exp(scores - highest)
                    total = jnp.sum(fold(scores), -1, keepdims=True)
                    mixed = mm(scores.astype(BF16), kv_ref[0:end, PAIR : 2 * PAIR])
                    if far:
                        total = total + jnp.sum(fold(beyond), -1, keepdims=True)
                        mixed = mixed + mm(beyond.astype(BF16), fkv_ref[:, PAIR : 2 * PAIR])
                    sums.append(mixed / total)
                    logs.append(jnp.broadcast_to(highest + jnp.log(total), (tile, PAIR)))
                o_ref[t * tile : end] = jnp.where(lane_of(0), sums[0], sums[1]).astype(BF16)
                turned = jnp.transpose(jnp.where(lane_of(0), logs[0], logs[1]))
                upper = lax.broadcasted_iota(jnp.int32, (8, tile), 0) < 4
                l_ref[0, :, t * tile : end] = jnp.where(upper, turned[0:8], turned[HEAD_DIM : HEAD_DIM + 8])

        @pl.when(s_ref[1] == 0)
        def _():
            run(False)

        @pl.when(s_ref[1] != 0)
        def _():
            run(True)

    spec = pl.BlockSpec((rows, PAIR), lambda i, s: (0, i))
    both = pl.BlockSpec((rows, 2 * PAIR), lambda i, s: (0, i))
    log_spec = pl.BlockSpec((1, 8, rows), lambda i, s: (i, 0, 0))
    return call(
        body,
        "attend",
        (shaped((rows, width), BF16), shaped((pairs, 8, rows), F32)),
        (pairs,),
        [spec, both, both],
        (spec, log_spec),
    )(scalars, queries, near, far_side)


def attend_back(queries, near, far_side, grads, attended, logs, scalars, first, pairs):
    rows = queries.shape[0]
    tile = min(TILE, rows)
    width = pairs * PAIR

    def body(
        s_ref, q_ref, kv_ref, fkv_ref, d_ref, o_ref, l_ref,
        dq_ref, dkv_ref, fdkv_ref,
    ):
        offset = s_ref[1] * rows
        length = s_ref[2]

        def run(far):
            query = q_ref[...] * jnp.asarray(0.125, BF16)
            grad = d_ref[...]
            picker = jnp.where(
                lax.broadcasted_iota(jnp.int32, (8, PAIR), 1) // HEAD_DIM
                == lax.broadcasted_iota(jnp.int32, (8, PAIR), 0),
                1.0,
                0.0,
            ).astype(F32)
            dots = lax.dot_general(
                picker,
                grad.astype(F32) * o_ref[...].astype(F32),
                (((1,), (1,)), ((), ())),
                precision=lax.Precision.HIGHEST,
                preferred_element_type=F32,
            )
            blocks = [
                (kv_ref, dkv_ref, t * tile, t * tile, True)
                for t in range(rows // tile)
            ]
            if far:
                blocks += [
                    (fkv_ref, fdkv_ref, t * tile, 0, False)
                    for t in range(rows // tile)
                ]
            turned = [[jnp.zeros((HEAD_DIM, tile), F32) for _ in range(rows // tile)] for _ in range(2)]
            for pair_ref, dpair_ref, at, low, masked in blocks:
                key = pair_ref[at : at + tile, 0:PAIR]
                value = pair_ref[at : at + tile, PAIR : 2 * PAIR]
                key_turned = jnp.transpose(key)
                count = rows - low
                kgrads, vgrads = [], []
                if masked:
                    key_at = lax.broadcasted_iota(jnp.int32, (tile, count), 0) + at
                    place = lax.broadcasted_iota(jnp.int32, (tile, count), 1) + low
                    allowed = (key_at <= place) & (key_at + offset < length)
                all_scores, all_grads = [], []
                for head in range(2):
                    lanes = lane_of(head)
                    mine = jnp.where(lanes, query[low:rows], jnp.zeros((), BF16))
                    mine_grad = jnp.where(lanes, grad[low:rows], jnp.zeros((), BF16))
                    all_scores.append(mm_tail(key, mine))
                    all_grads.append(mm_tail(value, mine_grad))
                for head in range(2):
                    scores = all_scores[head]
                    if masked:
                        scores = jnp.where(allowed, scores, MASKED)
                    base = head * HEAD_DIM
                    probs = jnp.exp(scores - l_ref[0, 4 * head : 4 * head + 1, low:rows])
                    score_grad = (probs * (all_grads[head] - dots[head : head + 1, low:rows])).astype(BF16)
                    vgrads.append(mm(probs.astype(BF16), grad[low:rows]))
                    kgrads.append(mm(score_grad, query[low:rows]))
                    part = mm(key_turned[base : base + HEAD_DIM], score_grad)
                    for t in range(low // tile, rows // tile):
                        turned[head][t] = turned[head][t] + part[:, t * tile - low : (t + 1) * tile - low]
                dpair_ref[at : at + tile, 0:PAIR] = jnp.where(lane_of(0), kgrads[0], kgrads[1]).astype(dpair_ref.dtype)
                dpair_ref[at : at + tile, PAIR : 2 * PAIR] = jnp.where(lane_of(0), vgrads[0], vgrads[1]).astype(dpair_ref.dtype)
            for t in range(rows // tile):
                both = jnp.concatenate([turned[0][t], turned[1][t]], 0)
                dq_ref[t * tile : (t + 1) * tile] = (jnp.transpose(both) * 0.125).astype(BF16)

        @pl.when(s_ref[1] == 0)
        def _():
            run(False)
            fdkv_ref[...] = jnp.zeros_like(fdkv_ref)

        @pl.when(s_ref[1] != 0)
        def _():
            run(True)

    spec = pl.BlockSpec((rows, PAIR), lambda i, s: (0, i + first))
    both = pl.BlockSpec((rows, 2 * PAIR), lambda i, s: (0, i + first))
    own = pl.BlockSpec((rows, PAIR), lambda i, s: (0, i))
    own_both = pl.BlockSpec((rows, 2 * PAIR), lambda i, s: (0, i))
    log_spec = pl.BlockSpec((1, 8, rows), lambda i, s: (i + first, 0, 0))
    return call(
        body,
        "attend_back",
        (shaped((rows, width), BF16), shaped((rows, 2 * width), BF16), shaped((rows, 2 * width), BF16)),
        (pairs,),
        [spec, both, both, spec, spec, log_spec],
        (own, own_both, own_both),
    )(scalars, queries, near, far_side, grads, attended, logs)


def join(attended, inputs, parts, places, gains, scalars):
    rows, width = attended.shape
    tile = min(TILE, rows)
    flat = parts

    def body(s_ref, a_ref, x_ref, g_ref, *refs):
        pieces, (sub_ref, mid_ref, ffn_ref, w_ref) = refs[: len(flat)], refs[len(flat) :]

        @pl.when(pl.program_id(0) == 0)
        def _():
            if len(parts) == 2:
                put_rows(s_ref, pieces[0], pieces[1], places, w_ref, 0, width // pieces[0].shape[2])
            else:
                put_blocks(s_ref, pieces, places, w_ref, 0, width)

        hat, _ = norm_stats(a_ref[...].astype(F32))
        low = (hat * g_ref[1:2, :]).astype(BF16)
        sub_ref[...] = low
        middle = x_ref[...].astype(F32) + mm(low, w_ref[...])
        mid_ref[...] = middle
        hat, _ = norm_stats(middle)
        ffn_ref[...] = (hat * g_ref[2:3, :]).astype(BF16)

    spec = rows_of((tile, width))
    return call(
        body,
        "join",
        (
            shaped((rows, width), BF16),
            shaped((rows, width), F32),
            shaped((rows, width), BF16),
            shaped((width, width), BF16),
        ),
        (rows // tile,),
        [spec, spec, whole((8, width))] + [whole(p.shape) for p in flat],
        (spec,) * 3 + (whole((width, width)),),
    )(scalars, attended, inputs, gains, *flat)


def join_back(branch, far_branch, fgrad, far_fgrad, middle, cotangent, attended, weights, gains, scalars):
    rows, width = middle.shape
    tile = min(TILE, rows)
    steps = rows // tile

    def body(
        s_ref, b_ref, fb_ref, f_ref, ff_ref, m_ref, c_ref, a_ref, w_ref, g_ref,
        out_ref, mg_ref, ml_ref, ag_ref,
    ):
        step = pl.program_id(0)
        places = lax.broadcasted_iota(jnp.int32, (tile, 1), 0) + (step * tile + s_ref[1] * rows)
        kept = (places < s_ref[2]).astype(F32)
        middle = m_ref[...]
        branch = b_ref[...].astype(F32) + fb_ref[...].astype(F32)
        out_ref[...] = (kept * (middle + branch)).astype(BF16)
        hat, inverse = norm_stats(middle)
        grad = f_ref[...].astype(F32) + ff_ref[...].astype(F32)
        middle_grad = c_ref[...].astype(F32) * kept + norm_back(grad, g_ref[2:3, :], hat, inverse)
        mg_ref[...] = middle_grad
        low = middle_grad.astype(BF16)
        ml_ref[...] = low
        sub_grad = mm_tail(low, w_ref[...])
        hat, inverse = norm_stats(a_ref[...].astype(F32))
        ag_ref[...] = norm_back(sub_grad, g_ref[1:2, :], hat, inverse).astype(BF16)

    spec = rows_of((tile, width))
    return call(
        body,
        "join_back",
        (
            shaped((rows, width), BF16),
            shaped((rows, width), F32),
            shaped((rows, width), BF16),
            shaped((rows, width), BF16),
        ),
        (steps,),
        [spec] * 7 + [whole((width, width)), whole((8, width))],
        (spec,) * 4,
    )(scalars, branch, far_branch, fgrad, far_fgrad, middle, cotangent, attended, weights, gains)


def two_sided(tile, width, steps):
    near = pl.BlockSpec((tile, width), lambda i, s: (jnp.minimum(i, steps - 1), 0))
    far = pl.BlockSpec((tile, width), lambda i, s: (jnp.maximum(i - steps, 0), 0))
    return near, far


def stat_rows(first, second):
    lanes = lax.broadcasted_iota(jnp.int32, (first.shape[0], 128), 1)
    return jnp.transpose(jnp.where(lanes == 0, first, jnp.where(lanes == 1, second, 0.0)))[0:8]


def stat_columns(mine, other):
    both = jnp.transpose(mine + other)
    return both[:, 0:1], both[:, 1:2]


def unit_norm(mine, other, total):
    sums, squares = stat_columns(mine, other)
    center = sums / total
    return center, lax.rsqrt(squares / total - center * center + EPSILON)


def fold(value):
    out = value[:, 0:128]
    for at in range(128, value.shape[1], 128):
        out = out + value[:, at : at + 128]
    return out


def to_side(near, near_ref, far_ref, value):
    low = value.astype(BF16)

    @pl.when(near)
    def _():
        near_ref[...] = low

    @pl.when(jnp.logical_not(near))
    def _():
        far_ref[...] = low


def stats_of(tile):
    return pl.BlockSpec((8, tile), lambda i, s: (0, i))


def other_stats(tile, steps):
    return pl.BlockSpec((8, tile), lambda i, s: (0, lax.rem(i + steps, 2 * steps)))


def ffn_in(near, far, parts, places, units, scalars):
    rows, width = near.shape
    pieces = [piece for part in parts for piece in part]
    cuts = [part[0].shape[2] for part in parts]
    cuts[-1] = units - sum(cuts[:-1])
    tile = min(TILE, rows)
    steps = rows // tile
    chunk = 256

    def body(s_ref, n_ref, f_ref, *refs):
        blocks, (act_ref, slope_ref, stat_ref, w_ref) = refs[: len(pieces)], refs[len(pieces) :]

        @pl.when(pl.program_id(0) == 0)
        def _():
            at = 0
            for k, part in enumerate(parts):
                put_blocks(s_ref, blocks[at : at + len(part)], places[k], w_ref, sum(cuts[:k]), cuts[k])
                at += len(part)

        low = jnp.where(pl.program_id(0) < steps, n_ref[...], f_ref[...])
        sums = jnp.zeros((tile, 128), F32)
        squares = jnp.zeros((tile, 128), F32)
        for at in range(0, units, chunk):
            pre = mm(low, w_ref[:, at : at + chunk])
            cdf = 0.5 * (1.0 + lax.erf(pre * 0.7071067811865476))
            pdf = 0.3989422804014327 * jnp.exp(-0.5 * pre * pre)
            act = pre * cdf
            act_ref[:, at : at + chunk] = act.astype(BF16)
            slope_ref[:, at : at + chunk] = (cdf + pre * pdf).astype(slope_ref.dtype)
            sums = sums + fold(act)
            squares = squares + fold(act * act)
        stat_ref[...] = stat_rows(
            jnp.sum(sums, -1, keepdims=True), jnp.sum(squares, -1, keepdims=True)
        )

    near_spec, far_spec = two_sided(tile, width, steps)
    return call(
        body,
        "ffn_in",
        (
            shaped((2 * rows, units), BF16),
            shaped((2 * rows, units), BF16),
            shaped((8, 2 * rows), F32),
            shaped((width, units), BF16),
        ),
        (2 * steps,),
        [near_spec, far_spec] + [whole(p.shape) for p in pieces],
        (rows_of((tile, units)), rows_of((tile, units)), stats_of(tile), whole((width, units))),
    )(scalars, near, far, *pieces)


def ffn_out(act, stats, far_stats, gain, near_grad, far_grad, weights, scalars, order):
    rows, width = near_grad.shape
    units = act.shape[1]
    tile = min(TILE, rows)
    steps = rows // tile
    depth = width // len(order)
    chunk = 256

    def body(s_ref, a_ref, st_ref, fs_ref, g_ref, n_ref, f_ref, w_ref, b_ref, fb_ref, stat_ref, out_ref, stash, tilt):
        step = pl.program_id(0)
        weight = w_ref.at[0]

        @pl.when(step == 0)
        def _():
            tilt[...] = mm_tail(jnp.broadcast_to(g_ref[...], (8, units)).astype(BF16), weight[...])

        center, inverse = unit_norm(st_ref[...], fs_ref[...], 2 * units)
        at_row = pl.multiple_of(step * tile, tile)
        for at in range(0, units, chunk):
            hat = (a_ref[:, at : at + chunk].astype(F32) - center) * inverse
            stash[pl.ds(at_row, tile), at : at + chunk] = (hat * g_ref[:, at : at + chunk]).astype(BF16)
        branch = mm_tail(stash[pl.ds(at_row, tile), :], weight[...])
        to_side(step < steps, b_ref, fb_ref, branch)
        inside = pl.multiple_of(lax.rem(step, steps) * tile, tile)
        grad = jnp.where(step < steps, n_ref[pl.ds(inside, tile)], f_ref[pl.ds(inside, tile)]).astype(F32)
        stat_ref[...] = stat_rows(
            jnp.sum(fold(grad * tilt[0:1, :]), -1, keepdims=True),
            jnp.sum(fold(grad * branch), -1, keepdims=True),
        )

        @pl.when(step == 2 * steps - 1)
        def _():
            near_turned, far_turned = jnp.transpose(n_ref[...]), jnp.transpose(f_ref[...])
            for at in range(0, units, 512):
                part = mm(near_turned, stash[0:rows, at : at + 512]) + mm(far_turned, stash[rows:, at : at + 512])
                for to, block in enumerate(order):
                    out_ref[to * depth : (to + 1) * depth, at : at + 512] = part[
                        block * depth : (block + 1) * depth
                    ].astype(BF16)

    return call(
        body,
        "ffn_out",
        (
            shaped((rows, width), BF16),
            shaped((rows, width), BF16),
            shaped((8, 2 * rows), F32),
            shaped((width, units), BF16),
        ),
        (2 * steps,),
        [
            rows_of((tile, units)),
            stats_of(tile),
            other_stats(tile, steps),
            whole((1, units)),
            whole((rows, width)),
            whole((rows, width)),
            whole((1, width, units)),
        ],
        two_sided(tile, width, steps) + (stats_of(tile), whole((width, units))),
        scratch=[pltpu.VMEM((2 * rows, units), BF16), pltpu.VMEM((8, width), F32)],
    )(scalars, act, stats, far_stats, gain, near_grad, far_grad, weights)


def ffn_back(
    act, slope, stats, far_stats, grads, far_grads, gain, near_grad, far_grad, near, far, out_weights, in_weights, scalars, blocks
):
    rows, width = near.shape
    units = act.shape[1]
    tile = min(TILE, rows)
    steps = rows // tile
    depth = width // blocks
    chunk = 256
    piece = units // 4

    def body(
        s_ref, a_ref, sl_ref, st_ref, fs_ref, gt_ref, fg_ref, g_ref, ng_ref, fgr_ref, n_ref, f_ref, wo_ref, wi_ref,
        b_ref, fb_ref, four_ref, *rest,
    ):
        outs, (stash, fourth, total) = rest[:-3], rest[-3:]
        step = pl.program_id(0)
        center, inverse = unit_norm(st_ref[...], fs_ref[...], 2 * units)
        first, second = stat_columns(gt_ref[...], fg_ref[...])
        first, second = first / (2 * units), second / (2 * units)
        at_row = pl.multiple_of(step * tile, tile)
        inside = pl.multiple_of(lax.rem(step, steps) * tile, tile)
        grad = jnp.where(step < steps, ng_ref[pl.ds(inside, tile)], fgr_ref[pl.ds(inside, tile)])

        @pl.when(step == 0)
        def _():
            fourth[...] = jnp.zeros_like(fourth)

        for at in range(0, units, chunk):
            normed = mm(grad, wo_ref[0, :, at : at + chunk])
            hat = (a_ref[:, at : at + chunk].astype(F32) - center) * inverse
            fourth[:, at : at + chunk] += jnp.sum((normed * hat).reshape(tile // 8, 8, chunk), 0)
            act_grad = inverse * (normed * g_ref[:, at : at + chunk] - first - hat * second)
            stash[pl.ds(at_row, tile), at : at + chunk] = (
                act_grad * sl_ref[:, at : at + chunk].astype(F32)
            ).astype(BF16)
        to_side(step < steps, b_ref, fb_ref, mm_tail(stash[pl.ds(at_row, tile), :], wi_ref[...]))

        @pl.when(step == 2 * steps - 1)
        def _():
            value = jnp.sum(fourth[...], 0, keepdims=True)
            four_ref[...] = jnp.broadcast_to(value, four_ref.shape)
            near_turned, far_turned = jnp.transpose(n_ref[...]), jnp.transpose(f_ref[...])
            for at in range(0, units, piece):
                part = mm(near_turned, stash[0:rows, at : at + piece]) + mm(far_turned, stash[rows:, at : at + piece])
                if blocks == 1:
                    outs[0][:, at : at + piece] = part.astype(BF16)
                else:
                    total[...] = part
                    order = 0 if at < units // 2 else 1
                    inside = at - order * (units // 2)
                    for block in range(blocks):
                        slot = slot_of(block ^ s_ref[0], order, blocks)
                        low = total[block * depth : (block + 1) * depth].astype(BF16)

                        @pl.when(slot < blocks // 2)
                        def _():
                            outs[0][pl.ds(pl.multiple_of(slot * depth, 16), depth), at : at + piece] = low

                        @pl.when(slot >= blocks // 2)
                        def _():
                            row = pl.multiple_of((slot - blocks // 2) * depth, 16)
                            outs[1 + order][pl.ds(row, depth), inside : inside + piece] = low
            if blocks > 1:
                high = value.astype(BF16)
                rest_of = (value - high.astype(F32)).astype(BF16)
                at_line = lax.broadcasted_iota(jnp.int32, (EXTRA, units), 0)
                extra = jnp.where(at_line == 0, high.astype(F32), jnp.where(at_line == 1, rest_of.astype(F32), 0.0))
                extra = extra.astype(BF16)
                outs[1][width // 2 : width // 2 + EXTRA] = extra[:, : units // 2]
                outs[2][width // 2 : width // 2 + EXTRA] = extra[:, units // 2 :]

    wide = rows_of((tile, units))
    crossing = (width // 2 + EXTRA, units // 2)
    shapes = ((width, units),) if blocks == 1 else ((width // 2, units), crossing, crossing)
    return call(
        body,
        "ffn_back",
        (shaped((rows, width), BF16), shaped((rows, width), BF16), shaped((8, units), F32))
        + tuple(shaped(shape, BF16) for shape in shapes),
        (2 * steps,),
        [
            wide, wide, stats_of(tile), other_stats(tile, steps), stats_of(tile), other_stats(tile, steps),
            whole((1, units)),
        ]
        + [whole((rows, width))] * 4
        + [whole((1, width, units)), whole((width, units))],
        two_sided(tile, width, steps) + (whole((8, units)),) + tuple(whole(shape) for shape in shapes),
        scratch=[
            pltpu.VMEM((2 * rows, units), BF16),
            pltpu.VMEM((8, units), F32),
            pltpu.VMEM((width, piece), F32),
        ],
    )(
        scalars, act, slope, stats, far_stats, grads, far_grads, gain, near_grad, far_grad, near, far, out_weights,
        in_weights,
    )


def slot_of(position, order, blocks):
    if blocks < 4:
        return position
    low = (position >> order) & 1
    high = (position >> (1 - order)) & 1
    return low * (blocks // 2) + high * (blocks // 4) + (position >> 2)


def project_grads(normed, dq, dkv, far_dkv, extra, parts, scalars, blocks):
    rows, width = normed.shape
    cols = dq.shape[1]
    depth = width // blocks
    own = depth // 2
    total = 3 * cols + (width if extra else 0)
    pairs = cols // PAIR
    shape = (blocks, own, total) if blocks > 1 else (1, width, total)

    def body(s_ref, n_ref, q_ref, kv_ref, fkv_ref, *refs):
        if extra:
            left_ref, right_ref = refs[:2]
            refs = refs[2:]
        low_ref, *outs, grad_ref = refs
        me, core = s_ref[0], s_ref[1]
        near = core == 0
        both = kv_ref[...].astype(F32) + jnp.where(near, fkv_ref[...].astype(F32), 0.0)
        low_ref[:, 0:cols] = q_ref[...]
        for pair in range(pairs):
            for which in range(2):
                to = (1 + which) * cols + pair * PAIR
                at = (2 * pair + which) * PAIR
                low_ref[:, to : to + PAIR] = both[:, at : at + PAIR].astype(BF16)
        turned = jnp.transpose(n_ref[...])
        grad_ref[:, 0 : 3 * cols] = mm(turned, low_ref[...])
        if extra:
            grad_ref[:, 3 * cols : total] = mm_lead(left_ref[...], right_ref[...])
        if blocks == 1:
            outs[0][0] = grad_ref[...].astype(BF16)
            return
        for side in range(2):
            owner = core if side == 0 else 1 - core
            later, *firsts = outs[3 * side : 3 * side + 3]
            for block in range(blocks):
                position = block ^ me
                row = pl.multiple_of(block * depth + owner * own, 8)
                for order, start, end in parts:
                    slot = slot_of(position, order, blocks)
                    low = grad_ref[pl.ds(row, own), start:end].astype(BF16)

                    @pl.when(slot < blocks // 2)
                    def _():
                        later[slot, :, start:end] = low

                    @pl.when(slot >= blocks // 2)
                    def _():
                        firsts[order][slot - blocks // 2] = low

    more = list(extra) if extra else []
    shapes = [shape]
    if blocks > 1:
        shapes = [(blocks // 2, own, total)] + [(blocks // 2, own, end - start) for _, start, end in parts]
        shapes = shapes * 2
    return call(
        body,
        "project_grads",
        (shaped((rows, 3 * cols), BF16),) + tuple(shaped(each, BF16) for each in shapes),
        (1,),
        [whole((rows, width)), whole((rows, cols)), whole((rows, 2 * cols)), whole((rows, 2 * cols))]
        + [whole((rows, width))] * len(more),
        (whole((rows, 3 * cols)),) + tuple(whole(each) for each in shapes),
        scratch=[pltpu.VMEM((width, total), F32)],
    )(scalars, normed, dq, dkv, far_dkv, *more)


def finish(pieces, query_key, value_proj, output_proj, gains, scalars):
    rows, columns = pieces[0].shape
    width = columns // 4

    def body(s_ref, *refs):
        ins = refs[: len(pieces)]
        qk_ref, v_ref, o_ref, one_ref, two_ref, qk_out, v_out, o_out, one_out, two_out = refs[len(pieces) :]

        def total(start, end):
            value = ins[0][:, start:end].astype(F32)
            for piece in ins[1:]:
                value = value + piece[:, start:end].astype(F32)
            return value

        qk, v, o = total(0, 2 * width), total(2 * width, 3 * width), total(3 * width, columns)
        qk_out[...] = qk
        v_out[...] = v
        o_out[...] = o
        one = fold(qk * qk_ref[...].astype(F32)) + fold(v * v_ref[...].astype(F32))
        two = fold(o * o_ref[...].astype(F32))
        for sums, gain_ref, out in ((one, one_ref, one_out), (two, two_ref, two_out)):
            turned = lax.dot_general(
                jnp.ones((8, 128), F32),
                sums,
                (((1,), (1,)), ((), ())),
                precision=lax.Precision.HIGHEST,
                preferred_element_type=F32,
            )
            out[...] = turned[0:1] / gain_ref[...]

    shapes = ((rows, 2 * width), (rows, width), (rows, width), (1, rows), (1, rows))
    return call(
        body,
        "finish",
        tuple(shaped(shape, F32) for shape in shapes),
        (1,),
        [whole(p.shape) for p in pieces] + [whole(shape) for shape in shapes],
        tuple(whole(shape) for shape in shapes),
    )(scalars, *pieces, query_key, value_proj, output_proj, *gains)


def project_back(lows, inputs, middle_grad, weights, gains, scalars):
    rows, width = inputs.shape
    tile = min(TILE, rows)
    sizes = [low.shape[1] // 3 for low in lows]

    def body(s_ref, *refs):
        low_refs, (x_ref, m_ref, w_ref, g_ref, out_ref) = refs[: len(lows)], refs[len(lows) :]
        hat, inverse = norm_stats(x_ref[...].astype(F32))
        grad = jnp.zeros((tile, width), F32)
        at = 0
        for low_ref, size in zip(low_refs, sizes):
            for which in range(3):
                base = which * width + at
                grad = grad + mm_tail(
                    low_ref[:, which * size : (which + 1) * size], w_ref[:, base : base + size]
                )
            at += size
        out_ref[...] = (m_ref[...] + norm_back(grad, g_ref[0:1, :], hat, inverse)).astype(BF16)

    spec = rows_of((tile, width))
    return call(
        body,
        "project_back",
        shaped((rows, width), BF16),
        (rows // tile,),
        [rows_of((tile, 3 * size)) for size in sizes]
        + [spec, spec, whole((width, 3 * width)), whole((8, width))],
        spec,
    )(scalars, *lows, inputs, middle_grad, weights, gains)


CHIPS = ("outer", "inner")
CORES = "tensor"


def other_core(array):
    return lax.ppermute(array, CORES, [(0, 1), (1, 0)])


def exchange(array, mask, chips):
    return lax.ppermute(array, CHIPS, [(i, i ^ mask) for i in range(chips)])


def bit_count(chips):
    return chips.bit_length() - 1


def by_core(mine, other, axis):
    core = lax.axis_index(CORES)
    return jnp.where(
        core == 0,
        jnp.concatenate([mine, other], axis),
        jnp.concatenate([other, mine], axis),
    )


def after(value, *others):
    return lax.optimization_barrier((value,) + others)[0]


def gather_outer(shard, chips):
    places = list(range(0, chips, 4))
    return jnp.stack([shard] + [exchange(shard, mask, chips) for mask in places[1:]], 0), places


def widen(pieces, places, mask, chips):
    held = pieces[0] if len(pieces) == 1 else jnp.concatenate(pieces, 0)
    return pieces + [exchange(held, mask, chips)], places + [p | mask for p in places]


def on_device(
    inputs,
    cotangent,
    lengths,
    query_key,
    value_proj,
    output_proj,
    hidden_in,
    hidden_out,
    first_gain,
    second_gain,
    third_gain,
    fourth_gain,
):
    rows, width = inputs.shape[1:]
    chips = lax.axis_size(CHIPS)
    inner = lax.axis_size("inner")
    chip = lax.axis_index(CHIPS)
    core = lax.axis_index(CORES)
    barrier = lax.optimization_barrier
    depth = width // chips
    pairwise = chips & (chips - 1) == 0 and chips >= 4 and depth % 16 == 0
    series = inputs[0]
    scalars = jnp.stack([chip if pairwise else jnp.zeros_like(chip), core, lengths[0]]).astype(jnp.int32)
    scalars = jnp.concatenate([scalars, jnp.zeros((5,), jnp.int32)])

    gain_columns = jnp.stack([first_gain, second_gain, third_gain], 1)
    gain_columns = jnp.pad(gain_columns, ((0, 0), (0, 256 - 3)))
    shard = jnp.concatenate([query_key, value_proj, gain_columns], 1)
    half = shard.shape[1]
    units = hidden_in.shape[1]
    if pairwise:
        stack, places = gather_outer(shard, chips)
        cut = -(-half // 256) * 128
        o_folded = jnp.concatenate([output_proj[:, : width // 2], output_proj[:, width // 2 :]], 0)
        late_shard = jnp.concatenate([hidden_in, o_folded], 1)
        late_out = hidden_out.T
        stack, late_shard = barrier((stack, late_shard))
        out_weights_ff = lax.all_gather(late_out, CHIPS, axis=0, tiled=True)[None]
        first, first_places = widen([stack[:, :, :cut]], places, 2, chips)
        second, second_places = widen([stack[:, :, cut:]], places, 1, chips)
        late, late_places = gather_outer(late_shard, chips)
        first[-1], second[-1] = barrier((first[-1], second[-1]))
        first, first_places = widen(first, first_places, 1, chips)
        second, second_places = widen(second, second_places, 2, chips)
        first[-1], second[-1], late = barrier((first[-1], second[-1], late))
        late_cut = -(-late.shape[2] // 256) * 128
        in_first, in_first_places = widen([late[:, :, :late_cut]], late_places, 1, chips)
        in_second, in_second_places = widen([late[:, :, late_cut:]], late_places, 2, chips)
        mine = [jnp.concatenate(first, 0), jnp.concatenate(second, 0)]
        parts = [[p, other_core(p)] for p in mine]
        part_places = [first_places, second_places]
    else:
        gathered = lax.all_gather(shard, CHIPS + (CORES,), axis=0, tiled=True)
        parts, part_places = [[gathered[None]]], [[0]]
        in_parts = [[lax.all_gather(hidden_in, CHIPS, axis=0, tiled=True)[None]]]
        in_part_places = [[0]]
        out_weights = lax.all_gather(output_proj, CHIPS + (CORES,), axis=0, tiled=True)
        out_weights_ff = lax.all_gather(hidden_out.T, CHIPS, axis=0, tiled=True)[None]

    kept = (core * rows + jnp.arange(rows) < lengths[0])[:, None]
    near_grad = jnp.where(kept, cotangent[0], jnp.zeros((), BF16))
    far_grad = other_core(near_grad)

    if pairwise:
        series, in_first[0], in_second[0] = barrier((series, in_first[0], in_second[0]))
    queries, near_kv, normed, weights, gains = project(series, parts, part_places, scalars)
    if pairwise:
        near_kv, in_first[-1], in_second[-1] = barrier((near_kv, in_first[-1], in_second[-1]))
    far_kv = lax.ppermute(near_kv, CORES, [(0, 1)])
    if pairwise:
        in_first, in_first_places = widen(in_first, in_first_places, 2, chips)
        in_second, in_second_places = widen(in_second, in_second_places, 1, chips)
    attended, logs = attend(queries, near_kv, far_kv, scalars)
    if pairwise:
        attended, in_first[-1], in_second[-1] = barrier((attended, in_first[-1], in_second[-1]))
        in_parts = [in_first, in_second]
        in_part_places = [in_first_places, in_second_places]
        extra_columns = units - late_cut
        o_mine = jnp.concatenate(in_second, 0)[:, :, extra_columns:]
        out_parts = [o_mine, other_core(o_mine)]
        sub_low, middle, near, out_weights = join(attended, series, out_parts, in_second_places, gains, scalars)
    else:
        sub_low, middle, near, out_weights = join(attended, series, [out_weights[None]], [0], gains, scalars)
    far = other_core(near)

    if pairwise:
        far, out_weights_ff = barrier((far, out_weights_ff))
    act, slope, stats, in_weights = ffn_in(near, far, in_parts, in_part_places, units, scalars)
    far_stats = other_core(stats)
    outer = chips // inner
    order = list(range(chips))
    if pairwise:
        order = [o * inner + i for i in range(inner) for o in range(outer)]
    gain_four = fourth_gain.astype(F32)[None, :]
    branch, branch_sent, grad_stats, out_payload = ffn_out(
        act, stats, far_stats, gain_four, near_grad, far_grad, out_weights_ff, scalars, order
    )
    if pairwise:
        out_payload = lax.psum_scatter(out_payload, "inner", scatter_dimension=0, tiled=True)
    else:
        out_payload = lax.psum_scatter(out_payload, CHIPS, scatter_dimension=0, tiled=True)
    far_grad_stats = other_core(grad_stats)
    far_branch = other_core(branch_sent)
    blocks = chips if pairwise else 1
    ffn_grad, ffn_grad_sent, fourth_term, *in_payload = ffn_back(
        act, slope, stats, far_stats, grad_stats, far_grad_stats, gain_four, near_grad, far_grad, near, far,
        out_weights_ff, in_weights, scalars, blocks,
    )
    far_ffn_grad = other_core(ffn_grad_sent)
    if pairwise:
        got = [exchange(in_payload[1], 1, chips), exchange(in_payload[2], 2, chips)]
    outputs, middle_grad, middle_low, attended_low = join_back(
        branch, far_branch, ffn_grad, far_ffn_grad, middle, near_grad, attended, out_weights, gains, scalars
    )

    pairs = width // PAIR
    extra = (sub_low, middle_low)
    if pairwise:
        columns = 4 * width
        cut = columns // 2
        middle, lower = chips // 2, chips // 4
        count = width // 2
        dq, dkv, far_dkv = attend_back(queries, near_kv, far_kv, attended_low, attended, logs, scalars, 0, pairs)
        got[0], got[1], out_payload, far_dkv = barrier((got[0], got[1], out_payload, far_dkv))
        far_dkv = lax.ppermute(far_dkv, CORES, [(1, 0)])
        out_payload = lax.psum_scatter(out_payload, "outer", scatter_dimension=0, tiled=True)
        in_kept, fourth = add_parts(in_payload[0][: count // 2], fourth_term[0:1], got, 0, count)
        in_sent, _ = add_parts(in_payload[0][count // 2 :], fourth_term[0:1], got, count // 2, count)
        rows_low = low_rows(fourth)
        sent = [
            jnp.concatenate([in_sent[:, : units // 2], rows_low[:, : units // 2]], 0),
            jnp.concatenate([in_sent[:, units // 2 :], rows_low[:, units // 2 :]], 0),
        ]
        far_dkv, sent[0], sent[1], in_kept = barrier((far_dkv, sent[0], sent[1], in_kept))
        got = [exchange(sent[0], 2, chips), exchange(sent[1], 1, chips)]
        low, keep, keep_one, keep_two, send, send_one, send_two = project_grads(
            normed, dq, dkv, far_dkv, extra, ((0, 0, cut), (1, cut, columns)), scalars, chips
        )
        middle_grad, send, send_one, send_two = barrier((middle_grad, send, send_one, send_two))
        other_one, other_two, other = other_core(send_one), other_core(send_two), other_core(send)
        inputs_grad = project_back([low], series, middle_grad, weights, gains, scalars)
        inputs_grad, other_one, other_two, other, got[0], got[1] = barrier(
            (inputs_grad, other_one, other_two, other, got[0], got[1])
        )
        upper_one, upper_two = add_low(keep_one, other_one), add_low(keep_two, other_two)
        upper_one, upper_two, keep, other = barrier((upper_one, upper_two, keep, other))
        got_one, got_two = exchange(upper_one, 1, chips), exchange(upper_two, 2, chips)
        in_held, fourth = add_parts(in_kept, fourth, got, 0, count // 2)
        in_held = in_held.reshape(chips // 4, depth, units)
        sends = barrier(tuple(outer_sends(in_held, fourth)))
        in_got = exchange_outer(sends, chips)
        sent_first = sum_low(keep[lower:, :, :cut], other[lower:, :, :cut], got_one[lower:])
        sent_second = sum_low(keep[lower:, :, cut:], other[lower:, :, cut:], got_two[lower:])
        sent_first, sent_second = barrier((sent_first, sent_second))
        got_first, got_second = exchange(sent_first, 2, chips), exchange(sent_second, 1, chips)
        kept = sum_low(keep[:lower], other[:lower], jnp.concatenate([got_one[:lower], got_two[:lower]], -1))
        got_first, got_second, kept, out_payload = barrier((got_first, got_second, kept, out_payload))
        both = add_low(kept, jnp.concatenate([got_first, got_second], -1))
        both_sends = barrier(tuple(outer_sends(both, None)))
        both_got = exchange_outer(both_sends, chips)
        both_got[0], *in_got = barrier((both_got[0], *in_got))
        in_payload = in_held[0].astype(F32)
        for piece in in_got:
            in_payload = in_payload + piece[:depth].astype(F32)
            fourth = add_rows(fourth, piece[depth:])
        third_part = jnp.sum(hidden_in.astype(F32) * in_payload, 1, keepdims=True)
        third_part = jnp.broadcast_to(third_part, (depth, 128))
        third_part = third_part + other_core(third_part)
        *both_got, third_part = barrier((*both_got, third_part))
        last = [both[0], *both_got]
    else:
        dq, dkv, far_dkv = attend_back(queries, near_kv, far_kv, attended_low, attended, logs, scalars, 0, pairs)
        far_dkv = lax.ppermute(far_dkv, CORES, [(1, 0)])
        low, mine = project_grads(normed, dq, dkv, far_dkv, extra, None, scalars, 1)
        mine = lax.psum_scatter(mine[0], CHIPS, scatter_dimension=0, tiled=True).astype(F32)
        mine = lax.psum(mine, CORES)
        inputs_grad = project_back([low], series, middle_grad, weights, gains, scalars)
        in_payload = lax.psum_scatter(in_payload[0], CHIPS, scatter_dimension=0, tiled=True).astype(F32)
        fourth = lax.psum(fourth_term[0:1], CHIPS)
        last = [lax.dynamic_slice_in_dim(mine, core * (depth // 2), depth // 2, 0)]
        third_part = lax.psum(jnp.sum(hidden_in.astype(F32) * in_payload, 1, keepdims=True), CORES)
    hidden_out_sum = out_payload.astype(F32).T
    hidden_in_sum = in_payload
    third_sum = lax.dynamic_slice_in_dim(third_part[:, 0], core * (depth // 2), depth // 2) / third_gain.astype(F32)
    gain_rows = [gain.astype(F32)[None, :] for gain in (first_gain, second_gain)]
    qk_sum, value_sum, output_sum, first_sum, second_sum = finish(
        last, query_key, value_proj, output_proj, gain_rows, scalars
    )
    first_sum, second_sum = first_sum[0], second_sum[0]
    return (
        outputs[None],
        inputs_grad[None],
        qk_sum,
        value_sum,
        output_sum,
        hidden_in_sum,
        hidden_out_sum,
        first_sum,
        second_sum,
        third_sum,
        fourth[0],
    )


def add_low(kept, got):
    return (kept.astype(F32) + got.astype(F32)).astype(BF16)


def add_rows(value, rows):
    return value + (rows[0:1].astype(F32) + rows[1:2].astype(F32))


def low_rows(vector):
    high = lax.reduce_precision(vector, 8, 7)
    rest = lax.reduce_precision(vector - high, 8, 7)
    return jnp.concatenate([high, rest, jnp.zeros((EXTRA - 2, vector.shape[1]), F32)], 0).astype(BF16)


def outer_sends(held, vector):
    rows = [] if vector is None else [low_rows(vector)]
    return [jnp.concatenate([held[at]] + rows, 0) if rows else held[at] for at in range(1, held.shape[0])]


def exchange_outer(sends, chips):
    return [exchange(send, 4 * (at + 1), chips) for at, send in enumerate(sends)]


def add_parts(kept, vector, got, start, count):
    part = jnp.concatenate([piece[start : start + kept.shape[0]] for piece in got], 1)
    rows = jnp.concatenate([piece[count:] for piece in got], 1)
    return add_low(kept, part), add_rows(vector, rows)


def sum_low(*arrays):
    total = arrays[0].astype(F32)
    for array in arrays[1:]:
        total = total + array.astype(F32)
    return total.astype(BF16)


def solution(mesh):
    chips, cores = mesh.devices.shape
    inner = 4 if chips % 4 == 0 else 1
    split = Mesh(mesh.devices.reshape(chips // inner, inner, cores), CHIPS + (CORES,))
    every = CHIPS + (CORES,)
    return jax.shard_map(
        on_device,
        mesh=split,
        in_specs=(
            P(CHIPS, CORES, None),
            P(CHIPS, CORES, None),
            P(CHIPS),
            P(every, None),
            P(every, None),
            P(every, None),
            P(CHIPS, CORES),
            P(CORES, CHIPS),
            P(every),
            P(every),
            P(every),
            P(CORES),
        ),
        out_specs=(
            P(CHIPS, CORES, None),
            P(CHIPS, CORES, None),
            P(every, None),
            P(every, None),
            P(every, None),
            P(CHIPS, CORES),
            P(CORES, CHIPS),
            P(every),
            P(every),
            P(every),
            P(CORES),
        ),
        check_vma=False,
    )
```

```python
import jax
import jax.numpy as jnp
from jax import lax
from jax.experimental import pallas as pl
from jax.experimental.pallas import tpu as pltpu
from jax.sharding import Mesh
from jax.sharding import PartitionSpec as P

HEAD_DIM = 64
PAIR = 2 * HEAD_DIM
EPSILON = 1e-05
MASKED = -1000000000.0
F32 = jnp.float32
BF16 = jnp.bfloat16
VMEM_LIMIT = 60 * 1024 * 1024
VMEM_LIMITS = {"project_grads": 30 * 1024 * 1024, "project_back": 30 * 1024 * 1024, "finish": 30 * 1024 * 1024}
TILE = 256
EXTRA = 16
COST_SCALE = 0.05
COSTS = {
    "project": 8,
    "attend": 15,
    "join": 5,
    "ffn_in": 10,
    "ffn_out": 10,
    "ffn_back": 14,
    "join_back": 7,
    "attend_back": 20,
    "project_grads": 11,
    "project_back": 7,
    "finish": 2,
}


def mm(former, latter):
    return jnp.dot(former, latter, preferred_element_type=F32)


def mm_tail(former, latter):
    return lax.dot_general(former, latter, (((1,), (1,)), ((), ())), preferred_element_type=F32)


def mm_lead(former, latter):
    return lax.dot_general(former, latter, (((0,), (0,)), ((), ())), preferred_element_type=F32)


def call(body, name, out_shape, grid, in_specs, out_specs, scratch=(), aliases=None):
    return pl.pallas_call(
        body,
        name=name,
        out_shape=out_shape,
        grid_spec=pltpu.PrefetchScalarGridSpec(
            num_scalar_prefetch=1,
            grid=grid,
            in_specs=in_specs,
            out_specs=out_specs,
            scratch_shapes=list(scratch),
        ),
        input_output_aliases=aliases or {},
        compiler_params=pltpu.CompilerParams(vmem_limit_bytes=VMEM_LIMITS.get(name, VMEM_LIMIT)),
        cost_estimate=pl.CostEstimate(
            flops=1, bytes_accessed=int(COST_SCALE * COSTS[name] * 3690000), transcendentals=0
        ),
    )


def shaped(shape, kind):
    return jax.ShapeDtypeStruct(shape, kind)


def whole(shape):
    return pl.BlockSpec(shape, lambda i, s: (0,) * len(shape), pipeline_mode=pl.Buffered(1))


def rows_of(shape):
    return pl.BlockSpec(shape, lambda i, s: (i, 0))


def norm_stats(series):
    center = jnp.mean(series, -1, keepdims=True)
    spread = jnp.mean(series * series, -1, keepdims=True) - center * center
    inverse = lax.rsqrt(spread + EPSILON)
    return (series - center) * inverse, inverse


def norm_back(grad, gain, hat, inverse):
    scaled = grad * gain
    first = jnp.mean(scaled, -1, keepdims=True)
    second = jnp.mean(scaled * hat, -1, keepdims=True)
    return inverse * (scaled - first - hat * second)


def put_blocks(s_ref, pieces, places, target, column, width):
    at = 0
    for piece in pieces:
        depth = piece.shape[1]
        for block in range(piece.shape[0]):
            row = (s_ref[0] ^ places[at]) * depth
            if depth % 16 == 0:
                row = pl.multiple_of(row, 16)
            target[pl.ds(row, depth), pl.ds(column, width)] = piece[block, :, 0:width]
            at += 1


def put_rows(s_ref, mine, other, places, target, column, folds):
    near = s_ref[1] == 0
    own = mine.shape[1] // folds
    width = mine.shape[2]
    for block in range(mine.shape[0]):
        row = pl.multiple_of((s_ref[0] ^ places[block]) * (2 * own), 16)
        one, two = mine[block].astype(F32), other[block].astype(F32)
        upper, lower = jnp.where(near, one, two), jnp.where(near, two, one)
        for at in range(folds):
            rows = slice(at * own, (at + 1) * own)
            target[pl.ds(row, 2 * own), column + at * width : column + (at + 1) * width] = jnp.concatenate(
                [upper[rows], lower[rows]], 0
            ).astype(BF16)


def project(inputs, parts, places, scalars):
    rows, width = inputs.shape
    tile = min(TILE, rows)
    flat = [piece for part in parts for piece in part]
    cuts = [part[0].shape[2] for part in parts]
    columns = sum(cuts)

    def body(s_ref, x_ref, *refs):
        pieces, (q_ref, kv_ref, n_ref, w_ref, g_ref, full) = refs[: len(flat)], refs[len(flat) :]

        @pl.when(pl.program_id(0) == 0)
        def _():
            at = 0
            for k, part in enumerate(parts):
                column = sum(cuts[:k])
                if len(part) == 2:
                    put_rows(s_ref, pieces[at], pieces[at + 1], places[k], full, column, 1)
                else:
                    put_blocks(s_ref, pieces[at : at + 1], places[k], full, column, cuts[k])
                at += len(part)
            w_ref[...] = full[:, 0 : 3 * width]
            g_ref[...] = jnp.transpose(full[:, 3 * width : 3 * width + 128].astype(F32))[0:8]

        hat, _ = norm_stats(x_ref[...].astype(F32))
        low = (hat * g_ref[0:1, :]).astype(BF16)
        n_ref[...] = low
        q_ref[...] = mm(low, full[:, 0:width]).astype(BF16)
        for which in range(2):
            part = mm(low, full[:, (1 + which) * width : (2 + which) * width]).astype(BF16)
            for pair in range(width // PAIR):
                at = (2 * pair + which) * PAIR
                kv_ref[:, at : at + PAIR] = part[:, pair * PAIR : (pair + 1) * PAIR]

    spec = rows_of((tile, width))
    return call(
        body,
        "project",
        (
            shaped((rows, width), BF16),
            shaped((rows, 2 * width), BF16),
            shaped((rows, width), BF16),
            shaped((width, 3 * width), BF16),
            shaped((8, width), F32),
        ),
        (rows // tile,),
        [spec] + [whole(p.shape) for p in flat],
        (spec, rows_of((tile, 2 * width)), spec, whole((width, 3 * width)), whole((8, width))),
        scratch=[pltpu.VMEM((width, columns), BF16)],
    )(scalars, inputs, *flat)


def lane_of(head):
    lanes = lax.broadcasted_iota(jnp.int32, (1, PAIR), 1)
    return (lanes >= head * HEAD_DIM) & (lanes < (head + 1) * HEAD_DIM)


def attend(queries, near, far_side, scalars):
    rows, width = queries.shape
    tile = min(TILE, rows)
    pairs = width // PAIR

    def body(s_ref, q_ref, kv_ref, fkv_ref, o_ref, l_ref):
        offset = s_ref[1] * rows
        length = s_ref[2]

        def run(far):
            query = q_ref[...] * jnp.asarray(0.125, BF16)
            for t in range(rows // tile):
                end = (t + 1) * tile
                place = lax.broadcasted_iota(jnp.int32, (tile, end), 0) + t * tile
                key_at = lax.broadcasted_iota(jnp.int32, (tile, end), 1)
                allowed = (key_at <= place) & (key_at + offset < length)
                sums = []
                logs = []
                near_scores, far_scores = [], []
                for head in range(2):
                    mine = jnp.where(
                        lane_of(head), query[t * tile : end], jnp.zeros((), BF16)
                    )
                    near_scores.append(mm_tail(mine, kv_ref[0:end, 0:PAIR]))
                    if far:
                        far_scores.append(mm_tail(mine, fkv_ref[:, 0:PAIR]))
                for head in range(2):
                    scores = jnp.where(allowed, near_scores[head], MASKED)
                    highest = jnp.max(scores, -1, keepdims=True)
                    if far:
                        beyond = far_scores[head]
                        highest = jnp.maximum(highest, jnp.max(beyond, -1, keepdims=True))
                        beyond = jnp.exp(beyond - highest)
                    scores = jnp.exp(scores - highest)
                    total = jnp.sum(fold(scores), -1, keepdims=True)
                    mixed = mm(scores.astype(BF16), kv_ref[0:end, PAIR : 2 * PAIR])
                    if far:
                        total = total + jnp.sum(fold(beyond), -1, keepdims=True)
                        mixed = mixed + mm(beyond.astype(BF16), fkv_ref[:, PAIR : 2 * PAIR])
                    sums.append(mixed / total)
                    logs.append(jnp.broadcast_to(highest + jnp.log(total), (tile, PAIR)))
                o_ref[t * tile : end] = jnp.where(lane_of(0), sums[0], sums[1]).astype(BF16)
                turned = jnp.transpose(jnp.where(lane_of(0), logs[0], logs[1]))
                upper = lax.broadcasted_iota(jnp.int32, (8, tile), 0) < 4
                l_ref[0, :, t * tile : end] = jnp.where(upper, turned[0:8], turned[HEAD_DIM : HEAD_DIM + 8])

        @pl.when(s_ref[1] == 0)
        def _():
            run(False)

        @pl.when(s_ref[1] != 0)
        def _():
            run(True)

    spec = pl.BlockSpec((rows, PAIR), lambda i, s: (0, i))
    both = pl.BlockSpec((rows, 2 * PAIR), lambda i, s: (0, i))
    log_spec = pl.BlockSpec((1, 8, rows), lambda i, s: (i, 0, 0))
    return call(
        body,
        "attend",
        (shaped((rows, width), BF16), shaped((pairs, 8, rows), F32)),
        (pairs,),
        [spec, both, both],
        (spec, log_spec),
    )(scalars, queries, near, far_side)


def attend_back(queries, near, far_side, grads, attended, logs, scalars, first, pairs):
    rows = queries.shape[0]
    tile = min(TILE, rows)
    width = pairs * PAIR

    def body(
        s_ref, q_ref, kv_ref, fkv_ref, d_ref, o_ref, l_ref,
        dq_ref, dkv_ref, fdkv_ref,
    ):
        offset = s_ref[1] * rows
        length = s_ref[2]

        def run(far):
            query = q_ref[...] * jnp.asarray(0.125, BF16)
            grad = d_ref[...]
            picker = jnp.where(
                lax.broadcasted_iota(jnp.int32, (8, PAIR), 1) // HEAD_DIM
                == lax.broadcasted_iota(jnp.int32, (8, PAIR), 0),
                1.0,
                0.0,
            ).astype(F32)
            dots = lax.dot_general(
                picker,
                grad.astype(F32) * o_ref[...].astype(F32),
                (((1,), (1,)), ((), ())),
                precision=lax.Precision.HIGHEST,
                preferred_element_type=F32,
            )
            blocks = [
                (kv_ref, dkv_ref, t * tile, t * tile, True)
                for t in range(rows // tile)
            ]
            if far:
                blocks += [
                    (fkv_ref, fdkv_ref, t * tile, 0, False)
                    for t in range(rows // tile)
                ]
            turned = [[jnp.zeros((HEAD_DIM, tile), F32) for _ in range(rows // tile)] for _ in range(2)]
            for pair_ref, dpair_ref, at, low, masked in blocks:
                key = pair_ref[at : at + tile, 0:PAIR]
                value = pair_ref[at : at + tile, PAIR : 2 * PAIR]
                key_turned = jnp.transpose(key)
                count = rows - low
                kgrads, vgrads = [], []
                if masked:
                    key_at = lax.broadcasted_iota(jnp.int32, (tile, count), 0) + at
                    place = lax.broadcasted_iota(jnp.int32, (tile, count), 1) + low
                    allowed = (key_at <= place) & (key_at + offset < length)
                all_scores, all_grads = [], []
                for head in range(2):
                    lanes = lane_of(head)
                    mine = jnp.where(lanes, query[low:rows], jnp.zeros((), BF16))
                    mine_grad = jnp.where(lanes, grad[low:rows], jnp.zeros((), BF16))
                    all_scores.append(mm_tail(key, mine))
                    all_grads.append(mm_tail(value, mine_grad))
                for head in range(2):
                    scores = all_scores[head]
                    if masked:
                        scores = jnp.where(allowed, scores, MASKED)
                    base = head * HEAD_DIM
                    probs = jnp.exp(scores - l_ref[0, 4 * head : 4 * head + 1, low:rows])
                    score_grad = (probs * (all_grads[head] - dots[head : head + 1, low:rows])).astype(BF16)
                    vgrads.append(mm(probs.astype(BF16), grad[low:rows]))
                    kgrads.append(mm(score_grad, query[low:rows]))
                    part = mm(key_turned[base : base + HEAD_DIM], score_grad)
                    for t in range(low // tile, rows // tile):
                        turned[head][t] = turned[head][t] + part[:, t * tile - low : (t + 1) * tile - low]
                dpair_ref[at : at + tile, 0:PAIR] = jnp.where(lane_of(0), kgrads[0], kgrads[1]).astype(dpair_ref.dtype)
                dpair_ref[at : at + tile, PAIR : 2 * PAIR] = jnp.where(lane_of(0), vgrads[0], vgrads[1]).astype(dpair_ref.dtype)
            for t in range(rows // tile):
                both = jnp.concatenate([turned[0][t], turned[1][t]], 0)
                dq_ref[t * tile : (t + 1) * tile] = (jnp.transpose(both) * 0.125).astype(BF16)

        @pl.when(s_ref[1] == 0)
        def _():
            run(False)
            fdkv_ref[...] = jnp.zeros_like(fdkv_ref)

        @pl.when(s_ref[1] != 0)
        def _():
            run(True)

    spec = pl.BlockSpec((rows, PAIR), lambda i, s: (0, i + first))
    both = pl.BlockSpec((rows, 2 * PAIR), lambda i, s: (0, i + first))
    own = pl.BlockSpec((rows, PAIR), lambda i, s: (0, i))
    own_both = pl.BlockSpec((rows, 2 * PAIR), lambda i, s: (0, i))
    log_spec = pl.BlockSpec((1, 8, rows), lambda i, s: (i + first, 0, 0))
    return call(
        body,
        "attend_back",
        (shaped((rows, width), BF16), shaped((rows, 2 * width), BF16), shaped((rows, 2 * width), BF16)),
        (pairs,),
        [spec, both, both, spec, spec, log_spec],
        (own, own_both, own_both),
    )(scalars, queries, near, far_side, grads, attended, logs)


def join(attended, inputs, parts, places, gains, scalars):
    rows, width = attended.shape
    tile = min(TILE, rows)
    flat = parts

    def body(s_ref, a_ref, x_ref, g_ref, *refs):
        pieces, (sub_ref, mid_ref, ffn_ref, w_ref) = refs[: len(flat)], refs[len(flat) :]

        @pl.when(pl.program_id(0) == 0)
        def _():
            if len(parts) == 2:
                put_rows(s_ref, pieces[0], pieces[1], places, w_ref, 0, width // pieces[0].shape[2])
            else:
                put_blocks(s_ref, pieces, places, w_ref, 0, width)

        hat, _ = norm_stats(a_ref[...].astype(F32))
        low = (hat * g_ref[1:2, :]).astype(BF16)
        sub_ref[...] = low
        middle = x_ref[...].astype(F32) + mm(low, w_ref[...])
        mid_ref[...] = middle
        hat, _ = norm_stats(middle)
        ffn_ref[...] = (hat * g_ref[2:3, :]).astype(BF16)

    spec = rows_of((tile, width))
    return call(
        body,
        "join",
        (
            shaped((rows, width), BF16),
            shaped((rows, width), F32),
            shaped((rows, width), BF16),
            shaped((width, width), BF16),
        ),
        (rows // tile,),
        [spec, spec, whole((8, width))] + [whole(p.shape) for p in flat],
        (spec,) * 3 + (whole((width, width)),),
    )(scalars, attended, inputs, gains, *flat)


def join_back(branch, far_branch, fgrad, far_fgrad, middle, cotangent, attended, weights, gains, scalars):
    rows, width = middle.shape
    tile = min(TILE, rows)
    steps = rows // tile

    def body(
        s_ref, b_ref, fb_ref, f_ref, ff_ref, m_ref, c_ref, a_ref, w_ref, g_ref,
        out_ref, mg_ref, ml_ref, ag_ref,
    ):
        step = pl.program_id(0)
        places = lax.broadcasted_iota(jnp.int32, (tile, 1), 0) + (step * tile + s_ref[1] * rows)
        kept = (places < s_ref[2]).astype(F32)
        middle = m_ref[...]
        branch = b_ref[...].astype(F32) + fb_ref[...].astype(F32)
        out_ref[...] = (kept * (middle + branch)).astype(BF16)
        hat, inverse = norm_stats(middle)
        grad = f_ref[...].astype(F32) + ff_ref[...].astype(F32)
        middle_grad = c_ref[...].astype(F32) * kept + norm_back(grad, g_ref[2:3, :], hat, inverse)
        mg_ref[...] = middle_grad
        low = middle_grad.astype(BF16)
        ml_ref[...] = low
        sub_grad = mm_tail(low, w_ref[...])
        hat, inverse = norm_stats(a_ref[...].astype(F32))
        ag_ref[...] = norm_back(sub_grad, g_ref[1:2, :], hat, inverse).astype(BF16)

    spec = rows_of((tile, width))
    return call(
        body,
        "join_back",
        (
            shaped((rows, width), BF16),
            shaped((rows, width), F32),
            shaped((rows, width), BF16),
            shaped((rows, width), BF16),
        ),
        (steps,),
        [spec] * 7 + [whole((width, width)), whole((8, width))],
        (spec,) * 4,
    )(scalars, branch, far_branch, fgrad, far_fgrad, middle, cotangent, attended, weights, gains)


def two_sided(tile, width, steps):
    near = pl.BlockSpec((tile, width), lambda i, s: (jnp.minimum(i, steps - 1), 0))
    far = pl.BlockSpec((tile, width), lambda i, s: (jnp.maximum(i - steps, 0), 0))
    return near, far


def stat_rows(first, second):
    lanes = lax.broadcasted_iota(jnp.int32, (first.shape[0], 128), 1)
    return jnp.transpose(jnp.where(lanes == 0, first, jnp.where(lanes == 1, second, 0.0)))[0:8]


def stat_columns(mine, other):
    both = jnp.transpose(mine + other)
    return both[:, 0:1], both[:, 1:2]


def unit_norm(mine, other, total):
    sums, squares = stat_columns(mine, other)
    center = sums / total
    return center, lax.rsqrt(squares / total - center * center + EPSILON)


def fold(value):
    out = value[:, 0:128]
    for at in range(128, value.shape[1], 128):
        out = out + value[:, at : at + 128]
    return out


def to_side(near, near_ref, far_ref, value):
    low = value.astype(BF16)

    @pl.when(near)
    def _():
        near_ref[...] = low

    @pl.when(jnp.logical_not(near))
    def _():
        far_ref[...] = low


def stats_of(tile):
    return pl.BlockSpec((8, tile), lambda i, s: (0, i))


def other_stats(tile, steps):
    return pl.BlockSpec((8, tile), lambda i, s: (0, lax.rem(i + steps, 2 * steps)))


def ffn_in(near, far, parts, places, units, scalars):
    rows, width = near.shape
    pieces = [piece for part in parts for piece in part]
    cuts = [part[0].shape[2] for part in parts]
    cuts[-1] = units - sum(cuts[:-1])
    tile = min(TILE, rows)
    steps = rows // tile
    chunk = 256

    def body(s_ref, n_ref, f_ref, *refs):
        blocks, (act_ref, slope_ref, stat_ref, w_ref) = refs[: len(pieces)], refs[len(pieces) :]

        @pl.when(pl.program_id(0) == 0)
        def _():
            at = 0
            for k, part in enumerate(parts):
                put_blocks(s_ref, blocks[at : at + len(part)], places[k], w_ref, sum(cuts[:k]), cuts[k])
                at += len(part)

        low = jnp.where(pl.program_id(0) < steps, n_ref[...], f_ref[...])
        sums = jnp.zeros((tile, 128), F32)
        squares = jnp.zeros((tile, 128), F32)
        for at in range(0, units, chunk):
            pre = mm(low, w_ref[:, at : at + chunk])
            cdf = 0.5 * (1.0 + lax.erf(pre * 0.7071067811865476))
            pdf = 0.3989422804014327 * jnp.exp(-0.5 * pre * pre)
            act = pre * cdf
            act_ref[:, at : at + chunk] = act.astype(BF16)
            slope_ref[:, at : at + chunk] = (cdf + pre * pdf).astype(slope_ref.dtype)
            sums = sums + fold(act)
            squares = squares + fold(act * act)
        stat_ref[...] = stat_rows(
            jnp.sum(sums, -1, keepdims=True), jnp.sum(squares, -1, keepdims=True)
        )

    near_spec, far_spec = two_sided(tile, width, steps)
    return call(
        body,
        "ffn_in",
        (
            shaped((2 * rows, units), BF16),
            shaped((2 * rows, units), BF16),
            shaped((8, 2 * rows), F32),
            shaped((width, units), BF16),
        ),
        (2 * steps,),
        [near_spec, far_spec] + [whole(p.shape) for p in pieces],
        (rows_of((tile, units)), rows_of((tile, units)), stats_of(tile), whole((width, units))),
    )(scalars, near, far, *pieces)


def ffn_out(act, stats, far_stats, gain, near_grad, far_grad, weights, scalars, order):
    rows, width = near_grad.shape
    units = act.shape[1]
    tile = min(TILE, rows)
    steps = rows // tile
    depth = width // len(order)
    chunk = 256

    def body(s_ref, a_ref, st_ref, fs_ref, g_ref, n_ref, f_ref, w_ref, b_ref, fb_ref, stat_ref, out_ref, stash, tilt):
        step = pl.program_id(0)
        weight = w_ref.at[0]

        @pl.when(step == 0)
        def _():
            tilt[...] = mm_tail(jnp.broadcast_to(g_ref[...], (8, units)).astype(BF16), weight[...])

        center, inverse = unit_norm(st_ref[...], fs_ref[...], 2 * units)
        at_row = pl.multiple_of(step * tile, tile)
        for at in range(0, units, chunk):
            hat = (a_ref[:, at : at + chunk].astype(F32) - center) * inverse
            stash[pl.ds(at_row, tile), at : at + chunk] = (hat * g_ref[:, at : at + chunk]).astype(BF16)
        branch = mm_tail(stash[pl.ds(at_row, tile), :], weight[...])
        to_side(step < steps, b_ref, fb_ref, branch)
        inside = pl.multiple_of(lax.rem(step, steps) * tile, tile)
        grad = jnp.where(step < steps, n_ref[pl.ds(inside, tile)], f_ref[pl.ds(inside, tile)]).astype(F32)
        stat_ref[...] = stat_rows(
            jnp.sum(fold(grad * tilt[0:1, :]), -1, keepdims=True),
            jnp.sum(fold(grad * branch), -1, keepdims=True),
        )

        @pl.when(step == 2 * steps - 1)
        def _():
            near_turned, far_turned = jnp.transpose(n_ref[...]), jnp.transpose(f_ref[...])
            for at in range(0, units, 512):
                part = mm(near_turned, stash[0:rows, at : at + 512]) + mm(far_turned, stash[rows:, at : at + 512])
                for to, block in enumerate(order):
                    out_ref[to * depth : (to + 1) * depth, at : at + 512] = part[
                        block * depth : (block + 1) * depth
                    ].astype(BF16)

    return call(
        body,
        "ffn_out",
        (
            shaped((rows, width), BF16),
            shaped((rows, width), BF16),
            shaped((8, 2 * rows), F32),
            shaped((width, units), BF16),
        ),
        (2 * steps,),
        [
            rows_of((tile, units)),
            stats_of(tile),
            other_stats(tile, steps),
            whole((1, units)),
            whole((rows, width)),
            whole((rows, width)),
            whole((1, width, units)),
        ],
        two_sided(tile, width, steps) + (stats_of(tile), whole((width, units))),
        scratch=[pltpu.VMEM((2 * rows, units), BF16), pltpu.VMEM((8, width), F32)],
    )(scalars, act, stats, far_stats, gain, near_grad, far_grad, weights)


def ffn_back(
    act, slope, stats, far_stats, grads, far_grads, gain, near_grad, far_grad, near, far, out_weights, in_weights, scalars, blocks
):
    rows, width = near.shape
    units = act.shape[1]
    tile = min(TILE, rows)
    steps = rows // tile
    depth = width // blocks
    chunk = 256
    piece = units // 4

    def body(
        s_ref, a_ref, sl_ref, st_ref, fs_ref, gt_ref, fg_ref, g_ref, ng_ref, fgr_ref, n_ref, f_ref, wo_ref, wi_ref,
        b_ref, fb_ref, four_ref, *rest,
    ):
        outs, (stash, fourth, total) = rest[:-3], rest[-3:]
        step = pl.program_id(0)
        center, inverse = unit_norm(st_ref[...], fs_ref[...], 2 * units)
        first, second = stat_columns(gt_ref[...], fg_ref[...])
        first, second = first / (2 * units), second / (2 * units)
        at_row = pl.multiple_of(step * tile, tile)
        inside = pl.multiple_of(lax.rem(step, steps) * tile, tile)
        grad = jnp.where(step < steps, ng_ref[pl.ds(inside, tile)], fgr_ref[pl.ds(inside, tile)])

        @pl.when(step == 0)
        def _():
            fourth[...] = jnp.zeros_like(fourth)

        for at in range(0, units, chunk):
            normed = mm(grad, wo_ref[0, :, at : at + chunk])
            hat = (a_ref[:, at : at + chunk].astype(F32) - center) * inverse
            fourth[:, at : at + chunk] += jnp.sum((normed * hat).reshape(tile // 8, 8, chunk), 0)
            act_grad = inverse * (normed * g_ref[:, at : at + chunk] - first - hat * second)
            stash[pl.ds(at_row, tile), at : at + chunk] = (
                act_grad * sl_ref[:, at : at + chunk].astype(F32)
            ).astype(BF16)
        to_side(step < steps, b_ref, fb_ref, mm_tail(stash[pl.ds(at_row, tile), :], wi_ref[...]))

        @pl.when(step == 2 * steps - 1)
        def _():
            value = jnp.sum(fourth[...], 0, keepdims=True)
            four_ref[...] = jnp.broadcast_to(value, four_ref.shape)
            near_turned, far_turned = jnp.transpose(n_ref[...]), jnp.transpose(f_ref[...])
            for at in range(0, units, piece):
                part = mm(near_turned, stash[0:rows, at : at + piece]) + mm(far_turned, stash[rows:, at : at + piece])
                if blocks == 1:
                    outs[0][:, at : at + piece] = part.astype(BF16)
                else:
                    total[...] = part
                    order = 0 if at < units // 2 else 1
                    inside = at - order * (units // 2)
                    for block in range(blocks):
                        slot = slot_of(block ^ s_ref[0], order, blocks)
                        low = total[block * depth : (block + 1) * depth].astype(BF16)

                        @pl.when(slot < blocks // 2)
                        def _():
                            outs[0][pl.ds(pl.multiple_of(slot * depth, 16), depth), at : at + piece] = low

                        @pl.when(slot >= blocks // 2)
                        def _():
                            row = pl.multiple_of((slot - blocks // 2) * depth, 16)
                            outs[1 + order][pl.ds(row, depth), inside : inside + piece] = low
            if blocks > 1:
                high = value.astype(BF16)
                rest_of = (value - high.astype(F32)).astype(BF16)
                at_line = lax.broadcasted_iota(jnp.int32, (EXTRA, units), 0)
                extra = jnp.where(at_line == 0, high.astype(F32), jnp.where(at_line == 1, rest_of.astype(F32), 0.0))
                extra = extra.astype(BF16)
                outs[1][width // 2 : width // 2 + EXTRA] = extra[:, : units // 2]
                outs[2][width // 2 : width // 2 + EXTRA] = extra[:, units // 2 :]

    wide = rows_of((tile, units))
    crossing = (width // 2 + EXTRA, units // 2)
    shapes = ((width, units),) if blocks == 1 else ((width // 2, units), crossing, crossing)
    return call(
        body,
        "ffn_back",
        (shaped((rows, width), BF16), shaped((rows, width), BF16), shaped((8, units), F32))
        + tuple(shaped(shape, BF16) for shape in shapes),
        (2 * steps,),
        [
            wide, wide, stats_of(tile), other_stats(tile, steps), stats_of(tile), other_stats(tile, steps),
            whole((1, units)),
        ]
        + [whole((rows, width))] * 4
        + [whole((1, width, units)), whole((width, units))],
        two_sided(tile, width, steps) + (whole((8, units)),) + tuple(whole(shape) for shape in shapes),
        scratch=[
            pltpu.VMEM((2 * rows, units), BF16),
            pltpu.VMEM((8, units), F32),
            pltpu.VMEM((width, piece), F32),
        ],
    )(
        scalars, act, slope, stats, far_stats, grads, far_grads, gain, near_grad, far_grad, near, far, out_weights,
        in_weights,
    )


def slot_of(position, order, blocks):
    if blocks < 4:
        return position
    low = (position >> order) & 1
    high = (position >> (1 - order)) & 1
    return low * (blocks // 2) + high * (blocks // 4) + (position >> 2)


def project_grads(normed, dq, dkv, far_dkv, extra, parts, scalars, blocks):
    rows, width = normed.shape
    cols = dq.shape[1]
    depth = width // blocks
    own = depth // 2
    total = 3 * cols + (width if extra else 0)
    pairs = cols // PAIR
    shape = (blocks, own, total) if blocks > 1 else (1, width, total)

    def body(s_ref, n_ref, q_ref, kv_ref, fkv_ref, *refs):
        if extra:
            left_ref, right_ref = refs[:2]
            refs = refs[2:]
        low_ref, *outs, grad_ref = refs
        me, core = s_ref[0], s_ref[1]
        near = core == 0
        both = kv_ref[...].astype(F32) + jnp.where(near, fkv_ref[...].astype(F32), 0.0)
        low_ref[:, 0:cols] = q_ref[...]
        for pair in range(pairs):
            for which in range(2):
                to = (1 + which) * cols + pair * PAIR
                at = (2 * pair + which) * PAIR
                low_ref[:, to : to + PAIR] = both[:, at : at + PAIR].astype(BF16)
        turned = jnp.transpose(n_ref[...])
        grad_ref[:, 0 : 3 * cols] = mm(turned, low_ref[...])
        if extra:
            grad_ref[:, 3 * cols : total] = mm_lead(left_ref[...], right_ref[...])
        if blocks == 1:
            outs[0][0] = grad_ref[...].astype(BF16)
            return
        for side in range(2):
            owner = core if side == 0 else 1 - core
            later, *firsts = outs[3 * side : 3 * side + 3]
            for block in range(blocks):
                position = block ^ me
                row = pl.multiple_of(block * depth + owner * own, 8)
                for order, start, end in parts:
                    slot = slot_of(position, order, blocks)
                    low = grad_ref[pl.ds(row, own), start:end].astype(BF16)

                    @pl.when(slot < blocks // 2)
                    def _():
                        later[slot, :, start:end] = low

                    @pl.when(slot >= blocks // 2)
                    def _():
                        firsts[order][slot - blocks // 2] = low

    more = list(extra) if extra else []
    shapes = [shape]
    if blocks > 1:
        shapes = [(blocks // 2, own, total)] + [(blocks // 2, own, end - start) for _, start, end in parts]
        shapes = shapes * 2
    return call(
        body,
        "project_grads",
        (shaped((rows, 3 * cols), BF16),) + tuple(shaped(each, BF16) for each in shapes),
        (1,),
        [whole((rows, width)), whole((rows, cols)), whole((rows, 2 * cols)), whole((rows, 2 * cols))]
        + [whole((rows, width))] * len(more),
        (whole((rows, 3 * cols)),) + tuple(whole(each) for each in shapes),
        scratch=[pltpu.VMEM((width, total), F32)],
    )(scalars, normed, dq, dkv, far_dkv, *more)


def finish(pieces, query_key, value_proj, output_proj, gains, scalars):
    rows, columns = pieces[0].shape
    width = columns // 4

    def body(s_ref, *refs):
        ins = refs[: len(pieces)]
        qk_ref, v_ref, o_ref, one_ref, two_ref, qk_out, v_out, o_out, one_out, two_out = refs[len(pieces) :]

        def total(start, end):
            value = ins[0][:, start:end].astype(F32)
            for piece in ins[1:]:
                value = value + piece[:, start:end].astype(F32)
            return value

        qk, v, o = total(0, 2 * width), total(2 * width, 3 * width), total(3 * width, columns)
        qk_out[...] = qk
        v_out[...] = v
        o_out[...] = o
        one = fold(qk * qk_ref[...].astype(F32)) + fold(v * v_ref[...].astype(F32))
        two = fold(o * o_ref[...].astype(F32))
        for sums, gain_ref, out in ((one, one_ref, one_out), (two, two_ref, two_out)):
            turned = lax.dot_general(
                jnp.ones((8, 128), F32),
                sums,
                (((1,), (1,)), ((), ())),
                precision=lax.Precision.HIGHEST,
                preferred_element_type=F32,
            )
            out[...] = turned[0:1] / gain_ref[...]

    shapes = ((rows, 2 * width), (rows, width), (rows, width), (1, rows), (1, rows))
    return call(
        body,
        "finish",
        tuple(shaped(shape, F32) for shape in shapes),
        (1,),
        [whole(p.shape) for p in pieces] + [whole(shape) for shape in shapes],
        tuple(whole(shape) for shape in shapes),
    )(scalars, *pieces, query_key, value_proj, output_proj, *gains)


def project_back(lows, inputs, middle_grad, weights, gains, scalars):
    rows, width = inputs.shape
    tile = min(TILE, rows)
    sizes = [low.shape[1] // 3 for low in lows]

    def body(s_ref, *refs):
        low_refs, (x_ref, m_ref, w_ref, g_ref, out_ref) = refs[: len(lows)], refs[len(lows) :]
        hat, inverse = norm_stats(x_ref[...].astype(F32))
        grad = jnp.zeros((tile, width), F32)
        at = 0
        for low_ref, size in zip(low_refs, sizes):
            for which in range(3):
                base = which * width + at
                grad = grad + mm_tail(
                    low_ref[:, which * size : (which + 1) * size], w_ref[:, base : base + size]
                )
            at += size
        out_ref[...] = (m_ref[...] + norm_back(grad, g_ref[0:1, :], hat, inverse)).astype(BF16)

    spec = rows_of((tile, width))
    return call(
        body,
        "project_back",
        shaped((rows, width), BF16),
        (rows // tile,),
        [rows_of((tile, 3 * size)) for size in sizes]
        + [spec, spec, whole((width, 3 * width)), whole((8, width))],
        spec,
    )(scalars, *lows, inputs, middle_grad, weights, gains)


CHIPS = ("outer", "inner")
CORES = "tensor"


def other_core(array):
    return lax.ppermute(array, CORES, [(0, 1), (1, 0)])


def exchange(array, mask, chips):
    return lax.ppermute(array, CHIPS, [(i, i ^ mask) for i in range(chips)])


def bit_count(chips):
    return chips.bit_length() - 1


def by_core(mine, other, axis):
    core = lax.axis_index(CORES)
    return jnp.where(
        core == 0,
        jnp.concatenate([mine, other], axis),
        jnp.concatenate([other, mine], axis),
    )


def after(value, *others):
    return lax.optimization_barrier((value,) + others)[0]


def gather_outer(shard, chips):
    places = list(range(0, chips, 4))
    return jnp.stack([shard] + [exchange(shard, mask, chips) for mask in places[1:]], 0), places


def widen(pieces, places, mask, chips):
    held = pieces[0] if len(pieces) == 1 else jnp.concatenate(pieces, 0)
    return pieces + [exchange(held, mask, chips)], places + [p | mask for p in places]


def on_device(
    inputs,
    cotangent,
    lengths,
    query_key,
    value_proj,
    output_proj,
    hidden_in,
    hidden_out,
    first_gain,
    second_gain,
    third_gain,
    fourth_gain,
):
    rows, width = inputs.shape[1:]
    chips = lax.axis_size(CHIPS)
    inner = lax.axis_size("inner")
    chip = lax.axis_index(CHIPS)
    core = lax.axis_index(CORES)
    barrier = lax.optimization_barrier
    depth = width // chips
    pairwise = chips & (chips - 1) == 0 and chips >= 4 and depth % 16 == 0
    series = inputs[0]
    scalars = jnp.stack([chip if pairwise else jnp.zeros_like(chip), core, lengths[0]]).astype(jnp.int32)
    scalars = jnp.concatenate([scalars, jnp.zeros((5,), jnp.int32)])

    gain_columns = jnp.stack([first_gain, second_gain, third_gain], 1)
    gain_columns = jnp.pad(gain_columns, ((0, 0), (0, 256 - 3)))
    shard = jnp.concatenate([query_key, value_proj, gain_columns], 1)
    half = shard.shape[1]
    units = hidden_in.shape[1]
    if pairwise:
        stack, places = gather_outer(shard, chips)
        cut = -(-half // 256) * 128
        o_folded = jnp.concatenate([output_proj[:, : width // 2], output_proj[:, width // 2 :]], 0)
        late_shard = jnp.concatenate([hidden_in, o_folded], 1)
        late_out = hidden_out.T
        stack, late_shard = barrier((stack, late_shard))
        out_weights_ff = lax.all_gather(late_out, CHIPS, axis=0, tiled=True)[None]
        first, first_places = widen([stack[:, :, :cut]], places, 2, chips)
        second, second_places = widen([stack[:, :, cut:]], places, 1, chips)
        late, late_places = gather_outer(late_shard, chips)
        first[-1], second[-1] = barrier((first[-1], second[-1]))
        first, first_places = widen(first, first_places, 1, chips)
        second, second_places = widen(second, second_places, 2, chips)
        first[-1], second[-1], late = barrier((first[-1], second[-1], late))
        late_cut = -(-late.shape[2] // 256) * 128
        in_first, in_first_places = widen([late[:, :, :late_cut]], late_places, 1, chips)
        in_second, in_second_places = widen([late[:, :, late_cut:]], late_places, 2, chips)
        mine = [jnp.concatenate(first, 0), jnp.concatenate(second, 0)]
        parts = [[p, other_core(p)] for p in mine]
        part_places = [first_places, second_places]
    else:
        gathered = lax.all_gather(shard, CHIPS + (CORES,), axis=0, tiled=True)
        parts, part_places = [[gathered[None]]], [[0]]
        in_parts = [[lax.all_gather(hidden_in, CHIPS, axis=0, tiled=True)[None]]]
        in_part_places = [[0]]
        out_weights = lax.all_gather(output_proj, CHIPS + (CORES,), axis=0, tiled=True)
        out_weights_ff = lax.all_gather(hidden_out.T, CHIPS, axis=0, tiled=True)[None]

    kept = (core * rows + jnp.arange(rows) < lengths[0])[:, None]
    near_grad = jnp.where(kept, cotangent[0], jnp.zeros((), BF16))
    far_grad = other_core(near_grad)

    if pairwise:
        series, in_first[0], in_second[0] = barrier((series, in_first[0], in_second[0]))
    queries, near_kv, normed, weights, gains = project(series, parts, part_places, scalars)
    if pairwise:
        near_kv, in_first[-1], in_second[-1] = barrier((near_kv, in_first[-1], in_second[-1]))
    far_kv = lax.ppermute(near_kv, CORES, [(0, 1)])
    if pairwise:
        in_first, in_first_places = widen(in_first, in_first_places, 2, chips)
        in_second, in_second_places = widen(in_second, in_second_places, 1, chips)
    attended, logs = attend(queries, near_kv, far_kv, scalars)
    if pairwise:
        attended, in_first[-1], in_second[-1] = barrier((attended, in_first[-1], in_second[-1]))
        in_parts = [in_first, in_second]
        in_part_places = [in_first_places, in_second_places]
        extra_columns = units - late_cut
        o_mine = jnp.concatenate(in_second, 0)[:, :, extra_columns:]
        out_parts = [o_mine, other_core(o_mine)]
        sub_low, middle, near, out_weights = join(attended, series, out_parts, in_second_places, gains, scalars)
    else:
        sub_low, middle, near, out_weights = join(attended, series, [out_weights[None]], [0], gains, scalars)
    far = other_core(near)

    if pairwise:
        far, out_weights_ff = barrier((far, out_weights_ff))
    act, slope, stats, in_weights = ffn_in(near, far, in_parts, in_part_places, units, scalars)
    far_stats = other_core(stats)
    outer = chips // inner
    order = list(range(chips))
    if pairwise:
        order = [o * inner + i for i in range(inner) for o in range(outer)]
    gain_four = fourth_gain.astype(F32)[None, :]
    branch, branch_sent, grad_stats, out_payload = ffn_out(
        act, stats, far_stats, gain_four, near_grad, far_grad, out_weights_ff, scalars, order
    )
    if pairwise:
        out_payload = lax.psum_scatter(out_payload, "inner", scatter_dimension=0, tiled=True)
    else:
        out_payload = lax.psum_scatter(out_payload, CHIPS, scatter_dimension=0, tiled=True)
    far_grad_stats = other_core(grad_stats)
    far_branch = other_core(branch_sent)
    blocks = chips if pairwise else 1
    ffn_grad, ffn_grad_sent, fourth_term, *in_payload = ffn_back(
        act, slope, stats, far_stats, grad_stats, far_grad_stats, gain_four, near_grad, far_grad, near, far,
        out_weights_ff, in_weights, scalars, blocks,
    )
    far_ffn_grad = other_core(ffn_grad_sent)
    if pairwise:
        got = [exchange(in_payload[1], 1, chips), exchange(in_payload[2], 2, chips)]
    outputs, middle_grad, middle_low, attended_low = join_back(
        branch, far_branch, ffn_grad, far_ffn_grad, middle, near_grad, attended, out_weights, gains, scalars
    )

    pairs = width // PAIR
    extra = (sub_low, middle_low)
    if pairwise:
        columns = 4 * width
        cut = columns // 2
        middle, lower = chips // 2, chips // 4
        count = width // 2
        dq, dkv, far_dkv = attend_back(queries, near_kv, far_kv, attended_low, attended, logs, scalars, 0, pairs)
        got[0], got[1], out_payload, far_dkv = barrier((got[0], got[1], out_payload, far_dkv))
        far_dkv = lax.ppermute(far_dkv, CORES, [(1, 0)])
        out_payload = lax.psum_scatter(out_payload, "outer", scatter_dimension=0, tiled=True)
        in_kept, fourth = add_parts(in_payload[0][: count // 2], fourth_term[0:1], got, 0, count)
        in_sent, _ = add_parts(in_payload[0][count // 2 :], fourth_term[0:1], got, count // 2, count)
        rows_low = low_rows(fourth)
        sent = [
            jnp.concatenate([in_sent[:, : units // 2], rows_low[:, : units // 2]], 0),
            jnp.concatenate([in_sent[:, units // 2 :], rows_low[:, units // 2 :]], 0),
        ]
        far_dkv, sent[0], sent[1], in_kept = barrier((far_dkv, sent[0], sent[1], in_kept))
        got = [exchange(sent[0], 2, chips), exchange(sent[1], 1, chips)]
        low, keep, keep_one, keep_two, send, send_one, send_two = project_grads(
            normed, dq, dkv, far_dkv, extra, ((0, 0, cut), (1, cut, columns)), scalars, chips
        )
        middle_grad, send, send_one, send_two = barrier((middle_grad, send, send_one, send_two))
        other_one, other_two, other = other_core(send_one), other_core(send_two), other_core(send)
        inputs_grad = project_back([low], series, middle_grad, weights, gains, scalars)
        inputs_grad, other_one, other_two, other, got[0], got[1] = barrier(
            (inputs_grad, other_one, other_two, other, got[0], got[1])
        )
        upper_one, upper_two = add_low(keep_one, other_one), add_low(keep_two, other_two)
        upper_one, upper_two, keep, other = barrier((upper_one, upper_two, keep, other))
        got_one, got_two = exchange(upper_one, 1, chips), exchange(upper_two, 2, chips)
        in_held, fourth = add_parts(in_kept, fourth, got, 0, count // 2)
        in_held = in_held.reshape(chips // 4, depth, units)
        sends = barrier(tuple(outer_sends(in_held, fourth)))
        in_got = exchange_outer(sends, chips)
        sent_first = sum_low(keep[lower:, :, :cut], other[lower:, :, :cut], got_one[lower:])
        sent_second = sum_low(keep[lower:, :, cut:], other[lower:, :, cut:], got_two[lower:])
        sent_first, sent_second = barrier((sent_first, sent_second))
        got_first, got_second = exchange(sent_first, 2, chips), exchange(sent_second, 1, chips)
        kept = sum_low(keep[:lower], other[:lower], jnp.concatenate([got_one[:lower], got_two[:lower]], -1))
        got_first, got_second, kept, out_payload = barrier((got_first, got_second, kept, out_payload))
        both = add_low(kept, jnp.concatenate([got_first, got_second], -1))
        both_sends = barrier(tuple(outer_sends(both, None)))
        both_got = exchange_outer(both_sends, chips)
        both_got[0], *in_got = barrier((both_got[0], *in_got))
        in_payload = in_held[0].astype(F32)
        for piece in in_got:
            in_payload = in_payload + piece[:depth].astype(F32)
            fourth = add_rows(fourth, piece[depth:])
        third_part = jnp.sum(hidden_in.astype(F32) * in_payload, 1, keepdims=True)
        third_part = jnp.broadcast_to(third_part, (depth, 128))
        third_part = third_part + other_core(third_part)
        *both_got, third_part = barrier((*both_got, third_part))
        last = [both[0], *both_got]
    else:
        dq, dkv, far_dkv = attend_back(queries, near_kv, far_kv, attended_low, attended, logs, scalars, 0, pairs)
        far_dkv = lax.ppermute(far_dkv, CORES, [(1, 0)])
        low, mine = project_grads(normed, dq, dkv, far_dkv, extra, None, scalars, 1)
        mine = lax.psum_scatter(mine[0], CHIPS, scatter_dimension=0, tiled=True).astype(F32)
        mine = lax.psum(mine, CORES)
        inputs_grad = project_back([low], series, middle_grad, weights, gains, scalars)
        in_payload = lax.psum_scatter(in_payload[0], CHIPS, scatter_dimension=0, tiled=True).astype(F32)
        fourth = lax.psum(fourth_term[0:1], CHIPS)
        last = [lax.dynamic_slice_in_dim(mine, core * (depth // 2), depth // 2, 0)]
        third_part = lax.psum(jnp.sum(hidden_in.astype(F32) * in_payload, 1, keepdims=True), CORES)
    hidden_out_sum = out_payload.astype(F32).T
    hidden_in_sum = in_payload
    third_sum = lax.dynamic_slice_in_dim(third_part[:, 0], core * (depth // 2), depth // 2) / third_gain.astype(F32)
    gain_rows = [gain.astype(F32)[None, :] for gain in (first_gain, second_gain)]
    qk_sum, value_sum, output_sum, first_sum, second_sum = finish(
        last, query_key, value_proj, output_proj, gain_rows, scalars
    )
    first_sum, second_sum = first_sum[0], second_sum[0]
    return (
        outputs[None],
        inputs_grad[None],
        qk_sum,
        value_sum,
        output_sum,
        hidden_in_sum,
        hidden_out_sum,
        first_sum,
        second_sum,
        third_sum,
        fourth[0],
    )


def add_low(kept, got):
    return (kept.astype(F32) + got.astype(F32)).astype(BF16)


def add_rows(value, rows):
    return value + (rows[0:1].astype(F32) + rows[1:2].astype(F32))


def low_rows(vector):
    high = lax.reduce_precision(vector, 8, 7)
    rest = lax.reduce_precision(vector - high, 8, 7)
    return jnp.concatenate([high, rest, jnp.zeros((EXTRA - 2, vector.shape[1]), F32)], 0).astype(BF16)


def outer_sends(held, vector):
    rows = [] if vector is None else [low_rows(vector)]
    return [jnp.concatenate([held[at]] + rows, 0) if rows else held[at] for at in range(1, held.shape[0])]


def exchange_outer(sends, chips):
    return [exchange(send, 4 * (at + 1), chips) for at, send in enumerate(sends)]


def add_parts(kept, vector, got, start, count):
    part = jnp.concatenate([piece[start : start + kept.shape[0]] for piece in got], 1)
    rows = jnp.concatenate([piece[count:] for piece in got], 1)
    return add_low(kept, part), add_rows(vector, rows)


def sum_low(*arrays):
    total = arrays[0].astype(F32)
    for array in arrays[1:]:
        total = total + array.astype(F32)
    return total.astype(BF16)


def solution(mesh):
    chips, cores = mesh.devices.shape
    inner = 4 if chips % 4 == 0 else 1
    split = Mesh(mesh.devices.reshape(chips // inner, inner, cores), CHIPS + (CORES,))
    every = CHIPS + (CORES,)
    return jax.shard_map(
        on_device,
        mesh=split,
        in_specs=(
            P(CHIPS, CORES, None),
            P(CHIPS, CORES, None),
            P(CHIPS),
            P(every, None),
            P(every, None),
            P(every, None),
            P(CHIPS, CORES),
            P(CORES, CHIPS),
            P(every),
            P(every),
            P(every),
            P(CORES),
        ),
        out_specs=(
            P(CHIPS, CORES, None),
            P(CHIPS, CORES, None),
            P(every, None),
            P(every, None),
            P(every, None),
            P(CHIPS, CORES),
            P(CORES, CHIPS),
            P(every),
            P(every),
            P(every),
            P(CORES),
        ),
        check_vma=False,
    )
```
